256 devices in a mesh: row: 32 (over x, y, core), col: 8 (over z).
Axes of the slice: x: 4, y: 4, z: 8, core: 2. Of those that a mesh axis runs over, the one named last changes fastest.
Arguments:
- object_field: float32 [2, 24576, 4096], P(None, 'row', 'col'), may hold values from -6 to 6
- probe: float32 [2, 256, 256], replicated, may hold values from -6 to 6
- amplitudes: bfloat16 [32, 8, 3, 4, 256, 256], P('row', 'col'), may hold values from 0 to 2
- positions: int32 [32, 8, 3, 4, 2], P('row', 'col'), may hold values from -128 to 640, as said below
- counts: int32 [32, 8, 3], P('row', 'col'), may hold values from 1 to 4, as said below
Outputs:
- gradient: float32 [2, 24576, 4096], P(None, 'row', 'col')
- updated_object: float32 [2, 24576, 4096], P(None, 'row', 'col')
The draws below stay inside these ranges and needn't reach their ends.
Inputs may be any that keep to these rules, and one draw needn't show every extreme that they name: `positions`: offsets lie from -128 to 640 for rows and from -128 to 384 for columns. In every tile slot 0 of micro-batch 0 sits at row -128 and column 384, and slot 0 of micro-batch 1 at row 640 and column -128. `counts`: slots 0 to count - 1 are live. Some tile has 4 live slots in every micro-batch.
All inputs are finite; a program needn't handle non-finite values.
Results may differ from the reference program's by a relative error of at most 0.0059.
Values may be sent and summed in bfloat16 or wider, within the bound.
No kernel may reach another device: no remote copies, remote signals or barrier semaphores. Data moves between devices by JAX's collectives and lax.ppermute only.
A program may use at most 128 MiB of HBM per device.

```python
import math
import jax
import jax.numpy as jnp
from jax import lax

WIN = 256
TILE_R = 768
TILE_C = 512
SLOTS = 4
MB = 3
HALO = 128
TILE_ROWS = 32
TILE_COLS = 8
NR = 24576
NC = 4096


def draw_positions(key, part):
    key_rows, key_cols = jax.random.split(key)
    shape = (TILE_ROWS, TILE_COLS, MB, SLOTS)
    rows = jax.random.randint(key_rows, shape, -HALO, TILE_R + HALO - WIN + 1)
    cols = jax.random.randint(key_cols, shape, -HALO, TILE_C + HALO - WIN + 1)
    rows = rows.at[:, :, 0, 0].set(-HALO)
    cols = cols.at[:, :, 0, 0].set(TILE_C + HALO - WIN)
    rows = rows.at[:, :, 1, 0].set(TILE_R + HALO - WIN)
    cols = cols.at[:, :, 1, 0].set(-HALO)
    return jnp.stack([rows, cols], axis=-1).astype(jnp.int32)


def draw_counts(key, part):
    key_first, key_second, key_full = jax.random.split(key, 3)
    shape = (TILE_ROWS, TILE_COLS, MB)
    first_draw = jax.random.randint(key_first, shape, 0, SLOTS)
    second_draw = jax.random.randint(key_second, shape, 0, SLOTS)
    values = 1 + first_draw * second_draw // max(SLOTS - 1, 1)
    full_tile = jax.random.randint(key_full, (), 0, TILE_ROWS * TILE_COLS)
    flat = values.reshape(TILE_ROWS * TILE_COLS, MB)
    chosen = (jnp.arange(TILE_ROWS * TILE_COLS) == full_tile)[:, None]
    flat = jnp.where(chosen, SLOTS, flat)
    return flat.reshape(shape).astype(jnp.int32)


def shard_levels(own_key, dims, cuts, smallest, top_value):
    level = 1.0
    for axis_at, blocks in cuts:
        draws = jax.random.uniform(jax.random.fold_in(jax.random.fold_in(own_key, 6), axis_at), (blocks,), jnp.float32, smallest / len(cuts), top_value / len(cuts))
        level = level * jnp.repeat(jnp.exp(draws), dims[axis_at] // blocks).reshape((-1,) + (1,) * (len(dims) - 1 - axis_at))
    return level


def scatter_about(own_key, dims, width, bound, pieces=(), kind=jnp.bfloat16):
    factor_of = shard_levels(own_key, dims, pieces, -0.22, 0.18) if pieces else 1.0
    result = jax.random.normal(own_key, dims, jnp.float32) * width * factor_of
    return jnp.minimum(jnp.maximum(result, -bound), bound).astype(kind)


def setup_inputs(seed: int = 0) -> dict:
    keys = jax.random.split(jax.random.key(seed), 6)
    return {
        "object_field": scatter_about(keys[0], (2, NR, NC), 1.0, 6.0, ((1, 32), (2, 8)), jnp.float32),
        "probe": scatter_about(keys[1], (2, WIN, WIN), 1.0, 6.0, (), jnp.float32),
        "amplitudes": jnp.clip(2.0 * jax.random.uniform(keys[2], (TILE_ROWS, TILE_COLS, MB, SLOTS, WIN, WIN), jnp.float32) ** shard_levels(keys[2], (TILE_ROWS, TILE_COLS, MB, SLOTS, WIN, WIN), ((0, 32), (1, 8)), -0.2, 0.2), 0.0, 2.0).astype(jnp.bfloat16),
        "positions": draw_positions(jax.random.fold_in(keys[5], 71), 0),
        "counts": draw_counts(jax.random.fold_in(keys[5], 71), 0),
    }


step_scale = 0.5

def dft_tables(window):
    counter = jnp.arange(window, dtype=jnp.int32)
    product = counter[:, None] * counter[None, :] % window
    angles = 2.0 * math.pi / window * product.astype(jnp.float32)
    scale_value = 1.0 / math.sqrt(window)
    return ((jnp.cos(angles) * scale_value).astype(jnp.bfloat16), (-jnp.sin(angles) * scale_value).astype(jnp.bfloat16))

def rows_apply(table_real, table_imag, field, inverse):
    first = jnp.einsum('kn,csnm->cskm', table_real.astype(jnp.float32), field.astype(jnp.float32))
    second = jnp.einsum('kn,csnm->cskm', table_imag.astype(jnp.float32), field.astype(jnp.float32))
    if inverse:
        return jnp.stack([first[0] + second[1], first[1] - second[0]])
    return jnp.stack([first[0] - second[1], first[1] + second[0]])

def cols_apply(table_real, table_imag, field, inverse):
    first = jnp.einsum('csnm,km->csnk', field.astype(jnp.float32), table_real.astype(jnp.float32))
    second = jnp.einsum('csnm,km->csnk', field.astype(jnp.float32), table_imag.astype(jnp.float32))
    if inverse:
        return jnp.stack([first[0] + second[1], first[1] - second[0]])
    return jnp.stack([first[0] - second[1], first[1] + second[0]])

def probe_terms(windows, probe, amplitude_block, live_mask, table_real, table_imag):
    object_win = windows.astype(jnp.float32)
    probe_real = probe[0][None]
    probe_imag = probe[1][None]
    exit_real = probe_real * object_win[0] - probe_imag * object_win[1]
    exit_imag = probe_real * object_win[1] + probe_imag * object_win[0]
    exit_wave = jnp.stack([exit_real, exit_imag]).astype(jnp.bfloat16)
    half_wave = rows_apply(table_real, table_imag, exit_wave, False).astype(jnp.bfloat16)
    farfield = cols_apply(table_real, table_imag, half_wave, False)
    magnitude = jnp.sqrt(farfield[0] * farfield[0] + farfield[1] * farfield[1] + 1.0)
    factor = 1.0 - amplitude_block.astype(jnp.float32) / magnitude
    residual_wave = (farfield * factor[None]).astype(jnp.bfloat16)
    back_half = rows_apply(table_real, table_imag, residual_wave, True).astype(jnp.bfloat16)
    back_wave = cols_apply(table_real, table_imag, back_half, True)
    weight = live_mask[:, None, None]
    grad_real = (probe_real * back_wave[0] + probe_imag * back_wave[1]) * weight
    grad_imag = (probe_real * back_wave[1] - probe_imag * back_wave[0]) * weight
    lighting = (probe_real * probe_real + probe_imag * probe_imag) * weight
    return jnp.stack([grad_real, grad_imag, lighting])

def reference(object_field, probe, amplitudes, positions, counts):
    table_real, table_imag = dft_tables(WIN)
    padded = jnp.pad(object_field.astype(jnp.bfloat16), ((0, 0), (HALO, HALO), (HALO, HALO)))
    canvas = jnp.zeros((3, NR + 2 * HALO, NC + 2 * HALO), jnp.float32)
    groups = TILE_ROWS * TILE_COLS * MB
    flat_pos = positions.reshape(groups, SLOTS, 2).astype(jnp.int32)
    flat_counts = counts.reshape(groups).astype(jnp.int32)
    flat_amp = amplitudes.reshape(groups, SLOTS, WIN, WIN)
    zero_index = jnp.zeros((), jnp.int32)

    def one_group(acc, inputs):
        group, offsets, count_now, amplitude_block = inputs
        tile_index = group // MB
        base_row = (tile_index // TILE_COLS * TILE_R + HALO).astype(jnp.int32)
        base_col = (tile_index % TILE_COLS * TILE_C + HALO).astype(jnp.int32)
        row_start = (offsets[:, 0] + base_row).astype(jnp.int32)
        col_start = (offsets[:, 1] + base_col).astype(jnp.int32)
        live_mask = (jnp.arange(SLOTS, dtype=jnp.int32) < count_now).astype(jnp.float32)

        def cut_window(row_at, col_at):
            return lax.dynamic_slice(padded, (zero_index, row_at, col_at), (2, WIN, WIN))
        windows = jax.vmap(cut_window, out_axes=1)(row_start, col_start)
        terms = probe_terms(windows, probe, amplitude_block, live_mask, table_real, table_imag)

        def add_slot(slot_index, inner):
            start = (zero_index, row_start[slot_index], col_start[slot_index])
            current = lax.dynamic_slice(inner, start, (3, WIN, WIN))
            return lax.dynamic_update_slice(inner, current + terms[:, slot_index], start)
        return (lax.fori_loop(0, SLOTS, add_slot, acc), None)
    canvas, unused = lax.scan(one_group, canvas, (jnp.arange(groups, dtype=jnp.int32), flat_pos, flat_counts, flat_amp))
    gradient = canvas[:2, HALO:HALO + NR, HALO:HALO + NC]
    lighting = canvas[2, HALO:HALO + NR, HALO:HALO + NC]
    updated_object = object_field - step_scale * gradient / (lighting[None] + 1.0)
    return (gradient, updated_object)
```

```python
import math

import jax
import jax.numpy as jnp
import numpy as np
from jax import lax
from jax.experimental import pallas as pl
from jax.experimental.pallas import tpu as pltpu
from jax.sharding import PartitionSpec as P

step_scale = 0.5
LANES = 128
CHUNK = 32


def hop(block, axis, distance):
    devices = range(lax.axis_size(axis))
    route = [(i - distance, i) for i in devices if i - distance in devices]
    return lax.ppermute(block, axis, route)


def dft_parts(window):
    counter = jnp.arange(window, dtype=jnp.int32)
    product = counter[:, None] * counter[None, :] % window
    angles = 2.0 * math.pi / window * product.astype(jnp.float32)
    scale_value = 1.0 / math.sqrt(window)
    return (
        (jnp.cos(angles) * scale_value).astype(jnp.bfloat16),
        (-jnp.sin(angles) * scale_value).astype(jnp.bfloat16),
    )


def slots_kernel(
    pos_ref, counts_ref,
    obj_hbm, left_ref, right_ref, top_ref, bottom_ref, probe_ref, amp_ref, fwd_ref, bwd_ref, ext_ref,
    canvas_ref,
    obj, prb, xs, hs, er, sem,
):
    batches = counts_ref.shape[0]
    slots = pos_ref.shape[0] // batches
    win = probe_ref.shape[1]
    margin = win // 2
    tile_r = obj_hbm.shape[1]
    tile_c = obj_hbm.shape[2]
    tiles = tile_c // LANES
    pieces = win // CHUNK
    f32 = jnp.float32
    bf16 = jnp.bfloat16

    copies = [
        pltpu.make_async_copy(
            obj_hbm.at[c, :, pl.ds(LANES * t, LANES)],
            obj.at[c, t + 1, pl.ds(margin, tile_r), :],
            sem.at[c, t],
        )
        for c in range(2)
        for t in range(tiles)
    ]
    for copy in copies:
        copy.start()
    canvas_ref[...] = jnp.zeros_like(canvas_ref)
    for c in range(2):
        obj[c, 0] = left_ref[c].astype(f32)
        obj[c, tiles + 1] = right_ref[c].astype(f32)
        for t in range(tiles):
            cols = slice(LANES * t, LANES * (t + 1))
            obj[c, t + 1, 0:margin, :] = top_ref[c, :, cols].astype(f32)
            obj[c, t + 1, margin + tile_r :, :] = bottom_ref[c, :, cols].astype(f32)
    for copy in copies:
        copy.wait()
    for c in range(2):
        for t in range(tiles):
            part = obj[c, t + 1, pl.ds(margin, tile_r), :]
            obj[c, t + 1, pl.ds(margin, tile_r), :] = part.astype(bf16).astype(f32)

    lane = lax.broadcasted_iota(jnp.int32, (CHUNK, LANES), 1)

    def one_slot(slot):
        row = pos_ref[slot, 0] + margin
        col = pos_ref[slot, 1] + margin
        tile = col // LANES
        shift = col - tile * LANES
        wrapped = jnp.minimum(tile + 2, tiles + 1)
        low = lane < shift

        def build_table(i, carry):
            start = pl.multiple_of(i * CHUNK, CHUNK)
            for h in range(2):
                real = ext_ref[0, h, pl.ds(win - shift + start, CHUNK), :].astype(bf16)
                imag = ext_ref[1, h, pl.ds(win - shift + start, CHUNK), :]
                a = slice(LANES * h, LANES * (h + 1))
                b = slice(win + LANES * h, win + LANES * (h + 1))
                er[pl.ds(start, CHUNK), a] = real
                er[pl.ds(start, CHUNK), b] = imag.astype(bf16)
                er[pl.ds(win + start, CHUNK), a] = (-imag).astype(bf16)
                er[pl.ds(win + start, CHUNK), b] = real
            return carry

        lax.fori_loop(0, pieces, build_table, 0, unroll=2)

        def exit_piece(i, carry):
            start = pl.multiple_of(i * CHUNK, CHUNK)
            rows = pl.ds(start, CHUNK)
            turned = []
            for c in range(2):
                first = pltpu.roll(probe_ref[c, rows, 0:LANES], shift, 1)
                second = pltpu.roll(probe_ref[c, rows, LANES:], shift, 1)
                turned.append((jnp.where(low, second, first), jnp.where(low, first, second)))
            window = []
            for c in range(2):
                at = pl.ds(row + start, CHUNK)
                window.append((
                    jnp.where(low, obj[c, wrapped, at, :], obj[c, tile, at, :]),
                    obj[c, tile + 1, at, :],
                ))
            for h in range(2):
                pr, pi = turned[0][h], turned[1][h]
                wr, wi = window[0][h], window[1][h]
                prb[0, h, rows, :] = pr
                prb[1, h, rows, :] = pi
                cols = slice(LANES * h, LANES * (h + 1))
                xs[rows, cols] = (pr * wr - pi * wi).astype(bf16)
                xs[pl.ds(win + start, CHUNK), cols] = (pr * wi + pi * wr).astype(bf16)
            return carry

        lax.fori_loop(0, pieces, exit_piece, 0, unroll=2)

        def rows_dft(table_ref):
            for part in range(2):
                out = jnp.dot(table_ref[win * part : win * (part + 1), :], xs[...], preferred_element_type=f32)
                hs[:, win * part : win * (part + 1)] = out.astype(bf16)

        rows_dft(fwd_ref)
        half = win // 2
        for m in range(2):
            rows = slice(half * m, half * (m + 1))
            far = jnp.dot(hs[rows, :], er[...], preferred_element_type=f32)
            real, imag = far[:, :win], far[:, win:]
            scale = 1.0 - amp_ref[slot, rows, :].astype(f32) * lax.rsqrt(real * real + imag * imag + 1.0)
            xs[half * m : half * (m + 1), :] = (real * scale).astype(bf16)
            xs[win + half * m : win + half * (m + 1), :] = (imag * scale).astype(bf16)
        rows_dft(bwd_ref)
        for m in range(2):
            rows = slice(half * m, half * (m + 1))
            back = lax.dot_general(
                hs[rows, :], er[...], (((1,), (1,)), ((), ())), preferred_element_type=f32
            )
            for h in range(2):
                pr, pi = prb[0, h, rows, :], prb[1, h, rows, :]
                br = back[:, LANES * h : LANES * (h + 1)]
                bi = back[:, win + LANES * h : win + LANES * (h + 1)]
                terms = (pr * br + pi * bi, pr * bi - pi * br, pr * pr + pi * pi)
                at = pl.ds(row + half * m, half)
                for c in range(3):
                    if h == 0:
                        keep = lax.broadcasted_iota(jnp.int32, (half, LANES), 1) < shift
                        canvas_ref[c, tile, at, :] += jnp.where(keep, 0.0, terms[c])
                        canvas_ref[c, wrapped, at, :] += jnp.where(keep, terms[c], 0.0)
                    else:
                        canvas_ref[c, tile + 1, at, :] += terms[c]

    def guarded(slot, carry):
        batch = slot // slots

        @pl.when(slot - batch * slots < counts_ref[batch])
        def _():
            one_slot(slot)

        return carry

    lax.fori_loop(0, batches * slots, guarded, 0)


def on_device(object_field, probe, amplitudes, positions, counts):
    tile_r, tile_c = object_field.shape[1:]
    window = probe.shape[1]
    margin = window // 2
    batches, slots = amplitudes.shape[2:4]
    tiles = tile_c // LANES
    bf16 = jnp.bfloat16
    real, imag = dft_parts(window)
    fwd = jnp.concatenate([jnp.concatenate([real, -imag], 1), jnp.concatenate([imag, real], 1)], 0)
    bwd = jnp.concatenate([jnp.concatenate([real, imag], 1), jnp.concatenate([-imag, real], 1)], 0)
    tables = jnp.stack([real, imag]).astype(jnp.float32)
    ext = jnp.concatenate([tables, tables], 1).reshape(2, 2 * window, 2, LANES).transpose(0, 2, 1, 3)

    right_edge = object_field[:, :, tile_c - margin :].astype(bf16)
    left_edge = object_field[:, :, :margin].astype(bf16)
    from_left = hop(right_edge, "col", 1)
    from_right = hop(left_edge, "col", -1)
    body = object_field.astype(bf16)
    last = jnp.concatenate([from_left[:, tile_r - margin :], body[:, tile_r - margin :], from_right[:, tile_r - margin :]], 2)
    first = jnp.concatenate([from_left[:, :margin], body[:, :margin], from_right[:, :margin]], 2)
    above = hop(last, "row", 1)
    below = hop(first, "row", -1)
    left = jnp.concatenate([above[:, :, :margin], from_left, below[:, :, :margin]], 1)
    right = jnp.concatenate([above[:, :, margin + tile_c :], from_right, below[:, :, margin + tile_c :]], 1)
    top = above[:, :, margin : margin + tile_c]
    bottom = below[:, :, margin : margin + tile_c]

    vmem = pl.BlockSpec(memory_space=pltpu.VMEM)
    smem = pl.BlockSpec(memory_space=pltpu.SMEM)
    canvas = pl.pallas_call(
        slots_kernel,
        out_shape=jax.ShapeDtypeStruct((3, tiles + 2, tile_r + 2 * margin, LANES), jnp.float32),
        in_specs=[smem, smem, pl.BlockSpec(memory_space=pl.ANY)] + [vmem] * 9,
        out_specs=vmem,
        scratch_shapes=[
            pltpu.VMEM((2, tiles + 2, tile_r + 2 * margin, LANES), jnp.float32),
            pltpu.VMEM((2, 2, window, LANES), jnp.float32),
            pltpu.VMEM((2 * window, window), bf16),
            pltpu.VMEM((window, 2 * window), bf16),
            pltpu.VMEM((2 * window, 2 * window), bf16),
            pltpu.SemaphoreType.DMA((2, tiles)),
        ],
        compiler_params=pltpu.CompilerParams(vmem_limit_bytes=48 << 20),
        name="slots",
    )(
        positions.reshape(batches * slots, 2),
        counts.reshape(batches),
        object_field, left, right, top, bottom, probe,
        amplitudes.reshape(batches * slots, window, window),
        fwd, bwd, ext,
    )

    from_below = hop(canvas[:, :, :margin].astype(bf16), "row", -1).astype(jnp.float32)
    from_above = hop(canvas[:, :, margin + tile_r :].astype(bf16), "row", 1).astype(jnp.float32)
    inner = canvas[:, :, margin : margin + tile_r]
    inner = inner.at[:, :, :margin].add(from_above)
    inner = inner.at[:, :, tile_r - margin :].add(from_below)
    from_right = hop(inner[:, 0].astype(bf16), "col", -1).astype(jnp.float32)
    from_left = hop(inner[:, tiles + 1].astype(bf16), "col", 1).astype(jnp.float32)
    core = inner[:, 1 : 1 + tiles]
    core = core.at[:, 0].add(from_left).at[:, tiles - 1].add(from_right)
    core = core.transpose(0, 2, 1, 3).reshape(3, tile_r, tile_c)
    gradient = core[:2]
    updated = object_field - step_scale * gradient / (core[2][None] + 1.0)
    return (gradient, updated)


def solution(mesh):
    in_specs = (
        P(None, "row", "col"),
        P(),
        P("row", "col", None, None, None, None),
        P("row", "col", None, None, None),
        P("row", "col", None),
    )
    out_specs = (P(None, "row", "col"), P(None, "row", "col"))
    return jax.shard_map(
        on_device, mesh=mesh, in_specs=in_specs, out_specs=out_specs, check_vma=False
    )
```

```python
import math

import jax
import jax.numpy as jnp
from jax import lax
from jax.experimental import pallas as pl
from jax.experimental.pallas import tpu as pltpu
from jax.sharding import PartitionSpec as P

step_scale = 0.5
LANES = 128
PACK = 16
CHUNK = 32
GROUP = 2
f32 = jnp.float32
bf16 = jnp.bfloat16
VMEM = pl.BlockSpec(memory_space=pltpu.VMEM)
SMEM = pl.BlockSpec(memory_space=pltpu.SMEM)
ANY = pl.BlockSpec(memory_space=pl.ANY)


def swap(block, axis, parity):
    size = lax.axis_size(axis)
    route = []
    for i in range(parity, size - 1, 2):
        route += [(i, i + 1), (i + 1, i)]
    return lax.ppermute(block, axis, route)


def even(axis):
    return lax.rem(lax.axis_index(axis), 2) == 0


def dft_parts(window):
    counter = jnp.arange(window, dtype=jnp.int32)
    product = counter[:, None] * counter[None, :] % window
    angles = 2.0 * math.pi / window * product.astype(f32)
    scale_value = 1.0 / math.sqrt(window)
    return (
        (jnp.cos(angles) * scale_value).astype(bf16),
        (-jnp.sin(angles) * scale_value).astype(bf16),
    )


def meta_rows(pos_ref, counts_ref):
    slots = pos_ref.shape[0] // 2
    lane = lax.broadcasted_iota(jnp.int32, (PACK, LANES), 1)
    row = jnp.zeros((PACK, LANES), jnp.int32)
    for k in range(2 * slots):
        value = pos_ref[k] + LANES
        row = jnp.where(lane == k, value // 16, row)
        row = jnp.where(lane == 2 * slots + k, lax.rem(value, 16), row)
    for k in range(counts_ref.shape[0]):
        row = jnp.where(lane == 4 * slots + k, counts_ref[k], row)
    return row.astype(f32).astype(bf16)


def edges_kernel(pos_ref, counts_ref, obj_hbm, first_ref, second_ref, low, high, sem):
    tile_r, tile_c = obj_hbm.shape[1:]
    copies = []
    for c in range(2):
        copies.append(pltpu.make_async_copy(obj_hbm.at[c, :, pl.ds(0, LANES)], low.at[c], sem.at[0, c]))
        copies.append(
            pltpu.make_async_copy(obj_hbm.at[c, :, pl.ds(tile_c - LANES, LANES)], high.at[c], sem.at[1, c])
        )
    for copy in copies:
        copy.start()
    upward = even("col")
    meta = meta_rows(pos_ref, counts_ref)
    first_ref[2 * tile_r :, :] = meta
    second_ref[2 * tile_r :, :] = meta
    for copy in copies:
        copy.wait()
    for c in range(2):
        for r in range(0, tile_r, 128):
            a = low[c, r : r + 128, :]
            b = high[c, r : r + 128, :]
            rows = slice(c * tile_r + r, c * tile_r + r + 128)
            first_ref[rows, :] = jnp.where(upward, b, a).astype(bf16)
            second_ref[rows, :] = jnp.where(upward, a, b).astype(bf16)


def prepare_kernel(obj_hbm, obj_ref, canvas_ref, sem):
    tile_r, tile_c = obj_hbm.shape[1:]
    margin = (obj_ref.shape[2] - tile_r) // 2
    tiles = tile_c // LANES
    body = pl.ds(margin, tile_r)
    copies = [
        pltpu.make_async_copy(
            obj_hbm.at[c, :, pl.ds(LANES * t, LANES)], obj_ref.at[c, t + 1, body, :], sem.at[c, t]
        )
        for c in range(2)
        for t in range(tiles)
    ]
    for copy in copies:
        copy.start()
    canvas_ref[...] = jnp.zeros_like(canvas_ref)
    for k, copy in enumerate(copies):
        copy.wait()
        c, t = divmod(k, tiles)
        obj_ref[c, t + 1, body, :] = obj_ref[c, t + 1, body, :].astype(bf16).astype(f32)


def sides_kernel(obj_in, za_ref, zb_ref, obj_ref, ya_ref, yb_ref):
    tiles = obj_ref.shape[1] - 2
    margin = LANES
    tile_r = obj_ref.shape[2] - 2 * margin
    right_first = even("col")
    downward = even("row")
    for c in range(2):
        for r in range(0, tile_r, 128):
            rows = slice(c * tile_r + r, c * tile_r + r + 128)
            a = za_ref[rows, :].astype(f32)
            b = zb_ref[rows, :].astype(f32)
            at = slice(margin + r, margin + r + 128)
            obj_ref[c, 0, at, :] = jnp.where(right_first, b, a)
            obj_ref[c, tiles + 1, at, :] = jnp.where(right_first, a, b)
    for c in range(2):
        for t in range(tiles + 2):
            top = obj_ref[c, t, margin : 2 * margin, :]
            bottom = obj_ref[c, t, tile_r : tile_r + margin, :]
            k = (c * (tiles + 2) + t) * margin
            ya_ref[k : k + margin, :] = jnp.where(downward, bottom, top).astype(bf16)
            yb_ref[k : k + margin, :] = jnp.where(downward, top, bottom).astype(bf16)


def slots_kernel(
    pos_ref, counts_ref, obj_in, canvas_in, ya_ref, yb_ref, probe_ref, amp_ref, fwd_ref, bwd_ref, ext_ref,
    obj, canvas_ref, ra_ref, rb_ref,
    todo, prb, xs, hs, er,
):
    batches = counts_ref.shape[0]
    slots = pos_ref.shape[0] // (2 * batches)
    win = probe_ref.shape[1]
    margin = win // 2
    tiles = obj.shape[1] - 2
    tile_r = obj.shape[2] - 2 * margin
    lower_first = even("row")
    for c in range(2):
        for t in range(tiles + 2):
            k = (c * (tiles + 2) + t) * margin
            a = ya_ref[k : k + margin, :].astype(f32)
            b = yb_ref[k : k + margin, :].astype(f32)
            obj[c, t, 0:margin, :] = jnp.where(lower_first, b, a)
            obj[c, t, margin + tile_r :, :] = jnp.where(lower_first, a, b)

    def collect(slot, count):
        batch = slot // slots
        live = slot - batch * slots < counts_ref[batch]

        @pl.when(live)
        def _():
            todo[count] = slot

        return count + live.astype(jnp.int32)

    total = lax.fori_loop(0, batches * slots, collect, jnp.int32(0))
    lane = lax.broadcasted_iota(jnp.int32, (CHUNK, LANES), 1)

    def group(p, carry):
        chosen = []
        for g in range(GROUP):
            at = p * GROUP + g
            slot = todo[jnp.minimum(at, total - 1)]
            row = pos_ref[2 * slot] + margin
            col = pos_ref[2 * slot + 1] + margin
            tile = col // LANES
            shift = col - tile * LANES
            chosen.append((slot, row, tile, jnp.minimum(tile + 2, tiles + 1), shift, at < total))

        def exit_waves(g):
            slot, row, tile, wrapped, shift, valid = chosen[g]
            low = lane < shift
            for i in range(0, win, CHUNK):
                turned = []
                window = []
                for c in range(2):
                    one = pltpu.roll(probe_ref[c, i : i + CHUNK, 0:LANES], shift, 1)
                    two = pltpu.roll(probe_ref[c, i : i + CHUNK, LANES:], shift, 1)
                    turned.append((jnp.where(low, two, one), jnp.where(low, one, two)))
                    at = pl.ds(row + i, CHUNK)
                    window.append(
                        (jnp.where(low, obj[c, wrapped, at, :], obj[c, tile, at, :]), obj[c, tile + 1, at, :])
                    )
                for h in range(2):
                    pr, pi = turned[0][h], turned[1][h]
                    wr, wi = window[0][h], window[1][h]
                    prb[g, 0, h, i : i + CHUNK, :] = pr
                    prb[g, 1, h, i : i + CHUNK, :] = pi
                    cols = slice(win * g + LANES * h, win * g + LANES * (h + 1))
                    xs[i : i + CHUNK, cols] = (pr * wr - pi * wi).astype(bf16)
                    xs[win + i : win + i + CHUNK, cols] = (pr * wi + pi * wr).astype(bf16)

        def rolled_table(g):
            shift = chosen[g][4]
            for i in range(0, win, CHUNK):
                for h in range(2):
                    real = ext_ref[0, h, pl.ds(win - shift + i, CHUNK), :].astype(bf16)
                    imag = ext_ref[1, h, pl.ds(win - shift + i, CHUNK), :].astype(bf16)
                    a = slice(LANES * h, LANES * (h + 1))
                    b = slice(win + LANES * h, win + LANES * (h + 1))
                    er[g, i : i + CHUNK, a] = real
                    er[g, i : i + CHUNK, b] = imag
                    er[g, win + i : win + i + CHUNK, a] = -imag
                    er[g, win + i : win + i + CHUNK, b] = real

        def rows_dft(table_ref):
            for g in range(GROUP):
                for part in range(2):
                    out = jnp.dot(
                        table_ref[win * part : win * (part + 1), :],
                        xs[:, win * g : win * (g + 1)],
                        preferred_element_type=f32,
                    )
                    hs[g, :, win * part : win * (part + 1)] = out.astype(bf16)

        def residual_waves(g):
            far = jnp.dot(hs[g], er[g], preferred_element_type=f32)
            real, imag = far[:, :win], far[:, win:]
            scale = 1.0 - amp_ref[chosen[g][0]].astype(f32) * lax.rsqrt(real * real + imag * imag + 1.0)
            xs[:win, win * g : win * (g + 1)] = (real * scale).astype(bf16)
            xs[win:, win * g : win * (g + 1)] = (imag * scale).astype(bf16)

        def accumulate(g):
            slot, row, tile, wrapped, shift, valid = chosen[g]
            back = lax.dot_general(hs[g], er[g], (((1,), (1,)), ((), ())), preferred_element_type=f32)
            keep = lax.broadcasted_iota(jnp.int32, (win, LANES), 1) < shift
            at = pl.ds(row, win)
            for h in range(2):
                pr, pi = prb[g, 0, h], prb[g, 1, h]
                br = back[:, LANES * h : LANES * (h + 1)]
                bi = back[:, win + LANES * h : win + LANES * (h + 1)]
                terms = [pr * br + pi * bi, pr * bi - pi * br]
                if g:
                    terms = [jnp.where(valid, term, 0.0) for term in terms]
                for c in range(2):
                    if h == 0:
                        canvas_ref[c, tile, at, :] += jnp.where(keep, 0.0, terms[c])
                        canvas_ref[c, wrapped, at, :] += jnp.where(keep, terms[c], 0.0)
                    else:
                        canvas_ref[c, tile + 1, at, :] += terms[c]

        for g in range(GROUP):
            exit_waves(g)
        rows_dft(fwd_ref)
        for g in range(GROUP):
            rolled_table(g)
        for g in range(GROUP):
            residual_waves(g)
        rows_dft(bwd_ref)
        for g in range(GROUP):
            accumulate(g)
        return carry

    lax.fori_loop(0, (total + GROUP - 1) // GROUP, group, 0)

    for c in range(2):
        for t in range(tiles + 2):
            k = (c * (tiles + 2) + t) * margin
            top = canvas_ref[c, t, 0:margin, :]
            bottom = canvas_ref[c, t, margin + tile_r :, :]
            ra_ref[k : k + margin, :] = jnp.where(lower_first, bottom, top).astype(bf16)
            rb_ref[k : k + margin, :] = jnp.where(lower_first, top, bottom).astype(bf16)


def light_kernel(meta_ref, probe_ref, scale_ref, power, light):
    win = probe_ref.shape[1]
    tiles, tile_r = scale_ref.shape[:2]
    tile_c = tiles * LANES
    fields = 51
    batches = 3
    slots = 4
    light[...] = jnp.zeros_like(light)
    for h in range(2):
        cols = slice(LANES * h, LANES * (h + 1))
        real, imag = probe_ref[0, :, cols], probe_ref[1, :, cols]
        power[h] = real * real + imag * imag
    step = 2 * batches * slots

    def tile_slots(n, carry):
        down = n // 3 - 1
        across = n - (down + 1) * 3 - 1

        def one(slot, inner):
            batch = slot // slots
            row = meta_ref[n, 2 * slot] * 16 + meta_ref[n, step + 2 * slot] - LANES + down * tile_r
            col = meta_ref[n, 2 * slot + 1] * 16 + meta_ref[n, step + 2 * slot + 1] - LANES + across * tile_c
            live = slot - batch * slots < meta_ref[n, 2 * step + batch]
            meets = (row > -win) & (row < tile_r) & (col > -win) & (col < tile_c)

            @pl.when(live & meets)
            def _():
                place = col + win
                tile = place // LANES
                shift = place - tile * LANES
                for i in range(0, win, 64):
                    low = lax.broadcasted_iota(jnp.int32, (64, LANES), 1) < shift
                    one_half = pltpu.roll(power[0, i : i + 64, :], shift, 1)
                    two_half = pltpu.roll(power[1, i : i + 64, :], shift, 1)
                    at = pl.ds(row + win + i, 64)
                    light[tile, at, :] += jnp.where(low, 0.0, one_half)
                    light[tile + 1, at, :] += jnp.where(low, one_half, two_half)
                    light[tile + 2, at, :] += jnp.where(low, two_half, 0.0)

            return inner

        return lax.fori_loop(0, batches * slots, one, carry)

    lax.fori_loop(0, 9, tile_slots, 0)
    for t in range(tiles):
        scale_ref[t] = step_scale / (light[t + 2, win : win + tile_r, :] + 1.0)


def strips_kernel(canvas_ref, ya_ref, yb_ref, sa_ref, sb_ref):
    tiles = canvas_ref.shape[1] - 2
    margin = LANES
    tile_r = canvas_ref.shape[2] - 2 * margin
    lower_first = even("row")
    right_first = even("col")
    for c in range(2):
        for r in range(0, tile_r, margin):
            sides = []
            for t in (0, tiles + 1):
                value = canvas_ref[c, t, margin + r : 2 * margin + r, :]
                k = (c * (tiles + 2) + t) * margin
                a, b = ya_ref[k : k + margin, :].astype(f32), yb_ref[k : k + margin, :].astype(f32)
                if r == 0:
                    value += jnp.where(lower_first, b, a)
                if r == tile_r - margin:
                    value += jnp.where(lower_first, a, b)
                sides.append(value)
            rows = slice(c * tile_r + r, c * tile_r + r + margin)
            sa_ref[rows, :] = jnp.where(right_first, sides[1], sides[0]).astype(bf16)
            sb_ref[rows, :] = jnp.where(right_first, sides[0], sides[1]).astype(bf16)


def update_kernel(obj_ref, canvas_ref, ya_ref, yb_ref, sa_ref, sb_ref, scale_ref, grad_ref, out_ref):
    tiles = canvas_ref.shape[1] - 2
    margin = LANES
    tile_r = canvas_ref.shape[2] - 2 * margin
    step = pl.program_id(0)
    lower_first = even("row")
    right_first = even("col")
    first = step == 0
    last = step == pl.num_programs(0) - 1
    start = pl.multiple_of(step * margin, margin)
    for c in range(2):
        for t in range(tiles):
            value = canvas_ref[c, t + 1, pl.ds(margin + start, margin), :]
            k = (c * (tiles + 2) + t + 1) * margin
            a, b = ya_ref[k : k + margin, :].astype(f32), yb_ref[k : k + margin, :].astype(f32)
            above = jnp.where(lower_first, b, a)
            below = jnp.where(lower_first, a, b)
            value += jnp.where(first, above, 0.0) + jnp.where(last, below, 0.0)
            if t in (0, tiles - 1):
                rows = pl.ds(pl.multiple_of(c * tile_r + start, margin), margin)
                a, b = sa_ref[rows, :].astype(f32), sb_ref[rows, :].astype(f32)
                if t == 0:
                    value += jnp.where(right_first, b, a)
                if t == tiles - 1:
                    value += jnp.where(right_first, a, b)
            cols = slice(LANES * t, LANES * (t + 1))
            grad_ref[c, :, cols] = value
            out_ref[c, :, cols] = obj_ref[c, :, cols] - scale_ref[t, pl.ds(start, margin), :] * value


def on_device(object_field, probe, amplitudes, positions, counts):
    tile_r, tile_c = object_field.shape[1:]
    window = probe.shape[1]
    margin = window // 2
    batches, slots = amplitudes.shape[2:4]
    tiles = tile_c // LANES
    padded = (2, tiles + 2, tile_r + 2 * margin, LANES)
    real, imag = dft_parts(window)
    fwd = jnp.concatenate([jnp.concatenate([real, -imag], 1), jnp.concatenate([imag, real], 1)], 0)
    bwd = jnp.concatenate([jnp.concatenate([real, imag], 1), jnp.concatenate([-imag, real], 1)], 0)
    tables = jnp.stack([real, imag]).astype(f32)
    ext = jnp.concatenate([tables, tables], 1).reshape(2, 2 * window, 2, LANES).transpose(0, 2, 1, 3)
    places = positions.reshape(2 * batches * slots)
    lives = counts.reshape(batches)
    shape = jax.ShapeDtypeStruct
    side = shape((2 * tile_r + PACK, LANES), bf16)
    strip = shape((2 * (tiles + 2) * margin, LANES), bf16)

    za, zb = pl.pallas_call(
        edges_kernel,
        out_shape=(side, side),
        in_specs=[SMEM, SMEM, ANY],
        out_specs=(VMEM, VMEM),
        scratch_shapes=[pltpu.VMEM((2, tile_r, LANES), f32)] * 2 + [pltpu.SemaphoreType.DMA((2, 2))],
        name="edges",
    )(places, lives, object_field)
    za, zb = swap(za, "col", 0), swap(zb, "col", 1)
    obj, canvas = pl.pallas_call(
        prepare_kernel,
        out_shape=(shape(padded, f32), shape(padded, f32)),
        in_specs=[ANY],
        out_specs=(VMEM, VMEM),
        scratch_shapes=[pltpu.SemaphoreType.DMA((2, tiles))],
        compiler_params=pltpu.CompilerParams(vmem_limit_bytes=4 << 20),
        cost_estimate=pl.CostEstimate(flops=4 << 20, bytes_accessed=16 << 20, transcendentals=0),
        name="prepare",
    )(object_field)
    obj, ya, yb = pl.pallas_call(
        sides_kernel,
        out_shape=(shape(padded, f32), strip, strip),
        in_specs=[VMEM] * 3,
        out_specs=(VMEM,) * 3,
        input_output_aliases={0: 0},
        compiler_params=pltpu.CompilerParams(vmem_limit_bytes=4 << 20),
        name="sides",
    )(obj, za, zb)
    meta_own = jnp.zeros((1, LANES), bf16)
    from_left = jnp.where(even("col"), zb[2 * tile_r :], za[2 * tile_r :])
    from_right = jnp.where(even("col"), za[2 * tile_r :], zb[2 * tile_r :])
    shifted = places + LANES
    own = jnp.concatenate([shifted // 16, shifted % 16, lives, jnp.zeros((LANES - 51,), jnp.int32)])
    own = jnp.broadcast_to(own.astype(bf16)[None], (PACK, LANES))
    metas = jnp.concatenate([from_left, own, from_right], 0)
    ya, yb = jnp.concatenate([ya, metas], 0), jnp.concatenate([yb, metas], 0)
    ya, yb = swap(ya, "row", 0), swap(yb, "row", 1)
    tail = strip.shape[0]
    above = jnp.where(even("row"), yb[tail:], ya[tail:])
    below = jnp.where(even("row"), ya[tail:], yb[tail:])
    table = jnp.concatenate([above, metas, below], 0)[::PACK].astype(jnp.int32)

    _, canvas, ya, yb = pl.pallas_call(
        slots_kernel,
        out_shape=(shape(padded, f32), shape(padded, f32), strip, strip),
        in_specs=[SMEM, SMEM] + [VMEM] * 9,
        out_specs=(VMEM,) * 4,
        input_output_aliases={2: 0, 3: 1},
        scratch_shapes=[
            pltpu.SMEM((batches * slots,), jnp.int32),
            pltpu.VMEM((GROUP, 2, 2, window, LANES), f32),
            pltpu.VMEM((2 * window, GROUP * window), bf16),
            pltpu.VMEM((GROUP, window, 2 * window), bf16),
            pltpu.VMEM((GROUP, 2 * window, 2 * window), bf16),
        ],
        compiler_params=pltpu.CompilerParams(vmem_limit_bytes=14 << 20),
        name="slots",
    )(
        places, lives, obj, canvas, ya, yb, probe,
        amplitudes.reshape(batches * slots, window, window), fwd, bwd, ext,
    )
    ya, yb = swap(ya, "row", 0), swap(yb, "row", 1)
    scale = pl.pallas_call(
        light_kernel,
        out_shape=shape((tiles, tile_r, LANES), f32),
        in_specs=[SMEM, VMEM],
        out_specs=VMEM,
        scratch_shapes=[
            pltpu.VMEM((2, window, LANES), f32),
            pltpu.VMEM((tiles + 4, tile_r + 2 * window, LANES), f32),
        ],
        compiler_params=pltpu.CompilerParams(vmem_limit_bytes=9 << 20),
        cost_estimate=pl.CostEstimate(flops=8 << 20, bytes_accessed=12 << 20, transcendentals=0),
        name="light",
    )(table, probe)
    rim = shape((2 * tile_r, LANES), bf16)
    sa, sb = pl.pallas_call(
        strips_kernel,
        out_shape=(rim, rim),
        in_specs=[VMEM] * 3,
        out_specs=(VMEM, VMEM),
        compiler_params=pltpu.CompilerParams(vmem_limit_bytes=4 << 20),
        name="strips",
    )(canvas, ya, yb)
    sa, sb = swap(sa, "col", 0), swap(sb, "col", 1)
    block = pl.BlockSpec((2, margin, tile_c), lambda i: (0, i, 0))
    field = shape((2, tile_r, tile_c), f32)
    return pl.pallas_call(
        update_kernel,
        grid=(tile_r // margin,),
        out_shape=(field, field),
        in_specs=[block] + [VMEM] * 6,
        out_specs=(block, block),
        compiler_params=pltpu.CompilerParams(vmem_limit_bytes=8 << 20),
        name="update",
    )(object_field, canvas, ya, yb, sa, sb, scale)


def solution(mesh):
    in_specs = (
        P(None, "row", "col"),
        P(),
        P("row", "col", None, None, None, None),
        P("row", "col", None, None, None),
        P("row", "col", None),
    )
    out_specs = (P(None, "row", "col"), P(None, "row", "col"))
    return jax.shard_map(
        on_device, mesh=mesh, in_specs=in_specs, out_specs=out_specs, check_vma=False
    )
```

```python
import functools
import math

import jax
import jax.numpy as jnp
from jax import lax
from jax.experimental import pallas as pl
from jax.experimental.pallas import tpu as pltpu
from jax.sharding import PartitionSpec as P

step_scale = 0.5
LANES = 128
PACK = 16
CHUNK = 32
GROUP = 2
f32 = jnp.float32
bf16 = jnp.bfloat16
VMEM = pl.BlockSpec(memory_space=pltpu.VMEM)
SMEM = pl.BlockSpec(memory_space=pltpu.SMEM)
ANY = pl.BlockSpec(memory_space=pl.ANY)


def swap(block, axis, parity):
    size = lax.axis_size(axis)
    route = []
    for i in range(parity, size - 1, 2):
        route += [(i, i + 1), (i + 1, i)]
    return lax.ppermute(block, axis, route)


def even(axis):
    return lax.rem(lax.axis_index(axis), 2) == 0


def dft_parts(window):
    counter = jnp.arange(window, dtype=jnp.int32)
    product = counter[:, None] * counter[None, :] % window
    angles = 2.0 * math.pi / window * product.astype(f32)
    scale_value = 1.0 / math.sqrt(window)
    return (
        (jnp.cos(angles) * scale_value).astype(bf16),
        (-jnp.sin(angles) * scale_value).astype(bf16),
    )


def meta_rows(pos_ref, counts_ref):
    slots = pos_ref.shape[0] // 2
    lane = lax.broadcasted_iota(jnp.int32, (PACK, LANES), 1)
    row = jnp.zeros((PACK, LANES), jnp.int32)
    for k in range(2 * slots):
        value = pos_ref[k] + LANES
        row = jnp.where(lane == k, value // 16, row)
        row = jnp.where(lane == 2 * slots + k, lax.rem(value, 16), row)
    for k in range(counts_ref.shape[0]):
        row = jnp.where(lane == 4 * slots + k, counts_ref[k], row)
    return row.astype(f32).astype(bf16)


def edges_kernel(pos_ref, counts_ref, obj_hbm, first_ref, second_ref, low, high, sem):
    tile_r, tile_c = obj_hbm.shape[1:]
    copies = []
    for c in range(2):
        copies.append(pltpu.make_async_copy(obj_hbm.at[c, :, pl.ds(0, LANES)], low.at[c], sem.at[0, c]))
        copies.append(
            pltpu.make_async_copy(obj_hbm.at[c, :, pl.ds(tile_c - LANES, LANES)], high.at[c], sem.at[1, c])
        )
    for copy in copies:
        copy.start()
    upward = even("col")
    meta = meta_rows(pos_ref, counts_ref)
    first_ref[2 * tile_r :, :] = meta
    second_ref[2 * tile_r :, :] = meta
    for copy in copies:
        copy.wait()
    for c in range(2):
        for r in range(0, tile_r, 128):
            a = low[c, r : r + 128, :]
            b = high[c, r : r + 128, :]
            rows = slice(c * tile_r + r, c * tile_r + r + 128)
            first_ref[rows, :] = jnp.where(upward, b, a).astype(bf16)
            second_ref[rows, :] = jnp.where(upward, a, b).astype(bf16)


def prepare_kernel(obj_hbm, obj_ref, canvas_ref, sem):
    tile_r, tile_c = obj_hbm.shape[1:]
    margin = (obj_ref.shape[2] - tile_r) // 2
    tiles = tile_c // LANES
    body = pl.ds(margin, tile_r)
    copies = [
        pltpu.make_async_copy(
            obj_hbm.at[c, :, pl.ds(LANES * t, LANES)], obj_ref.at[c, t + 1, body, :], sem.at[c, t]
        )
        for c in range(2)
        for t in range(tiles)
    ]
    for copy in copies:
        copy.start()
    canvas_ref[...] = jnp.zeros_like(canvas_ref)
    for k, copy in enumerate(copies):
        copy.wait()
        c, t = divmod(k, tiles)
        obj_ref[c, t + 1, body, :] = obj_ref[c, t + 1, body, :].astype(bf16).astype(f32)


def sides_kernel(obj_in, za_ref, zb_ref, own_ref, obj_ref, ya_ref, yb_ref, meta_ref):
    tiles = obj_ref.shape[1] - 2
    margin = LANES
    tile_r = obj_ref.shape[2] - 2 * margin
    right_first = even("col")
    downward = even("row")
    for c in range(2):
        for r in range(0, tile_r, 128):
            rows = slice(c * tile_r + r, c * tile_r + r + 128)
            a = za_ref[rows, :].astype(f32)
            b = zb_ref[rows, :].astype(f32)
            at = slice(margin + r, margin + r + 128)
            obj_ref[c, 0, at, :] = jnp.where(right_first, b, a)
            obj_ref[c, tiles + 1, at, :] = jnp.where(right_first, a, b)
    for c in range(2):
        for t in range(tiles + 2):
            top = obj_ref[c, t, margin : 2 * margin, :]
            bottom = obj_ref[c, t, tile_r : tile_r + margin, :]
            k = (c * (tiles + 2) + t) * margin
            ya_ref[k : k + margin, :] = jnp.where(downward, bottom, top).astype(bf16)
            yb_ref[k : k + margin, :] = jnp.where(downward, top, bottom).astype(bf16)
    tail = 2 * (tiles + 2) * margin
    a = za_ref[2 * tile_r :, :].astype(f32)
    b = zb_ref[2 * tile_r :, :].astype(f32)
    metas = (jnp.where(right_first, b, a).astype(bf16), own_ref[2 * tile_r :, :], jnp.where(right_first, a, b).astype(bf16))
    for k, meta in enumerate(metas):
        rows = slice(tail + PACK * k, tail + PACK * (k + 1))
        ya_ref[rows, :] = meta
        yb_ref[rows, :] = meta
        meta_ref[PACK * k : PACK * (k + 1), :] = meta


def slots_kernel(outer, *refs):
    if outer:
        (pos_ref, counts_ref, obj_in, canvas_in, ya_ref, yb_ref, probe_ref, amp_ref, fwd_ref, bwd_ref, ext_ref,
         obj, canvas_ref, ra_ref, rb_ref, todo, prb, xs, hs, er) = refs
    else:
        (pos_ref, counts_ref, obj, canvas_in, probe_ref, amp_ref, fwd_ref, bwd_ref, ext_ref,
         canvas_ref, todo, prb, xs, hs, er) = refs
    batches = counts_ref.shape[0]
    slots = pos_ref.shape[0] // (2 * batches)
    win = probe_ref.shape[1]
    margin = win // 2
    tiles = obj.shape[1] - 2
    tile_r = obj.shape[2] - 2 * margin
    lower_first = even("row")
    for c in range(2 if outer else 0):
        for t in range(tiles + 2):
            k = (c * (tiles + 2) + t) * margin
            a = ya_ref[k : k + margin, :].astype(f32)
            b = yb_ref[k : k + margin, :].astype(f32)
            obj[c, t, 0:margin, :] = jnp.where(lower_first, b, a)
            obj[c, t, margin + tile_r :, :] = jnp.where(lower_first, a, b)

    def collect(slot, count):
        batch = slot // slots
        row = pos_ref[2 * slot]
        inside = (row >= 0) & (row <= tile_r - win)
        live = (slot - batch * slots < counts_ref[batch]) & (inside != outer)

        @pl.when(live)
        def _():
            todo[count] = slot

        return count + live.astype(jnp.int32)

    total = lax.fori_loop(0, batches * slots, collect, jnp.int32(0))
    lane = lax.broadcasted_iota(jnp.int32, (CHUNK, LANES), 1)

    def group(p, carry):
        chosen = []
        for g in range(GROUP):
            at = p * GROUP + g
            slot = todo[jnp.minimum(at, total - 1)]
            row = pos_ref[2 * slot] + margin
            col = pos_ref[2 * slot + 1] + margin
            tile = col // LANES
            shift = col - tile * LANES
            chosen.append((slot, row, tile, jnp.minimum(tile + 2, tiles + 1), shift, at < total))

        def exit_waves(g):
            slot, row, tile, wrapped, shift, valid = chosen[g]
            low = lane < shift
            for i in range(0, win, CHUNK):
                turned = []
                window = []
                for c in range(2):
                    one = pltpu.roll(probe_ref[c, i : i + CHUNK, 0:LANES], shift, 1)
                    two = pltpu.roll(probe_ref[c, i : i + CHUNK, LANES:], shift, 1)
                    turned.append((jnp.where(low, two, one), jnp.where(low, one, two)))
                    at = pl.ds(row + i, CHUNK)
                    window.append(
                        (jnp.where(low, obj[c, wrapped, at, :], obj[c, tile, at, :]), obj[c, tile + 1, at, :])
                    )
                for h in range(2):
                    pr, pi = turned[0][h], turned[1][h]
                    wr, wi = window[0][h], window[1][h]
                    prb[g, 0, h, i : i + CHUNK, :] = pr
                    prb[g, 1, h, i : i + CHUNK, :] = pi
                    cols = slice(win * g + LANES * h, win * g + LANES * (h + 1))
                    xs[i : i + CHUNK, cols] = (pr * wr - pi * wi).astype(bf16)
                    xs[win + i : win + i + CHUNK, cols] = (pr * wi + pi * wr).astype(bf16)

        def rolled_table(g):
            shift = chosen[g][4]
            for i in range(0, win, CHUNK):
                for h in range(2):
                    real = ext_ref[0, h, pl.ds(win - shift + i, CHUNK), :].astype(bf16)
                    imag = ext_ref[1, h, pl.ds(win - shift + i, CHUNK), :].astype(bf16)
                    a = slice(LANES * h, LANES * (h + 1))
                    b = slice(win + LANES * h, win + LANES * (h + 1))
                    er[g, i : i + CHUNK, a] = real
                    er[g, i : i + CHUNK, b] = imag
                    er[g, win + i : win + i + CHUNK, a] = -imag
                    er[g, win + i : win + i + CHUNK, b] = real

        def rows_dft(table_ref):
            for g in range(GROUP):
                for part in range(2):
                    out = jnp.dot(
                        table_ref[win * part : win * (part + 1), :],
                        xs[:, win * g : win * (g + 1)],
                        preferred_element_type=f32,
                    )
                    hs[g, :, win * part : win * (part + 1)] = out.astype(bf16)

        def residual_waves(g):
            far = jnp.dot(hs[g], er[g], preferred_element_type=f32)
            real, imag = far[:, :win], far[:, win:]
            scale = 1.0 - amp_ref[chosen[g][0]].astype(f32) * lax.rsqrt(real * real + imag * imag + 1.0)
            xs[:win, win * g : win * (g + 1)] = (real * scale).astype(bf16)
            xs[win:, win * g : win * (g + 1)] = (imag * scale).astype(bf16)

        def accumulate(g):
            slot, row, tile, wrapped, shift, valid = chosen[g]
            back = lax.dot_general(hs[g], er[g], (((1,), (1,)), ((), ())), preferred_element_type=f32)
            keep = lax.broadcasted_iota(jnp.int32, (win, LANES), 1) < shift
            at = pl.ds(row, win)
            for h in range(2):
                pr, pi = prb[g, 0, h], prb[g, 1, h]
                br = back[:, LANES * h : LANES * (h + 1)]
                bi = back[:, win + LANES * h : win + LANES * (h + 1)]
                terms = [pr * br + pi * bi, pr * bi - pi * br]
                if g:
                    terms = [jnp.where(valid, term, 0.0) for term in terms]
                for c in range(2):
                    if h == 0:
                        canvas_ref[c, tile, at, :] += jnp.where(keep, 0.0, terms[c])
                        canvas_ref[c, wrapped, at, :] += jnp.where(keep, terms[c], 0.0)
                    else:
                        canvas_ref[c, tile + 1, at, :] += terms[c]

        for g in range(GROUP):
            exit_waves(g)
        rows_dft(fwd_ref)
        for g in range(GROUP):
            rolled_table(g)
        for g in range(GROUP):
            residual_waves(g)
        rows_dft(bwd_ref)
        for g in range(GROUP):
            accumulate(g)
        return carry

    lax.fori_loop(0, (total + GROUP - 1) // GROUP, group, 0)

    for c in range(2 if outer else 0):
        for t in range(tiles + 2):
            k = (c * (tiles + 2) + t) * margin
            top = canvas_ref[c, t, 0:margin, :]
            bottom = canvas_ref[c, t, margin + tile_r :, :]
            ra_ref[k : k + margin, :] = jnp.where(lower_first, bottom, top).astype(bf16)
            rb_ref[k : k + margin, :] = jnp.where(lower_first, top, bottom).astype(bf16)


def light_kernel(meta_ref, ya_ref, yb_ref, probe_ref, scale_ref, power, light, rows_ref, table_ref, sem):
    win = probe_ref.shape[1]
    tiles, tile_r = scale_ref.shape[:2]
    tile_c = tiles * LANES
    batches = 3
    slots = 4
    step = 2 * batches * slots
    lower_first = even("row")
    tail = ya_ref.shape[0] - 3 * PACK
    for k in range(3):
        rows = slice(tail + PACK * k, tail + PACK * (k + 1))
        a, b = ya_ref[rows, :].astype(f32), yb_ref[rows, :].astype(f32)
        rows_ref[k : k + 1, :] = jnp.where(lower_first, b, a)[0:1].astype(jnp.int32)
        rows_ref[3 + k : 4 + k, :] = meta_ref[PACK * k : PACK * (k + 1), :].astype(f32)[0:1].astype(jnp.int32)
        rows_ref[6 + k : 7 + k, :] = jnp.where(lower_first, a, b)[0:1].astype(jnp.int32)
    copy = pltpu.make_async_copy(rows_ref, table_ref, sem)
    copy.start()
    for t in range(tiles + 4):
        light[t] = jnp.zeros_like(light[t])
    for h in range(2):
        cols = slice(LANES * h, LANES * (h + 1))
        real, imag = probe_ref[0, :, cols], probe_ref[1, :, cols]
        power[h] = real * real + imag * imag
    copy.wait()

    def tile_slots(n, carry):
        down = n // 3 - 1
        across = n - (down + 1) * 3 - 1

        def one(slot, inner):
            row = table_ref[n, 2 * slot] * 16 + table_ref[n, step + 2 * slot] - LANES + down * tile_r
            col = table_ref[n, 2 * slot + 1] * 16 + table_ref[n, step + 2 * slot + 1] - LANES + across * tile_c
            meets = (row > -win) & (row < tile_r) & (col > -win) & (col < tile_c)

            @pl.when(meets)
            def _():
                place = col + win
                tile = place // LANES
                shift = place - tile * LANES
                low = lax.broadcasted_iota(jnp.int32, (64, LANES), 1) < shift
                for i in range(0, win, 64):
                    one_half = pltpu.roll(power[0, i : i + 64, :], shift, 1)
                    two_half = pltpu.roll(power[1, i : i + 64, :], shift, 1)
                    at = pl.ds(row + win + i, 64)
                    light[tile, at, :] += jnp.where(low, 0.0, one_half)
                    light[tile + 1, at, :] += jnp.where(low, one_half, two_half)
                    light[tile + 2, at, :] += jnp.where(low, two_half, 0.0)

            return inner

        for batch in range(batches):
            carry = lax.fori_loop(slots * batch, slots * batch + table_ref[n, 2 * step + batch], one, carry)
        return carry

    lax.fori_loop(0, 9, tile_slots, 0)
    for t in range(tiles):
        scale_ref[t] = step_scale / (light[t + 2, win : win + tile_r, :] + 1.0)


def strips_kernel(canvas_ref, ya_ref, yb_ref, sa_ref, sb_ref):
    tiles = canvas_ref.shape[1] - 2
    margin = LANES
    tile_r = canvas_ref.shape[2] - 2 * margin
    lower_first = even("row")
    right_first = even("col")
    for c in range(2):
        for r in range(0, tile_r, margin):
            sides = []
            for t in (0, tiles + 1):
                value = canvas_ref[c, t, margin + r : 2 * margin + r, :]
                k = (c * (tiles + 2) + t) * margin
                a, b = ya_ref[k : k + margin, :].astype(f32), yb_ref[k : k + margin, :].astype(f32)
                if r == 0:
                    value += jnp.where(lower_first, b, a)
                if r == tile_r - margin:
                    value += jnp.where(lower_first, a, b)
                sides.append(value)
            rows = slice(c * tile_r + r, c * tile_r + r + margin)
            sa_ref[rows, :] = jnp.where(right_first, sides[1], sides[0]).astype(bf16)
            sb_ref[rows, :] = jnp.where(right_first, sides[0], sides[1]).astype(bf16)


def update_kernel(obj_ref, canvas_ref, ya_ref, yb_ref, sa_ref, sb_ref, scale_ref, grad_ref, out_ref):
    tiles = canvas_ref.shape[1] - 2
    margin = LANES
    tile_r = canvas_ref.shape[2] - 2 * margin
    step = pl.program_id(0)
    lower_first = even("row")
    right_first = even("col")
    first = step == 0
    last = step == pl.num_programs(0) - 1
    start = pl.multiple_of(step * margin, margin)
    def write(edge):
        for c in range(2):
            for t in range(tiles):
                value = canvas_ref[c, t + 1, pl.ds(margin + start, margin), :]
                if edge:
                    k = (c * (tiles + 2) + t + 1) * margin
                    a, b = ya_ref[k : k + margin, :].astype(f32), yb_ref[k : k + margin, :].astype(f32)
                    value += jnp.where(lower_first == first, b, a)
                if t in (0, tiles - 1):
                    rows = pl.ds(pl.multiple_of(c * tile_r + start, margin), margin)
                    a, b = sa_ref[rows, :].astype(f32), sb_ref[rows, :].astype(f32)
                    if t == 0:
                        value += jnp.where(right_first, b, a)
                    if t == tiles - 1:
                        value += jnp.where(right_first, a, b)
                cols = slice(LANES * t, LANES * (t + 1))
                grad_ref[c, :, cols] = value
                out_ref[c, :, cols] = obj_ref[c, :, cols] - scale_ref[t, pl.ds(start, margin), :] * value

    @pl.when(first | last)
    def _():
        write(True)

    @pl.when(jnp.logical_not(first | last))
    def _():
        write(False)


def on_device(object_field, probe, amplitudes, positions, counts):
    tile_r, tile_c = object_field.shape[1:]
    window = probe.shape[1]
    margin = window // 2
    batches, slots = amplitudes.shape[2:4]
    tiles = tile_c // LANES
    padded = (2, tiles + 2, tile_r + 2 * margin, LANES)
    real, imag = dft_parts(window)
    fwd = jnp.concatenate([jnp.concatenate([real, -imag], 1), jnp.concatenate([imag, real], 1)], 0)
    bwd = jnp.concatenate([jnp.concatenate([real, imag], 1), jnp.concatenate([-imag, real], 1)], 0)
    tables = jnp.stack([real, imag]).astype(f32)
    ext = jnp.concatenate([tables, tables], 1).reshape(2, 2 * window, 2, LANES).transpose(0, 2, 1, 3)
    places = positions.reshape(2 * batches * slots)
    lives = counts.reshape(batches)
    shape = jax.ShapeDtypeStruct
    side = shape((2 * tile_r + PACK, LANES), bf16)
    strip = shape((2 * (tiles + 2) * margin, LANES), bf16)

    za, zb = pl.pallas_call(
        edges_kernel,
        out_shape=(side, side),
        in_specs=[SMEM, SMEM, ANY],
        out_specs=(VMEM, VMEM),
        scratch_shapes=[pltpu.VMEM((2, tile_r, LANES), f32)] * 2 + [pltpu.SemaphoreType.DMA((2, 2))],
        name="edges",
    )(places, lives, object_field)
    own = za
    za, zb = swap(za, "col", 0), swap(zb, "col", 1)
    obj, canvas = pl.pallas_call(
        prepare_kernel,
        out_shape=(shape(padded, f32), shape(padded, f32)),
        in_specs=[ANY],
        out_specs=(VMEM, VMEM),
        scratch_shapes=[pltpu.SemaphoreType.DMA((2, tiles))],
        compiler_params=pltpu.CompilerParams(vmem_limit_bytes=4 << 20),
        cost_estimate=pl.CostEstimate(flops=4 << 20, bytes_accessed=16 << 20, transcendentals=0),
        name="prepare",
    )(object_field)
    obj, fwd, bwd, ext = lax.optimization_barrier((obj, fwd, bwd, ext))
    packed = shape((strip.shape[0] + 3 * PACK, LANES), bf16)
    obj, ya, yb, meta = pl.pallas_call(
        sides_kernel,
        out_shape=(shape(padded, f32), packed, packed, shape((3 * PACK, LANES), bf16)),
        in_specs=[VMEM] * 4,
        out_specs=(VMEM,) * 4,
        input_output_aliases={0: 0},
        compiler_params=pltpu.CompilerParams(vmem_limit_bytes=4 << 20),
        name="sides",
    )(obj, za, zb, own)
    ya, yb = swap(ya, "row", 0), swap(yb, "row", 1)
    amps = amplitudes.reshape(batches * slots, window, window)
    scratch = [
        pltpu.SMEM((batches * slots,), jnp.int32),
        pltpu.VMEM((GROUP, 2, 2, window, LANES), f32),
        pltpu.VMEM((2 * window, GROUP * window), bf16),
        pltpu.VMEM((GROUP, window, 2 * window), bf16),
        pltpu.VMEM((GROUP, 2 * window, 2 * window), bf16),
    ]
    canvas = pl.pallas_call(
        functools.partial(slots_kernel, False),
        out_shape=shape(padded, f32),
        in_specs=[SMEM, SMEM] + [VMEM] * 7,
        out_specs=VMEM,
        input_output_aliases={3: 0},
        scratch_shapes=scratch,
        compiler_params=pltpu.CompilerParams(vmem_limit_bytes=14 << 20),
        cost_estimate=pl.CostEstimate(flops=4 << 30, bytes_accessed=20 << 20, transcendentals=0),
        name="inner",
    )(places, lives, obj, canvas, probe, amps, fwd, bwd, ext)
    _, canvas, ra, rb = pl.pallas_call(
        functools.partial(slots_kernel, True),
        out_shape=(shape(padded, f32), shape(padded, f32), strip, strip),
        in_specs=[SMEM, SMEM] + [VMEM] * 9,
        out_specs=(VMEM,) * 4,
        input_output_aliases={2: 0, 3: 1},
        scratch_shapes=scratch,
        compiler_params=pltpu.CompilerParams(vmem_limit_bytes=14 << 20),
        name="outer",
    )(places, lives, obj, canvas, ya, yb, probe, amps, fwd, bwd, ext)
    ra, rb = swap(ra, "row", 0), swap(rb, "row", 1)
    scale = pl.pallas_call(
        light_kernel,
        out_shape=shape((tiles, tile_r, LANES), f32),
        in_specs=[VMEM] * 4,
        out_specs=VMEM,
        scratch_shapes=[
            pltpu.VMEM((2, window, LANES), f32),
            pltpu.VMEM((tiles + 4, tile_r + 2 * window, LANES), f32),
            pltpu.VMEM((PACK, LANES), jnp.int32),
            pltpu.SMEM((PACK, LANES), jnp.int32),
            pltpu.SemaphoreType.DMA,
        ],
        compiler_params=pltpu.CompilerParams(vmem_limit_bytes=9 << 20),
        cost_estimate=pl.CostEstimate(flops=8 << 20, bytes_accessed=12 << 20, transcendentals=0),
        name="light",
    )(meta, ya, yb, probe)
    canvas, scale = lax.optimization_barrier((canvas, scale))
    ya, yb = ra, rb
    rim = shape((2 * tile_r, LANES), bf16)
    sa, sb = pl.pallas_call(
        strips_kernel,
        out_shape=(rim, rim),
        in_specs=[VMEM] * 3,
        out_specs=(VMEM, VMEM),
        compiler_params=pltpu.CompilerParams(vmem_limit_bytes=4 << 20),
        name="strips",
    )(canvas, ya, yb)
    sa, sb = swap(sa, "col", 0), swap(sb, "col", 1)
    block = pl.BlockSpec((2, margin, tile_c), lambda i: (0, i, 0))
    field = shape((2, tile_r, tile_c), f32)
    return pl.pallas_call(
        update_kernel,
        grid=(tile_r // margin,),
        out_shape=(field, field),
        in_specs=[block] + [VMEM] * 6,
        out_specs=(block, block),
        compiler_params=pltpu.CompilerParams(vmem_limit_bytes=8 << 20),
        name="update",
    )(object_field, canvas, ya, yb, sa, sb, scale)


def solution(mesh):
    in_specs = (
        P(None, "row", "col"),
        P(),
        P("row", "col", None, None, None, None),
        P("row", "col", None, None, None),
        P("row", "col", None),
    )
    out_specs = (P(None, "row", "col"), P(None, "row", "col"))
    return jax.shard_map(
        on_device, mesh=mesh, in_specs=in_specs, out_specs=out_specs, check_vma=False
    )
```

```python
import functools
import math

import jax
import jax.numpy as jnp
from jax import lax
from jax.experimental import pallas as pl
from jax.experimental.pallas import tpu as pltpu
from jax.sharding import PartitionSpec as P

step_scale = 0.5
LANES = 128
PACK = 16
CHUNK = 32
GROUP = 2
f32 = jnp.float32
bf16 = jnp.bfloat16
VMEM = pl.BlockSpec(memory_space=pltpu.VMEM)
SMEM = pl.BlockSpec(memory_space=pltpu.SMEM)
ANY = pl.BlockSpec(memory_space=pl.ANY)


def swap(block, axis, parity):
    size = lax.axis_size(axis)
    route = []
    for i in range(parity, size - 1, 2):
        route += [(i, i + 1), (i + 1, i)]
    return lax.ppermute(block, axis, route)


def even(axis):
    return lax.rem(lax.axis_index(axis), 2) == 0


def dft_parts(window):
    counter = jnp.arange(window, dtype=jnp.int32)
    product = counter[:, None] * counter[None, :] % window
    angles = 2.0 * math.pi / window * product.astype(f32)
    scale_value = 1.0 / math.sqrt(window)
    return (
        (jnp.cos(angles) * scale_value).astype(bf16),
        (-jnp.sin(angles) * scale_value).astype(bf16),
    )


def meta_rows(pos_ref, counts_ref):
    batches, slots = pos_ref.shape[2], pos_ref.shape[4]
    lane = lax.broadcasted_iota(jnp.int32, (PACK, LANES), 1)
    row = jnp.zeros((PACK, LANES), jnp.int32)
    fields = 2 * batches * slots
    for k in range(fields):
        value = pos_ref[0, 0, k // (2 * slots), k % 2, k // 2 % slots] + LANES
        row = jnp.where(lane == k, value // 16, row)
        row = jnp.where(lane == fields + k, lax.rem(value, 16), row)
    for k in range(batches):
        row = jnp.where(lane == 2 * fields + k, counts_ref[0, 0, k], row)
    return row.astype(f32).astype(bf16)


def edges_kernel(pos_ref, counts_ref, obj_hbm, first_ref, second_ref, low, high, sem):
    tile_r, tile_c = obj_hbm.shape[1:]
    part = 256
    copies = []
    for k in range(2 * tile_r // part):
        c, r = divmod(k * part, tile_r)
        for side, (start, target) in enumerate(((0, low), (tile_c - LANES, high))):
            source = obj_hbm.at[c, pl.ds(r, part), pl.ds(start, LANES)]
            copies.append(pltpu.make_async_copy(source, target.at[pl.ds(k * part, part), :], sem.at[side, k]))
    for copy in copies:
        copy.start()
    upward = even("col")
    meta = meta_rows(pos_ref, counts_ref)
    first_ref[2 * tile_r :, :] = meta
    second_ref[2 * tile_r :, :] = meta
    for k in range(2 * tile_r // part):
        copies[2 * k].wait()
        copies[2 * k + 1].wait()
        rows = slice(k * part, (k + 1) * part)
        a, b = low[rows, :], high[rows, :]
        first_ref[rows, :] = jnp.where(upward, b, a).astype(bf16)
        second_ref[rows, :] = jnp.where(upward, a, b).astype(bf16)


def prepare_kernel(obj_hbm, obj_ref, canvas_ref, sem):
    tile_r, tile_c = obj_hbm.shape[1:]
    margin = (obj_ref.shape[2] - tile_r) // 2
    tiles = tile_c // LANES
    body = pl.ds(margin, tile_r)
    copies = [
        pltpu.make_async_copy(
            obj_hbm.at[c, :, pl.ds(LANES * t, LANES)], obj_ref.at[c, t + 1, body, :], sem.at[c, t]
        )
        for c in range(2)
        for t in range(tiles)
    ]
    for copy in copies:
        copy.start()
    canvas_ref[...] = jnp.zeros_like(canvas_ref)
    for k, copy in enumerate(copies):
        copy.wait()
        c, t = divmod(k, tiles)
        obj_ref[c, t + 1, body, :] = obj_ref[c, t + 1, body, :].astype(bf16).astype(f32)


def sides_kernel(obj_in, za_ref, zb_ref, own_ref, obj_ref, ya_ref, yb_ref, meta_ref):
    tiles = obj_ref.shape[1] - 2
    margin = LANES
    tile_r = obj_ref.shape[2] - 2 * margin
    right_first = even("col")
    downward = even("row")
    for c in range(2):
        for r in range(0, tile_r, 128):
            rows = slice(c * tile_r + r, c * tile_r + r + 128)
            a = za_ref[rows, :].astype(f32)
            b = zb_ref[rows, :].astype(f32)
            at = slice(margin + r, margin + r + 128)
            obj_ref[c, 0, at, :] = jnp.where(right_first, b, a)
            obj_ref[c, tiles + 1, at, :] = jnp.where(right_first, a, b)
    for c in range(2):
        for t in range(tiles + 2):
            top = obj_ref[c, t, margin : 2 * margin, :]
            bottom = obj_ref[c, t, tile_r : tile_r + margin, :]
            k = (c * (tiles + 2) + t) * margin
            ya_ref[k : k + margin, :] = jnp.where(downward, bottom, top).astype(bf16)
            yb_ref[k : k + margin, :] = jnp.where(downward, top, bottom).astype(bf16)
    tail = 2 * (tiles + 2) * margin
    a = za_ref[2 * tile_r :, :].astype(f32)
    b = zb_ref[2 * tile_r :, :].astype(f32)
    metas = (jnp.where(right_first, b, a).astype(bf16), own_ref[2 * tile_r :, :], jnp.where(right_first, a, b).astype(bf16))
    for k, meta in enumerate(metas):
        rows = slice(tail + PACK * k, tail + PACK * (k + 1))
        ya_ref[rows, :] = meta
        yb_ref[rows, :] = meta
        meta_ref[PACK * k : PACK * (k + 1), :] = meta


def slots_kernel(outer, *refs):
    if outer:
        (pos_ref, counts_ref, obj_in, canvas_in, ya_ref, yb_ref, probe_ref, amp_ref, fwd_ref, bwd_ref, ext_ref,
         obj, canvas_ref, ra_ref, rb_ref, todo, prb, xs, hs, er) = refs
    else:
        (pos_ref, counts_ref, obj, canvas_in, probe_ref, amp_ref, fwd_ref, bwd_ref, ext_ref,
         canvas_ref, todo, prb, xs, hs, er) = refs
    batches, slots = pos_ref.shape[2], pos_ref.shape[4]
    win = probe_ref.shape[1]
    margin = win // 2
    tiles = obj.shape[1] - 2
    tile_r = obj.shape[2] - 2 * margin
    lower_first = even("row")
    for c in range(2 if outer else 0):
        for t in range(tiles + 2):
            k = (c * (tiles + 2) + t) * margin
            a = ya_ref[k : k + margin, :].astype(f32)
            b = yb_ref[k : k + margin, :].astype(f32)
            obj[c, t, 0:margin, :] = jnp.where(lower_first, b, a)
            obj[c, t, margin + tile_r :, :] = jnp.where(lower_first, a, b)

    def collect(slot, count):
        batch = slot // slots
        row = pos_ref[0, 0, batch, 0, slot - batch * slots]
        inside = (row >= 0) & (row <= tile_r - win)
        live = (slot - batch * slots < counts_ref[0, 0, batch]) & (inside != outer)

        @pl.when(live)
        def _():
            todo[count] = slot

        return count + live.astype(jnp.int32)

    total = lax.fori_loop(0, batches * slots, collect, jnp.int32(0))
    lane = lax.broadcasted_iota(jnp.int32, (CHUNK, LANES), 1)

    def group(p, carry):
        chosen = []
        for g in range(GROUP):
            at = p * GROUP + g
            slot = todo[jnp.minimum(at, total - 1)]
            batch = slot // slots
            row = pos_ref[0, 0, batch, 0, slot - batch * slots] + margin
            col = pos_ref[0, 0, batch, 1, slot - batch * slots] + margin
            tile = col // LANES
            shift = col - tile * LANES
            chosen.append((slot, row, tile, jnp.minimum(tile + 2, tiles + 1), shift, at < total))

        def exit_waves(g):
            slot, row, tile, wrapped, shift, valid = chosen[g]
            low = lane < shift
            for i in range(0, win, CHUNK):
                turned = []
                window = []
                for c in range(2):
                    one = pltpu.roll(probe_ref[c, i : i + CHUNK, 0:LANES], shift, 1)
                    two = pltpu.roll(probe_ref[c, i : i + CHUNK, LANES:], shift, 1)
                    turned.append((jnp.where(low, two, one), jnp.where(low, one, two)))
                    at = pl.ds(row + i, CHUNK)
                    window.append(
                        (jnp.where(low, obj[c, wrapped, at, :], obj[c, tile, at, :]), obj[c, tile + 1, at, :])
                    )
                for h in range(2):
                    pr, pi = turned[0][h], turned[1][h]
                    wr, wi = window[0][h], window[1][h]
                    prb[g, 0, h, i : i + CHUNK, :] = pr
                    prb[g, 1, h, i : i + CHUNK, :] = pi
                    cols = slice(win * g + LANES * h, win * g + LANES * (h + 1))
                    xs[i : i + CHUNK, cols] = (pr * wr - pi * wi).astype(bf16)
                    xs[win + i : win + i + CHUNK, cols] = (pr * wi + pi * wr).astype(bf16)

        def rolled_table(g):
            shift = chosen[g][4]
            for i in range(0, win, CHUNK):
                for h in range(2):
                    real = ext_ref[0, h, pl.ds(win - shift + i, CHUNK), :].astype(bf16)
                    imag = ext_ref[1, h, pl.ds(win - shift + i, CHUNK), :].astype(bf16)
                    a = slice(LANES * h, LANES * (h + 1))
                    b = slice(win + LANES * h, win + LANES * (h + 1))
                    er[g, i : i + CHUNK, a] = real
                    er[g, i : i + CHUNK, b] = imag
                    er[g, win + i : win + i + CHUNK, a] = -imag
                    er[g, win + i : win + i + CHUNK, b] = real

        def rows_dft(table_ref):
            for g in range(GROUP):
                for part in range(2):
                    out = jnp.dot(
                        table_ref[win * part : win * (part + 1), :],
                        xs[:, win * g : win * (g + 1)],
                        preferred_element_type=f32,
                    )
                    hs[g, :, win * part : win * (part + 1)] = out.astype(bf16)

        def residual_waves(g):
            far = jnp.dot(hs[g], er[g], preferred_element_type=f32)
            real, imag = far[:, :win], far[:, win:]
            scale = 1.0 - amp_ref[chosen[g][0]].astype(f32) * lax.rsqrt(real * real + imag * imag + 1.0)
            xs[:win, win * g : win * (g + 1)] = (real * scale).astype(bf16)
            xs[win:, win * g : win * (g + 1)] = (imag * scale).astype(bf16)

        def accumulate(g):
            slot, row, tile, wrapped, shift, valid = chosen[g]
            back = lax.dot_general(hs[g], er[g], (((1,), (1,)), ((), ())), preferred_element_type=f32)
            keep = lax.broadcasted_iota(jnp.int32, (win, LANES), 1) < shift
            at = pl.ds(row, win)
            for h in range(2):
                pr, pi = prb[g, 0, h], prb[g, 1, h]
                br = back[:, LANES * h : LANES * (h + 1)]
                bi = back[:, win + LANES * h : win + LANES * (h + 1)]
                terms = [pr * br + pi * bi, pr * bi - pi * br]
                if g:
                    terms = [jnp.where(valid, term, 0.0) for term in terms]
                for c in range(2):
                    if h == 0:
                        canvas_ref[c, tile, at, :] += jnp.where(keep, 0.0, terms[c])
                        canvas_ref[c, wrapped, at, :] += jnp.where(keep, terms[c], 0.0)
                    else:
                        canvas_ref[c, tile + 1, at, :] += terms[c]

        for g in range(GROUP):
            exit_waves(g)
        rows_dft(fwd_ref)
        for g in range(GROUP):
            rolled_table(g)
        for g in range(GROUP):
            residual_waves(g)
        rows_dft(bwd_ref)
        for g in range(GROUP):
            accumulate(g)
        return carry

    lax.fori_loop(0, (total + GROUP - 1) // GROUP, group, 0)

    for c in range(2 if outer else 0):
        for t in range(tiles + 2):
            k = (c * (tiles + 2) + t) * margin
            top = canvas_ref[c, t, 0:margin, :]
            bottom = canvas_ref[c, t, margin + tile_r :, :]
            ra_ref[k : k + margin, :] = jnp.where(lower_first, bottom, top).astype(bf16)
            rb_ref[k : k + margin, :] = jnp.where(lower_first, top, bottom).astype(bf16)


def light_kernel(meta_ref, ya_ref, yb_ref, probe_ref, scale_ref, power, light, rows_ref, table_ref, sem):
    win = probe_ref.shape[1]
    tiles, tile_r = scale_ref.shape[:2]
    tile_c = tiles * LANES
    batches = 3
    slots = 4
    step = 2 * batches * slots
    lower_first = even("row")
    tail = ya_ref.shape[0] - 3 * PACK
    for k in range(3):
        rows = slice(tail + PACK * k, tail + PACK * (k + 1))
        a, b = ya_ref[rows, :].astype(f32), yb_ref[rows, :].astype(f32)
        rows_ref[k : k + 1, :] = jnp.where(lower_first, b, a)[0:1].astype(jnp.int32)
        rows_ref[3 + k : 4 + k, :] = meta_ref[PACK * k : PACK * (k + 1), :].astype(f32)[0:1].astype(jnp.int32)
        rows_ref[6 + k : 7 + k, :] = jnp.where(lower_first, a, b)[0:1].astype(jnp.int32)
    copy = pltpu.make_async_copy(rows_ref, table_ref, sem)
    copy.start()
    for t in range(tiles + 4):
        light[t] = jnp.zeros_like(light[t])
    for h in range(2):
        cols = slice(LANES * h, LANES * (h + 1))
        real, imag = probe_ref[0, :, cols], probe_ref[1, :, cols]
        power[h] = real * real + imag * imag
    copy.wait()

    def tile_slots(n, carry):
        down = n // 3 - 1
        across = n - (down + 1) * 3 - 1

        def one(slot, inner):
            row = table_ref[n, 2 * slot] * 16 + table_ref[n, step + 2 * slot] - LANES + down * tile_r
            col = table_ref[n, 2 * slot + 1] * 16 + table_ref[n, step + 2 * slot + 1] - LANES + across * tile_c
            meets = (row > -win) & (row < tile_r) & (col > -win) & (col < tile_c)

            @pl.when(meets)
            def _():
                place = col + win
                tile = place // LANES
                shift = place - tile * LANES
                low = lax.broadcasted_iota(jnp.int32, (64, LANES), 1) < shift
                for i in range(0, win, 64):
                    one_half = pltpu.roll(power[0, i : i + 64, :], shift, 1)
                    two_half = pltpu.roll(power[1, i : i + 64, :], shift, 1)
                    at = pl.ds(row + win + i, 64)
                    light[tile, at, :] += jnp.where(low, 0.0, one_half)
                    light[tile + 1, at, :] += jnp.where(low, one_half, two_half)
                    light[tile + 2, at, :] += jnp.where(low, two_half, 0.0)

            return inner

        for batch in range(batches):
            carry = lax.fori_loop(slots * batch, slots * batch + table_ref[n, 2 * step + batch], one, carry)
        return carry

    lax.fori_loop(0, 9, tile_slots, 0)
    for t in range(tiles):
        scale_ref[t] = step_scale / (light[t + 2, win : win + tile_r, :] + 1.0)


def strips_kernel(canvas_ref, ya_ref, yb_ref, sa_ref, sb_ref):
    tiles = canvas_ref.shape[1] - 2
    margin = LANES
    tile_r = canvas_ref.shape[2] - 2 * margin
    lower_first = even("row")
    right_first = even("col")
    for c in range(2):
        for r in range(0, tile_r, margin):
            sides = []
            for t in (0, tiles + 1):
                value = canvas_ref[c, t, margin + r : 2 * margin + r, :]
                k = (c * (tiles + 2) + t) * margin
                a, b = ya_ref[k : k + margin, :].astype(f32), yb_ref[k : k + margin, :].astype(f32)
                if r == 0:
                    value += jnp.where(lower_first, b, a)
                if r == tile_r - margin:
                    value += jnp.where(lower_first, a, b)
                sides.append(value)
            rows = slice(c * tile_r + r, c * tile_r + r + margin)
            sa_ref[rows, :] = jnp.where(right_first, sides[1], sides[0]).astype(bf16)
            sb_ref[rows, :] = jnp.where(right_first, sides[0], sides[1]).astype(bf16)


def update_kernel(outer, *refs):
    if outer:
        obj_ref, canvas_ref, ya_ref, yb_ref, scale_ref, sa_ref, sb_ref, _, _, grad_hbm, out_hbm, grad, out, sem = refs
    else:
        obj_ref, canvas_ref, ya_ref, yb_ref, scale_ref, grad_hbm, out_hbm, grad, out, sem = refs
    tiles = canvas_ref.shape[1] - 2
    margin = LANES
    tile_r = canvas_ref.shape[2] - 2 * margin
    part = 256
    lower_first = even("row")
    right_first = even("col")
    copies = []
    for r in range(0, tile_r, part):
        for k, t in enumerate((0, tiles - 1) if outer else range(1, tiles - 1)):
            cols = slice(LANES * t, LANES * (t + 1))
            rows = slice(r, r + part)
            for c in range(2):
                value = canvas_ref[c, t + 1, margin + r : margin + r + part, :]
                if outer:
                    at = slice(c * tile_r + r, c * tile_r + r + part)
                    a, b = sa_ref[at, :].astype(f32), sb_ref[at, :].astype(f32)
                    value += jnp.where(right_first, b, a) if t == 0 else jnp.where(right_first, a, b)
                at = (c * (tiles + 2) + t + 1) * margin
                if r == 0 or r + part == tile_r:
                    a = ya_ref[at : at + margin, :].astype(f32)
                    b = yb_ref[at : at + margin, :].astype(f32)
                    if r == 0:
                        top = value[:margin] + jnp.where(lower_first, b, a)
                        value = jnp.concatenate([top, value[margin:]], 0)
                    else:
                        bottom = value[part - margin :] + jnp.where(lower_first, a, b)
                        value = jnp.concatenate([value[: part - margin], bottom], 0)
                grad[c, k, rows, :] = value
                out[c, k, rows, :] = obj_ref[c, rows, cols] - scale_ref[t, rows, :] * value
            for n, (source, target) in enumerate(((grad, grad_hbm), (out, out_hbm))):
                copy = pltpu.make_async_copy(
                    source.at[:, k, pl.ds(r, part), :],
                    target.at[:, pl.ds(r, part), pl.ds(LANES * t, LANES)],
                    sem.at[n, k, r // part],
                )
                copy.start()
                copies.append(copy)
    for copy in copies:
        copy.wait()


def on_device(object_field, probe, amplitudes, positions, counts):
    tile_r, tile_c = object_field.shape[1:]
    window = probe.shape[1]
    margin = window // 2
    batches, slots = amplitudes.shape[2:4]
    tiles = tile_c // LANES
    padded = (2, tiles + 2, tile_r + 2 * margin, LANES)
    real, imag = dft_parts(window)
    fwd = jnp.concatenate([jnp.concatenate([real, -imag], 1), jnp.concatenate([imag, real], 1)], 0)
    bwd = jnp.concatenate([jnp.concatenate([real, imag], 1), jnp.concatenate([-imag, real], 1)], 0)
    tables = jnp.stack([real, imag]).astype(f32)
    ext = jnp.concatenate([tables, tables], 1).reshape(2, 2 * window, 2, LANES).transpose(0, 2, 1, 3)
    places = jnp.swapaxes(positions, 3, 4)
    shape = jax.ShapeDtypeStruct
    side = shape((2 * tile_r + PACK, LANES), bf16)
    strip = shape((2 * (tiles + 2) * margin, LANES), bf16)

    za, zb = pl.pallas_call(
        edges_kernel,
        out_shape=(side, side),
        in_specs=[SMEM, SMEM, ANY],
        out_specs=(VMEM, VMEM),
        scratch_shapes=[pltpu.VMEM((2 * tile_r, LANES), f32)] * 2 + [pltpu.SemaphoreType.DMA((2, 2 * tile_r // 256))],
        name="edges",
    )(places, counts, object_field)
    own = za
    za, zb = swap(za, "col", 0), swap(zb, "col", 1)
    obj, canvas = pl.pallas_call(
        prepare_kernel,
        out_shape=(shape(padded, f32), shape(padded, f32)),
        in_specs=[ANY],
        out_specs=(VMEM, VMEM),
        scratch_shapes=[pltpu.SemaphoreType.DMA((2, tiles))],
        compiler_params=pltpu.CompilerParams(vmem_limit_bytes=4 << 20),
        cost_estimate=pl.CostEstimate(flops=4 << 20, bytes_accessed=16 << 20, transcendentals=0),
        name="prepare",
    )(object_field)
    obj, fwd, bwd, ext = lax.optimization_barrier((obj, fwd, bwd, ext))
    packed = shape((strip.shape[0] + 3 * PACK, LANES), bf16)
    obj, ya, yb, meta = pl.pallas_call(
        sides_kernel,
        out_shape=(shape(padded, f32), packed, packed, shape((3 * PACK, LANES), bf16)),
        in_specs=[VMEM] * 4,
        out_specs=(VMEM,) * 4,
        input_output_aliases={0: 0},
        compiler_params=pltpu.CompilerParams(vmem_limit_bytes=4 << 20),
        name="sides",
    )(obj, za, zb, own)
    ya, yb = swap(ya, "row", 0), swap(yb, "row", 1)
    amps = amplitudes.reshape(batches * slots, window, window)
    scratch = [
        pltpu.SMEM((batches * slots,), jnp.int32),
        pltpu.VMEM((GROUP, 2, 2, window, LANES), f32),
        pltpu.VMEM((2 * window, GROUP * window), bf16),
        pltpu.VMEM((GROUP, window, 2 * window), bf16),
        pltpu.VMEM((GROUP, 2 * window, 2 * window), bf16),
    ]
    canvas = pl.pallas_call(
        functools.partial(slots_kernel, False),
        out_shape=shape(padded, f32),
        in_specs=[SMEM, SMEM] + [VMEM] * 7,
        out_specs=VMEM,
        input_output_aliases={3: 0},
        scratch_shapes=scratch,
        compiler_params=pltpu.CompilerParams(vmem_limit_bytes=14 << 20),
        cost_estimate=pl.CostEstimate(flops=4 << 30, bytes_accessed=20 << 20, transcendentals=0),
        name="inner",
    )(places, counts, obj, canvas, probe, amps, fwd, bwd, ext)
    _, canvas, ra, rb = pl.pallas_call(
        functools.partial(slots_kernel, True),
        out_shape=(shape(padded, f32), shape(padded, f32), strip, strip),
        in_specs=[SMEM, SMEM] + [VMEM] * 9,
        out_specs=(VMEM,) * 4,
        input_output_aliases={2: 0, 3: 1},
        scratch_shapes=scratch,
        compiler_params=pltpu.CompilerParams(vmem_limit_bytes=14 << 20),
        name="outer",
    )(places, counts, obj, canvas, ya, yb, probe, amps, fwd, bwd, ext)
    ra, rb = swap(ra, "row", 0), swap(rb, "row", 1)
    scale = pl.pallas_call(
        light_kernel,
        out_shape=shape((tiles, tile_r, LANES), f32),
        in_specs=[VMEM] * 4,
        out_specs=VMEM,
        scratch_shapes=[
            pltpu.VMEM((2, window, LANES), f32),
            pltpu.VMEM((tiles + 4, tile_r + 2 * window, LANES), f32),
            pltpu.VMEM((PACK, LANES), jnp.int32),
            pltpu.SMEM((PACK, LANES), jnp.int32),
            pltpu.SemaphoreType.DMA,
        ],
        compiler_params=pltpu.CompilerParams(vmem_limit_bytes=9 << 20),
        cost_estimate=pl.CostEstimate(flops=8 << 20, bytes_accessed=12 << 20, transcendentals=0),
        name="light",
    )(meta, ya, yb, probe)
    canvas, scale = lax.optimization_barrier((canvas, scale))
    rim = shape((2 * tile_r, LANES), bf16)
    sa, sb = pl.pallas_call(
        strips_kernel,
        out_shape=(rim, rim),
        in_specs=[VMEM] * 3,
        out_specs=(VMEM, VMEM),
        compiler_params=pltpu.CompilerParams(vmem_limit_bytes=4 << 20),
        name="strips",
    )(canvas, ra, rb)
    sa, sb = swap(sa, "col", 0), swap(sb, "col", 1)
    field = shape((2, tile_r, tile_c), f32)

    def update(outer, aliases, *args):
        return pl.pallas_call(
            functools.partial(update_kernel, outer),
            out_shape=(field, field),
            in_specs=[VMEM] * (7 if outer else 5) + [ANY] * len(aliases),
            out_specs=(ANY, ANY),
            input_output_aliases=aliases,
            scratch_shapes=[pltpu.VMEM((2, 2, tile_r, LANES), f32)] * 2
            + [pltpu.SemaphoreType.DMA((2, 2, tile_r // 256))],
            compiler_params=pltpu.CompilerParams(vmem_limit_bytes=8 << 20),
            cost_estimate=pl.CostEstimate(flops=4 << 20, bytes_accessed=10 << 20, transcendentals=0),
            name="rims" if outer else "middle",
        )(*args)

    grad, out = update(False, {}, object_field, canvas, ra, rb, scale)
    return update(True, {7: 0, 8: 1}, object_field, canvas, ra, rb, scale, sa, sb, grad, out)


def solution(mesh):
    in_specs = (
        P(None, "row", "col"),
        P(),
        P("row", "col", None, None, None, None),
        P("row", "col", None, None, None),
        P("row", "col", None),
    )
    out_specs = (P(None, "row", "col"), P(None, "row", "col"))
    return jax.shard_map(
        on_device, mesh=mesh, in_specs=in_specs, out_specs=out_specs, check_vma=False
    )
```

```python
import functools
import math

import jax
import jax.numpy as jnp
from jax import lax
from jax.experimental import pallas as pl
from jax.experimental.pallas import tpu as pltpu
from jax.sharding import PartitionSpec as P

step_scale = 0.5
LANES = 128
PACK = 16
CHUNK = 32
GROUP = 2
f32 = jnp.float32
bf16 = jnp.bfloat16
VMEM = pl.BlockSpec(memory_space=pltpu.VMEM)
SMEM = pl.BlockSpec(memory_space=pltpu.SMEM)
ANY = pl.BlockSpec(memory_space=pl.ANY)


def swap(block, axis, parity):
    size = lax.axis_size(axis)
    route = []
    for i in range(parity, size - 1, 2):
        route += [(i, i + 1), (i + 1, i)]
    return lax.ppermute(block, axis, route)


def even(axis):
    return lax.rem(lax.axis_index(axis), 2) == 0


def dft_parts(window):
    counter = jnp.arange(window, dtype=jnp.int32)
    product = counter[:, None] * counter[None, :] % window
    angles = 2.0 * math.pi / window * product.astype(f32)
    scale_value = 1.0 / math.sqrt(window)
    return (
        (jnp.cos(angles) * scale_value).astype(bf16),
        (-jnp.sin(angles) * scale_value).astype(bf16),
    )


def meta_rows(pos_ref, counts_ref):
    batches, slots = pos_ref.shape[2], pos_ref.shape[4]
    lane = lax.broadcasted_iota(jnp.int32, (PACK, LANES), 1)
    row = jnp.zeros((PACK, LANES), jnp.int32)
    fields = 2 * batches * slots
    for k in range(fields):
        value = pos_ref[0, 0, k // (2 * slots), k % 2, k // 2 % slots] + LANES
        row = jnp.where(lane == k, value // 16, row)
        row = jnp.where(lane == fields + k, lax.rem(value, 16), row)
    for k in range(batches):
        row = jnp.where(lane == 2 * fields + k, counts_ref[0, 0, k], row)
    return row.astype(f32).astype(bf16)


def edges_kernel(pos_ref, counts_ref, obj_hbm, first_ref, second_ref, meta_ref, low, high, sem):
    tile_r, tile_c = obj_hbm.shape[1:]
    part = 256
    copies = []
    for k in range(2 * tile_r // part):
        c, r = divmod(k * part, tile_r)
        for side, (start, target) in enumerate(((0, low), (tile_c - LANES, high))):
            source = obj_hbm.at[c, pl.ds(r, part), pl.ds(start, LANES)]
            copies.append(pltpu.make_async_copy(source, target.at[pl.ds(k * part, part), :], sem.at[side, k]))
    for copy in copies:
        copy.start()
    upward = even("col")
    meta = meta_rows(pos_ref, counts_ref)
    first_ref[2 * tile_r :, :] = meta
    second_ref[2 * tile_r :, :] = meta
    meta_ref[...] = meta
    for k in range(2 * tile_r // part):
        copies[2 * k].wait()
        copies[2 * k + 1].wait()
        rows = slice(k * part, (k + 1) * part)
        a, b = low[rows, :], high[rows, :]
        first_ref[rows, :] = jnp.where(upward, b, a).astype(bf16)
        second_ref[rows, :] = jnp.where(upward, a, b).astype(bf16)


def prepare_kernel(obj_hbm, obj_ref, canvas_ref, sem):
    tile_r, tile_c = obj_hbm.shape[1:]
    margin = (obj_ref.shape[2] - tile_r) // 2
    tiles = tile_c // LANES
    body = pl.ds(margin, tile_r)
    copies = [
        pltpu.make_async_copy(
            obj_hbm.at[c, :, pl.ds(LANES * t, LANES)], obj_ref.at[c, t + 1, body, :], sem.at[c, t]
        )
        for c in range(2)
        for t in range(tiles)
    ]
    for copy in copies:
        copy.start()
    canvas_ref[...] = jnp.zeros_like(canvas_ref)
    for k, copy in enumerate(copies):
        copy.wait()
        c, t = divmod(k, tiles)
        obj_ref[c, t + 1, body, :] = obj_ref[c, t + 1, body, :].astype(bf16).astype(f32)


def sides_kernel(obj_in, za_ref, zb_ref, own_ref, obj_ref, ya_ref, yb_ref, meta_ref):
    tiles = obj_ref.shape[1] - 2
    margin = LANES
    tile_r = obj_ref.shape[2] - 2 * margin
    right_first = even("col")
    downward = even("row")
    for c in range(2):
        for r in range(0, tile_r, 128):
            rows = slice(c * tile_r + r, c * tile_r + r + 128)
            a = za_ref[rows, :].astype(f32)
            b = zb_ref[rows, :].astype(f32)
            at = slice(margin + r, margin + r + 128)
            obj_ref[c, 0, at, :] = jnp.where(right_first, b, a)
            obj_ref[c, tiles + 1, at, :] = jnp.where(right_first, a, b)
    for c in range(2):
        for t in range(tiles + 2):
            top = obj_ref[c, t, margin : 2 * margin, :]
            bottom = obj_ref[c, t, tile_r : tile_r + margin, :]
            k = (c * (tiles + 2) + t) * margin
            ya_ref[k : k + margin, :] = jnp.where(downward, bottom, top).astype(bf16)
            yb_ref[k : k + margin, :] = jnp.where(downward, top, bottom).astype(bf16)
    tail = 2 * (tiles + 2) * margin
    a = za_ref[2 * tile_r :, :].astype(f32)
    b = zb_ref[2 * tile_r :, :].astype(f32)
    metas = (jnp.where(right_first, b, a).astype(bf16), own_ref[...], jnp.where(right_first, a, b).astype(bf16))
    for k, meta in enumerate(metas):
        rows = slice(tail + PACK * k, tail + PACK * (k + 1))
        ya_ref[rows, :] = meta
        yb_ref[rows, :] = meta
        meta_ref[PACK * k : PACK * (k + 1), :] = meta


def slots_kernel(kind, *refs):
    if kind in ("far", "near"):
        (pos_ref, counts_ref, obj_in, canvas_in, halo_ref, probe_ref, amp_ref, fwd_ref, bwd_ref, ext_ref,
         obj, canvas_ref, rim_ref, todo, prb, xs, hs, er) = refs
    else:
        (pos_ref, counts_ref, obj, canvas_in, probe_ref, amp_ref, fwd_ref, bwd_ref, ext_ref,
         canvas_ref, todo, prb, xs, hs, er) = refs
    batches, slots = pos_ref.shape[2], pos_ref.shape[4]
    win = probe_ref.shape[1]
    margin = win // 2
    tiles = obj.shape[1] - 2
    tile_r = obj.shape[2] - 2 * margin
    tile_c = tiles * LANES
    upper = even("row") == (kind == "far")
    place = pl.multiple_of(jnp.where(upper, 0, margin + tile_r), margin)
    if kind in ("far", "near"):
        for c in range(2):
            for t in range(tiles + 2):
                k = (c * (tiles + 2) + t) * margin
                obj[c, t, pl.ds(place, margin), :] = halo_ref[k : k + margin, :].astype(f32)

    def member(row, col):
        inside = (row >= 0) & (row <= tile_r - win)
        between = (col >= 0) & (col <= tile_c - win)
        if kind == "core":
            return inside & between
        if kind == "inner":
            return inside & jnp.logical_not(between)
        return jnp.logical_not(inside) & ((row < 0) == upper)

    def collect(slot, count):
        batch = slot // slots
        row = pos_ref[0, 0, batch, 0, slot - batch * slots]
        col = pos_ref[0, 0, batch, 1, slot - batch * slots]
        live = (slot - batch * slots < counts_ref[0, 0, batch]) & member(row, col)

        @pl.when(live)
        def _():
            todo[count] = slot

        return count + live.astype(jnp.int32)

    total = lax.fori_loop(0, batches * slots, collect, jnp.int32(0))
    lane = lax.broadcasted_iota(jnp.int32, (CHUNK, LANES), 1)

    def group(p, carry):
        chosen = []
        for g in range(GROUP):
            at = p * GROUP + g
            slot = todo[jnp.minimum(at, total - 1)]
            batch = slot // slots
            row = pos_ref[0, 0, batch, 0, slot - batch * slots] + margin
            col = pos_ref[0, 0, batch, 1, slot - batch * slots] + margin
            tile = col // LANES
            shift = col - tile * LANES
            chosen.append((slot, row, tile, jnp.minimum(tile + 2, tiles + 1), shift, at < total))

        def exit_waves(g):
            slot, row, tile, wrapped, shift, valid = chosen[g]
            low = lane < shift
            for i in range(0, win, CHUNK):
                turned = []
                window = []
                for c in range(2):
                    one = pltpu.roll(probe_ref[c, i : i + CHUNK, 0:LANES], shift, 1)
                    two = pltpu.roll(probe_ref[c, i : i + CHUNK, LANES:], shift, 1)
                    turned.append((jnp.where(low, two, one), jnp.where(low, one, two)))
                    at = pl.ds(row + i, CHUNK)
                    window.append(
                        (jnp.where(low, obj[c, wrapped, at, :], obj[c, tile, at, :]), obj[c, tile + 1, at, :])
                    )
                for h in range(2):
                    pr, pi = turned[0][h], turned[1][h]
                    wr, wi = window[0][h], window[1][h]
                    prb[g, 0, h, i : i + CHUNK, :] = pr
                    prb[g, 1, h, i : i + CHUNK, :] = pi
                    cols = slice(win * g + LANES * h, win * g + LANES * (h + 1))
                    xs[i : i + CHUNK, cols] = (pr * wr - pi * wi).astype(bf16)
                    xs[win + i : win + i + CHUNK, cols] = (pr * wi + pi * wr).astype(bf16)

        def rolled_table(g):
            shift = chosen[g][4]
            for i in range(0, win, CHUNK):
                for h in range(2):
                    real = ext_ref[0, h, pl.ds(win - shift + i, CHUNK), :].astype(bf16)
                    imag = ext_ref[1, h, pl.ds(win - shift + i, CHUNK), :].astype(bf16)
                    a = slice(LANES * h, LANES * (h + 1))
                    b = slice(win + LANES * h, win + LANES * (h + 1))
                    er[g, i : i + CHUNK, a] = real
                    er[g, i : i + CHUNK, b] = imag
                    er[g, win + i : win + i + CHUNK, a] = -imag
                    er[g, win + i : win + i + CHUNK, b] = real

        def rows_dft(table_ref):
            for g in range(GROUP):
                for part in range(2):
                    out = jnp.dot(
                        table_ref[win * part : win * (part + 1), :],
                        xs[:, win * g : win * (g + 1)],
                        preferred_element_type=f32,
                    )
                    hs[g, :, win * part : win * (part + 1)] = out.astype(bf16)

        def residual_waves(g):
            far = jnp.dot(hs[g], er[g], preferred_element_type=f32)
            real, imag = far[:, :win], far[:, win:]
            scale = 1.0 - amp_ref[chosen[g][0]].astype(f32) * lax.rsqrt(real * real + imag * imag + 1.0)
            xs[:win, win * g : win * (g + 1)] = (real * scale).astype(bf16)
            xs[win:, win * g : win * (g + 1)] = (imag * scale).astype(bf16)

        def accumulate(g):
            slot, row, tile, wrapped, shift, valid = chosen[g]
            back = lax.dot_general(hs[g], er[g], (((1,), (1,)), ((), ())), preferred_element_type=f32)
            keep = lax.broadcasted_iota(jnp.int32, (win, LANES), 1) < shift
            at = pl.ds(row, win)
            for h in range(2):
                pr, pi = prb[g, 0, h], prb[g, 1, h]
                br = back[:, LANES * h : LANES * (h + 1)]
                bi = back[:, win + LANES * h : win + LANES * (h + 1)]
                terms = [pr * br + pi * bi, pr * bi - pi * br]
                if g:
                    terms = [jnp.where(valid, term, 0.0) for term in terms]
                for c in range(2):
                    if h == 0:
                        canvas_ref[c, tile, at, :] += jnp.where(keep, 0.0, terms[c])
                        canvas_ref[c, wrapped, at, :] += jnp.where(keep, terms[c], 0.0)
                    else:
                        canvas_ref[c, tile + 1, at, :] += terms[c]

        for g in range(GROUP):
            exit_waves(g)
        rows_dft(fwd_ref)
        for g in range(GROUP):
            rolled_table(g)
        for g in range(GROUP):
            residual_waves(g)
        rows_dft(bwd_ref)
        for g in range(GROUP):
            accumulate(g)
        return carry

    lax.fori_loop(0, (total + GROUP - 1) // GROUP, group, 0)

    if kind in ("far", "near"):
        for c in range(2):
            for t in range(tiles + 2):
                k = (c * (tiles + 2) + t) * margin
                rim_ref[k : k + margin, :] = canvas_ref[c, t, pl.ds(place, margin), :].astype(bf16)


def light_kernel(meta_ref, ya_ref, yb_ref, probe_ref, scale_ref, power, light, rows_ref, table_ref, sem):
    win = probe_ref.shape[1]
    tiles, tile_r = scale_ref.shape[:2]
    tile_c = tiles * LANES
    batches = 3
    slots = 4
    step = 2 * batches * slots
    lower_first = even("row")
    tail = ya_ref.shape[0] - 3 * PACK
    for k in range(3):
        rows = slice(tail + PACK * k, tail + PACK * (k + 1))
        a, b = ya_ref[rows, :].astype(f32), yb_ref[rows, :].astype(f32)
        rows_ref[k : k + 1, :] = jnp.where(lower_first, b, a)[0:1].astype(jnp.int32)
        rows_ref[3 + k : 4 + k, :] = meta_ref[PACK * k : PACK * (k + 1), :].astype(f32)[0:1].astype(jnp.int32)
        rows_ref[6 + k : 7 + k, :] = jnp.where(lower_first, a, b)[0:1].astype(jnp.int32)
    copy = pltpu.make_async_copy(rows_ref, table_ref, sem)
    copy.start()
    for t in range(tiles + 4):
        light[t] = jnp.zeros_like(light[t])
    for h in range(2):
        cols = slice(LANES * h, LANES * (h + 1))
        real, imag = probe_ref[0, :, cols], probe_ref[1, :, cols]
        power[h] = real * real + imag * imag
    copy.wait()

    def tile_slots(n, carry):
        down = n // 3 - 1
        across = n - (down + 1) * 3 - 1

        def one(slot, inner):
            row = table_ref[n, 2 * slot] * 16 + table_ref[n, step + 2 * slot] - LANES + down * tile_r
            col = table_ref[n, 2 * slot + 1] * 16 + table_ref[n, step + 2 * slot + 1] - LANES + across * tile_c
            meets = (row > -win) & (row < tile_r) & (col > -win) & (col < tile_c)

            @pl.when(meets)
            def _():
                place = col + win
                tile = place // LANES
                shift = place - tile * LANES
                low = lax.broadcasted_iota(jnp.int32, (64, LANES), 1) < shift
                for i in range(0, win, 64):
                    one_half = pltpu.roll(power[0, i : i + 64, :], shift, 1)
                    two_half = pltpu.roll(power[1, i : i + 64, :], shift, 1)
                    at = pl.ds(row + win + i, 64)
                    light[tile, at, :] += jnp.where(low, 0.0, one_half)
                    light[tile + 1, at, :] += jnp.where(low, one_half, two_half)
                    light[tile + 2, at, :] += jnp.where(low, two_half, 0.0)

            return inner

        for batch in range(batches):
            carry = lax.fori_loop(slots * batch, slots * batch + table_ref[n, 2 * step + batch], one, carry)
        return carry

    lax.fori_loop(0, 9, tile_slots, 0)
    for t in range(tiles):
        scale_ref[t] = step_scale / (light[t + 2, win : win + tile_r, :] + 1.0)


def strips_kernel(canvas_ref, ya_ref, yb_ref, sa_ref, sb_ref):
    tiles = canvas_ref.shape[1] - 2
    margin = LANES
    tile_r = canvas_ref.shape[2] - 2 * margin
    lower_first = even("row")
    right_first = even("col")
    for c in range(2):
        for r in range(0, tile_r, margin):
            sides = []
            for t in (0, tiles + 1):
                value = canvas_ref[c, t, margin + r : 2 * margin + r, :]
                k = (c * (tiles + 2) + t) * margin
                a, b = ya_ref[k : k + margin, :].astype(f32), yb_ref[k : k + margin, :].astype(f32)
                if r == 0:
                    value += jnp.where(lower_first, b, a)
                if r == tile_r - margin:
                    value += jnp.where(lower_first, a, b)
                sides.append(value)
            rows = slice(c * tile_r + r, c * tile_r + r + margin)
            sa_ref[rows, :] = jnp.where(right_first, sides[1], sides[0]).astype(bf16)
            sb_ref[rows, :] = jnp.where(right_first, sides[0], sides[1]).astype(bf16)


def update_kernel(outer, *refs):
    if outer:
        obj_ref, canvas_ref, ya_ref, yb_ref, scale_ref, sa_ref, sb_ref, _, _, grad_hbm, out_hbm, grad, out, sem = refs
    else:
        obj_ref, canvas_ref, ya_ref, yb_ref, scale_ref, grad_hbm, out_hbm, grad, out, sem = refs
    tiles = canvas_ref.shape[1] - 2
    margin = LANES
    tile_r = canvas_ref.shape[2] - 2 * margin
    part = 256
    lower_first = even("row")
    right_first = even("col")
    copies = []
    for r in range(0, tile_r, part):
        for k, t in enumerate((0, tiles - 1) if outer else range(1, tiles - 1)):
            cols = slice(LANES * t, LANES * (t + 1))
            rows = slice(r, r + part)
            for c in range(2):
                value = canvas_ref[c, t + 1, margin + r : margin + r + part, :]
                if outer:
                    at = slice(c * tile_r + r, c * tile_r + r + part)
                    a, b = sa_ref[at, :].astype(f32), sb_ref[at, :].astype(f32)
                    value += jnp.where(right_first, b, a) if t == 0 else jnp.where(right_first, a, b)
                at = (c * (tiles + 2) + t + 1) * margin
                if r == 0 or r + part == tile_r:
                    a = ya_ref[at : at + margin, :].astype(f32)
                    b = yb_ref[at : at + margin, :].astype(f32)
                    if r == 0:
                        top = value[:margin] + jnp.where(lower_first, b, a)
                        value = jnp.concatenate([top, value[margin:]], 0)
                    else:
                        bottom = value[part - margin :] + jnp.where(lower_first, a, b)
                        value = jnp.concatenate([value[: part - margin], bottom], 0)
                grad[c, k, rows, :] = value
                out[c, k, rows, :] = obj_ref[c, rows, cols] - scale_ref[t, rows, :] * value
            for n, (source, target) in enumerate(((grad, grad_hbm), (out, out_hbm))):
                copy = pltpu.make_async_copy(
                    source.at[:, k, pl.ds(r, part), :],
                    target.at[:, pl.ds(r, part), pl.ds(LANES * t, LANES)],
                    sem.at[n, k, r // part],
                )
                copy.start()
                copies.append(copy)
    for copy in copies:
        copy.wait()


def on_device(object_field, probe, amplitudes, positions, counts):
    tile_r, tile_c = object_field.shape[1:]
    window = probe.shape[1]
    margin = window // 2
    batches, slots = amplitudes.shape[2:4]
    tiles = tile_c // LANES
    padded = (2, tiles + 2, tile_r + 2 * margin, LANES)
    real, imag = dft_parts(window)
    fwd = jnp.concatenate([jnp.concatenate([real, -imag], 1), jnp.concatenate([imag, real], 1)], 0)
    bwd = jnp.concatenate([jnp.concatenate([real, imag], 1), jnp.concatenate([-imag, real], 1)], 0)
    tables = jnp.stack([real, imag]).astype(f32)
    ext = jnp.concatenate([tables, tables], 1).reshape(2, 2 * window, 2, LANES).transpose(0, 2, 1, 3)
    places = jnp.swapaxes(positions, 3, 4)
    shape = jax.ShapeDtypeStruct
    side = shape((2 * tile_r + PACK, LANES), bf16)
    strip = shape((2 * (tiles + 2) * margin, LANES), bf16)

    za, zb, own = pl.pallas_call(
        edges_kernel,
        out_shape=(side, side, shape((PACK, LANES), bf16)),
        in_specs=[SMEM, SMEM, ANY],
        out_specs=(VMEM,) * 3,
        scratch_shapes=[pltpu.VMEM((2 * tile_r, LANES), f32)] * 2 + [pltpu.SemaphoreType.DMA((2, 2 * tile_r // 256))],
        name="edges",
    )(places, counts, object_field)
    za, zb = swap(za, "col", 0), swap(zb, "col", 1)
    obj, canvas = pl.pallas_call(
        prepare_kernel,
        out_shape=(shape(padded, f32), shape(padded, f32)),
        in_specs=[ANY],
        out_specs=(VMEM, VMEM),
        scratch_shapes=[pltpu.SemaphoreType.DMA((2, tiles))],
        compiler_params=pltpu.CompilerParams(vmem_limit_bytes=4 << 20),
        cost_estimate=pl.CostEstimate(flops=4 << 20, bytes_accessed=16 << 20, transcendentals=0),
        name="prepare",
    )(object_field)
    obj, fwd, bwd, ext = lax.optimization_barrier((obj, fwd, bwd, ext))
    amps = amplitudes.reshape(batches * slots, window, window)
    tail = (probe, amps, fwd, bwd, ext)

    def run(kind, obj, canvas, *halo):
        edge = len(halo)
        big = shape(padded, f32)
        return pl.pallas_call(
            functools.partial(slots_kernel, kind),
            out_shape=(big, big, strip) if edge else big,
            in_specs=[SMEM, SMEM] + [VMEM] * (7 + edge),
            out_specs=(VMEM,) * 3 if edge else VMEM,
            input_output_aliases={2: 0, 3: 1} if edge else {3: 0},
            scratch_shapes=[
                pltpu.SMEM((batches * slots,), jnp.int32),
                pltpu.VMEM((GROUP, 2, 2, window, LANES), f32),
                pltpu.VMEM((2 * window, GROUP * window), bf16),
                pltpu.VMEM((GROUP, window, 2 * window), bf16),
                pltpu.VMEM((GROUP, 2 * window, 2 * window), bf16),
            ],
            compiler_params=pltpu.CompilerParams(vmem_limit_bytes=14 << 20),
            cost_estimate=pl.CostEstimate(flops=2 << 30, bytes_accessed=8 << 20, transcendentals=0),
            name=kind,
        )(places, counts, obj, canvas, *halo, *tail)

    canvas = run("core", obj, canvas)
    obj, canvas, za, zb = lax.optimization_barrier((obj, canvas, za, zb))
    packed = shape((strip.shape[0] + 3 * PACK, LANES), bf16)
    obj, ya, yb, meta = pl.pallas_call(
        sides_kernel,
        out_shape=(shape(padded, f32), packed, packed, shape((3 * PACK, LANES), bf16)),
        in_specs=[VMEM] * 4,
        out_specs=(VMEM,) * 4,
        input_output_aliases={0: 0},
        compiler_params=pltpu.CompilerParams(vmem_limit_bytes=4 << 20),
        name="sides",
    )(obj, za, zb, own)
    yb, ya = swap(yb, "row", 1), swap(ya, "row", 0)
    canvas = run("inner", obj, canvas)
    obj, canvas, rb = run("far", obj, canvas, yb)
    rb = swap(rb, "row", 1)
    obj, canvas, ra = run("near", obj, canvas, ya)
    ra = swap(ra, "row", 0)
    rim = shape((2 * tile_r, LANES), bf16)
    sa, sb = pl.pallas_call(
        strips_kernel,
        out_shape=(rim, rim),
        in_specs=[VMEM] * 3,
        out_specs=(VMEM, VMEM),
        compiler_params=pltpu.CompilerParams(vmem_limit_bytes=4 << 20),
        name="strips",
    )(canvas, ra, rb)
    sa, sb, probe = lax.optimization_barrier((sa, sb, probe))
    sa, sb = swap(sa, "col", 0), swap(sb, "col", 1)
    scale = pl.pallas_call(
        light_kernel,
        out_shape=shape((tiles, tile_r, LANES), f32),
        in_specs=[VMEM] * 4,
        out_specs=VMEM,
        scratch_shapes=[
            pltpu.VMEM((2, window, LANES), f32),
            pltpu.VMEM((tiles + 4, tile_r + 2 * window, LANES), f32),
            pltpu.VMEM((PACK, LANES), jnp.int32),
            pltpu.SMEM((PACK, LANES), jnp.int32),
            pltpu.SemaphoreType.DMA,
        ],
        compiler_params=pltpu.CompilerParams(vmem_limit_bytes=9 << 20),
        cost_estimate=pl.CostEstimate(flops=8 << 20, bytes_accessed=12 << 20, transcendentals=0),
        name="light",
    )(meta, ya, yb, probe)
    field = shape((2, tile_r, tile_c), f32)

    def update(outer, aliases, *args):
        return pl.pallas_call(
            functools.partial(update_kernel, outer),
            out_shape=(field, field),
            in_specs=[VMEM] * (7 if outer else 5) + [ANY] * len(aliases),
            out_specs=(ANY, ANY),
            input_output_aliases=aliases,
            scratch_shapes=[pltpu.VMEM((2, 2, tile_r, LANES), f32)] * 2
            + [pltpu.SemaphoreType.DMA((2, 2, tile_r // 256))],
            compiler_params=pltpu.CompilerParams(vmem_limit_bytes=8 << 20),
            cost_estimate=pl.CostEstimate(flops=4 << 20, bytes_accessed=10 << 20, transcendentals=0),
            name="rims" if outer else "middle",
        )(*args)

    grad, out = update(False, {}, object_field, canvas, ra, rb, scale)
    return update(True, {7: 0, 8: 1}, object_field, canvas, ra, rb, scale, sa, sb, grad, out)


def solution(mesh):
    in_specs = (
        P(None, "row", "col"),
        P(),
        P("row", "col", None, None, None, None),
        P("row", "col", None, None, None),
        P("row", "col", None),
    )
    out_specs = (P(None, "row", "col"), P(None, "row", "col"))
    return jax.shard_map(
        on_device, mesh=mesh, in_specs=in_specs, out_specs=out_specs, check_vma=False
    )
```

```python
import functools
import math

import jax
import jax.numpy as jnp
from jax import lax
from jax.experimental import pallas as pl
from jax.experimental.pallas import tpu as pltpu
from jax.sharding import PartitionSpec as P

step_scale = 0.5
LANES = 128
PACK = 16
CHUNK = 32
GROUP = 2
f32 = jnp.float32
bf16 = jnp.bfloat16
VMEM = pl.BlockSpec(memory_space=pltpu.VMEM)
SMEM = pl.BlockSpec(memory_space=pltpu.SMEM)
ANY = pl.BlockSpec(memory_space=pl.ANY)


def swap(block, axis, parity):
    size = lax.axis_size(axis)
    route = []
    for i in range(parity, size - 1, 2):
        route += [(i, i + 1), (i + 1, i)]
    return lax.ppermute(block, axis, route)


def even(axis):
    return lax.rem(lax.axis_index(axis), 2) == 0


def dft_parts(window):
    counter = jnp.arange(window, dtype=jnp.int32)
    product = counter[:, None] * counter[None, :] % window
    angles = 2.0 * math.pi / window * product.astype(f32)
    scale_value = 1.0 / math.sqrt(window)
    return (
        (jnp.cos(angles) * scale_value).astype(bf16),
        (-jnp.sin(angles) * scale_value).astype(bf16),
    )


def meta_rows(pos_ref, counts_ref):
    batches, slots = pos_ref.shape[2], pos_ref.shape[4]
    lane = lax.broadcasted_iota(jnp.int32, (PACK, LANES), 1)
    row = jnp.zeros((PACK, LANES), jnp.int32)
    fields = 2 * batches * slots
    for k in range(fields):
        value = pos_ref[0, 0, k // (2 * slots), k % 2, k // 2 % slots] + LANES
        row = jnp.where(lane == k, value // 16, row)
        row = jnp.where(lane == fields + k, lax.rem(value, 16), row)
    for k in range(batches):
        row = jnp.where(lane == 2 * fields + k, counts_ref[0, 0, k], row)
    return row.astype(f32).astype(bf16)


def edges_kernel(pos_ref, counts_ref, obj_hbm, first_ref, second_ref, meta_ref, low, high, sem):
    tile_r, tile_c = obj_hbm.shape[1:]
    part = 256
    copies = []
    for k in range(2 * tile_r // part):
        c, r = divmod(k * part, tile_r)
        for side, (start, target) in enumerate(((0, low), (tile_c - LANES, high))):
            source = obj_hbm.at[c, pl.ds(r, part), pl.ds(start, LANES)]
            copies.append(pltpu.make_async_copy(source, target.at[pl.ds(k * part, part), :], sem.at[side, k]))
    for copy in copies:
        copy.start()
    upward = even("col")
    meta = meta_rows(pos_ref, counts_ref)
    first_ref[2 * tile_r :, :] = meta
    second_ref[2 * tile_r :, :] = meta
    meta_ref[...] = meta
    for k in range(2 * tile_r // part):
        copies[2 * k].wait()
        copies[2 * k + 1].wait()
        rows = slice(k * part, (k + 1) * part)
        a, b = low[rows, :], high[rows, :]
        first_ref[rows, :] = jnp.where(upward, b, a).astype(bf16)
        second_ref[rows, :] = jnp.where(upward, a, b).astype(bf16)


def prepare_kernel(obj_hbm, obj_ref, canvas_ref, sem):
    tile_r, tile_c = obj_hbm.shape[1:]
    margin = (obj_ref.shape[2] - tile_r) // 2
    tiles = tile_c // LANES
    body = pl.ds(margin, tile_r)
    copies = [
        pltpu.make_async_copy(
            obj_hbm.at[c, :, pl.ds(LANES * t, LANES)], obj_ref.at[c, t + 1, body, :], sem.at[c, t]
        )
        for c in range(2)
        for t in range(tiles)
    ]
    for copy in copies:
        copy.start()
    canvas_ref[...] = jnp.zeros_like(canvas_ref)
    for k, copy in enumerate(copies):
        copy.wait()
        c, t = divmod(k, tiles)
        obj_ref[c, t + 1, body, :] = obj_ref[c, t + 1, body, :].astype(bf16).astype(f32)


def sides_kernel(obj_in, za_ref, zb_ref, own_ref, obj_ref, ya_ref, yb_ref, meta_ref):
    tiles = obj_ref.shape[1] - 2
    margin = LANES
    tile_r = obj_ref.shape[2] - 2 * margin
    right_first = even("col")
    downward = even("row")
    for c in range(2):
        for r in range(0, tile_r, 128):
            rows = slice(c * tile_r + r, c * tile_r + r + 128)
            a = za_ref[rows, :].astype(f32)
            b = zb_ref[rows, :].astype(f32)
            at = slice(margin + r, margin + r + 128)
            obj_ref[c, 0, at, :] = jnp.where(right_first, b, a)
            obj_ref[c, tiles + 1, at, :] = jnp.where(right_first, a, b)
    for c in range(2):
        for t in range(tiles + 2):
            top = obj_ref[c, t, margin : 2 * margin, :]
            bottom = obj_ref[c, t, tile_r : tile_r + margin, :]
            k = (c * (tiles + 2) + t) * margin
            ya_ref[k : k + margin, :] = jnp.where(downward, bottom, top).astype(bf16)
            yb_ref[k : k + margin, :] = jnp.where(downward, top, bottom).astype(bf16)
    tail = 2 * (tiles + 2) * margin
    a = za_ref[2 * tile_r :, :].astype(f32)
    b = zb_ref[2 * tile_r :, :].astype(f32)
    metas = (jnp.where(right_first, b, a).astype(bf16), own_ref[...], jnp.where(right_first, a, b).astype(bf16))
    for k, meta in enumerate(metas):
        rows = slice(tail + PACK * k, tail + PACK * (k + 1))
        ya_ref[rows, :] = meta
        yb_ref[rows, :] = meta
        meta_ref[PACK * k : PACK * (k + 1), :] = meta


def slots_kernel(kind, *refs):
    if kind in ("far", "near"):
        (pos_ref, counts_ref, obj_in, canvas_in, halo_ref, probe_ref, amp_ref, fwd_ref, bwd_ref, ext_ref,
         obj, canvas_ref, rim_ref, todo, prb, xs, hs, er) = refs
    else:
        (pos_ref, counts_ref, obj, canvas_in, probe_ref, amp_ref, fwd_ref, bwd_ref, ext_ref,
         canvas_ref, todo, prb, xs, hs, er) = refs
    batches, slots = pos_ref.shape[2], pos_ref.shape[4]
    win = probe_ref.shape[1]
    margin = win // 2
    tiles = obj.shape[1] - 2
    tile_r = obj.shape[2] - 2 * margin
    tile_c = tiles * LANES
    upper = even("row") == (kind == "far")
    place = pl.multiple_of(jnp.where(upper, 0, margin + tile_r), margin)
    if kind in ("far", "near"):
        for c in range(2):
            for t in range(tiles + 2):
                k = (c * (tiles + 2) + t) * margin
                obj[c, t, pl.ds(place, margin), :] = halo_ref[k : k + margin, :].astype(f32)

    def member(row, col):
        inside = (row >= 0) & (row <= tile_r - win)
        between = (col >= 0) & (col <= tile_c - win)
        if kind == "core":
            return inside & between
        if kind == "inner":
            return inside & jnp.logical_not(between)
        return jnp.logical_not(inside) & ((row < 0) == upper)

    def collect(slot, count):
        batch = slot // slots
        row = pos_ref[0, 0, batch, 0, slot - batch * slots]
        col = pos_ref[0, 0, batch, 1, slot - batch * slots]
        live = (slot - batch * slots < counts_ref[0, 0, batch]) & member(row, col)

        @pl.when(live)
        def _():
            todo[count] = slot

        return count + live.astype(jnp.int32)

    total = lax.fori_loop(0, batches * slots, collect, jnp.int32(0))
    lane = lax.broadcasted_iota(jnp.int32, (CHUNK, LANES), 1)

    def group(first, width):
        chosen = []
        for g in range(width):
            slot = todo[first + g]
            batch = slot // slots
            row = pos_ref[0, 0, batch, 0, slot - batch * slots] + margin
            col = pos_ref[0, 0, batch, 1, slot - batch * slots] + margin
            tile = col // LANES
            shift = col - tile * LANES
            chosen.append((slot, row, tile, jnp.minimum(tile + 2, tiles + 1), shift))

        def exit_waves(g):
            slot, row, tile, wrapped, shift = chosen[g]
            low = lane < shift
            for i in range(0, win, CHUNK):
                turned = []
                window = []
                for c in range(2):
                    one = pltpu.roll(probe_ref[c, i : i + CHUNK, 0:LANES], shift, 1)
                    two = pltpu.roll(probe_ref[c, i : i + CHUNK, LANES:], shift, 1)
                    turned.append((jnp.where(low, two, one), jnp.where(low, one, two)))
                    at = pl.ds(row + i, CHUNK)
                    window.append(
                        (jnp.where(low, obj[c, wrapped, at, :], obj[c, tile, at, :]), obj[c, tile + 1, at, :])
                    )
                for h in range(2):
                    pr, pi = turned[0][h], turned[1][h]
                    wr, wi = window[0][h], window[1][h]
                    prb[g, 0, h, i : i + CHUNK, :] = pr
                    prb[g, 1, h, i : i + CHUNK, :] = pi
                    cols = slice(win * g + LANES * h, win * g + LANES * (h + 1))
                    xs[i : i + CHUNK, cols] = (pr * wr - pi * wi).astype(bf16)
                    xs[win + i : win + i + CHUNK, cols] = (pr * wi + pi * wr).astype(bf16)

        def rolled_table(g):
            shift = chosen[g][4]
            for i in range(0, win, CHUNK):
                for h in range(2):
                    real = ext_ref[0, h, pl.ds(win - shift + i, CHUNK), :].astype(bf16)
                    imag = ext_ref[1, h, pl.ds(win - shift + i, CHUNK), :].astype(bf16)
                    a = slice(LANES * h, LANES * (h + 1))
                    b = slice(win + LANES * h, win + LANES * (h + 1))
                    er[g, i : i + CHUNK, a] = real
                    er[g, i : i + CHUNK, b] = imag
                    er[g, win + i : win + i + CHUNK, a] = -imag
                    er[g, win + i : win + i + CHUNK, b] = real

        def rows_dft(table_ref):
            for g in range(width):
                for part in range(2):
                    out = jnp.dot(
                        table_ref[win * part : win * (part + 1), :],
                        xs[:, win * g : win * (g + 1)],
                        preferred_element_type=f32,
                    )
                    hs[g, :, win * part : win * (part + 1)] = out.astype(bf16)

        def residual_waves(g):
            far = jnp.dot(hs[g], er[g], preferred_element_type=f32)
            real, imag = far[:, :win], far[:, win:]
            scale = 1.0 - amp_ref[chosen[g][0]].astype(f32) * lax.rsqrt(real * real + imag * imag + 1.0)
            xs[:win, win * g : win * (g + 1)] = (real * scale).astype(bf16)
            xs[win:, win * g : win * (g + 1)] = (imag * scale).astype(bf16)

        def accumulate(g):
            slot, row, tile, wrapped, shift = chosen[g]
            back = lax.dot_general(hs[g], er[g], (((1,), (1,)), ((), ())), preferred_element_type=f32)
            keep = lax.broadcasted_iota(jnp.int32, (win, LANES), 1) < shift
            at = pl.ds(row, win)
            for h in range(2):
                pr, pi = prb[g, 0, h], prb[g, 1, h]
                br = back[:, LANES * h : LANES * (h + 1)]
                bi = back[:, win + LANES * h : win + LANES * (h + 1)]
                terms = [pr * br + pi * bi, pr * bi - pi * br]
                for c in range(2):
                    if h == 0:
                        canvas_ref[c, tile, at, :] += jnp.where(keep, 0.0, terms[c])
                        canvas_ref[c, wrapped, at, :] += jnp.where(keep, terms[c], 0.0)
                    else:
                        canvas_ref[c, tile + 1, at, :] += terms[c]

        for g in range(width):
            exit_waves(g)
        rows_dft(fwd_ref)
        for g in range(width):
            rolled_table(g)
        for g in range(width):
            residual_waves(g)
        rows_dft(bwd_ref)
        for g in range(width):
            accumulate(g)

    def full_group(p, carry):
        group(p * GROUP, GROUP)
        return carry

    lax.fori_loop(0, total // GROUP, full_group, 0)

    @pl.when(lax.rem(total, GROUP) == 1)
    def _():
        group(total - 1, 1)

    if kind in ("far", "near"):
        for c in range(2):
            for t in range(tiles + 2):
                k = (c * (tiles + 2) + t) * margin
                rim_ref[k : k + margin, :] = canvas_ref[c, t, pl.ds(place, margin), :].astype(bf16)


def light_kernel(meta_ref, ya_ref, yb_ref, probe_ref, scale_ref, power, light, rows_ref, table_ref, sem):
    win = probe_ref.shape[1]
    tiles, tile_r = scale_ref.shape[:2]
    tile_c = tiles * LANES
    batches = 3
    slots = 4
    step = 2 * batches * slots
    lower_first = even("row")
    tail = ya_ref.shape[0] - 3 * PACK
    for k in range(3):
        rows = slice(tail + PACK * k, tail + PACK * (k + 1))
        a, b = ya_ref[rows, :].astype(f32), yb_ref[rows, :].astype(f32)
        rows_ref[k : k + 1, :] = jnp.where(lower_first, b, a)[0:1].astype(jnp.int32)
        rows_ref[3 + k : 4 + k, :] = meta_ref[PACK * k : PACK * (k + 1), :].astype(f32)[0:1].astype(jnp.int32)
        rows_ref[6 + k : 7 + k, :] = jnp.where(lower_first, a, b)[0:1].astype(jnp.int32)
    copy = pltpu.make_async_copy(rows_ref, table_ref, sem)
    copy.start()
    for t in range(tiles + 4):
        light[t] = jnp.zeros_like(light[t])
    for h in range(2):
        cols = slice(LANES * h, LANES * (h + 1))
        real, imag = probe_ref[0, :, cols], probe_ref[1, :, cols]
        power[h] = real * real + imag * imag
    copy.wait()

    def tile_slots(n, carry):
        down = n // 3 - 1
        across = n - (down + 1) * 3 - 1

        def one(slot, inner):
            row = table_ref[n, 2 * slot] * 16 + table_ref[n, step + 2 * slot] - LANES + down * tile_r
            col = table_ref[n, 2 * slot + 1] * 16 + table_ref[n, step + 2 * slot + 1] - LANES + across * tile_c
            meets = (row > -win) & (row < tile_r) & (col > -win) & (col < tile_c)

            @pl.when(meets)
            def _():
                place = col + win
                tile = place // LANES
                shift = place - tile * LANES
                low = lax.broadcasted_iota(jnp.int32, (64, LANES), 1) < shift
                for i in range(0, win, 64):
                    one_half = pltpu.roll(power[0, i : i + 64, :], shift, 1)
                    two_half = pltpu.roll(power[1, i : i + 64, :], shift, 1)
                    at = pl.ds(row + win + i, 64)
                    light[tile, at, :] += jnp.where(low, 0.0, one_half)
                    light[tile + 1, at, :] += jnp.where(low, one_half, two_half)
                    light[tile + 2, at, :] += jnp.where(low, two_half, 0.0)

            return inner

        for batch in range(batches):
            carry = lax.fori_loop(slots * batch, slots * batch + table_ref[n, 2 * step + batch], one, carry)
        return carry

    lax.fori_loop(0, 9, tile_slots, 0)
    for t in range(tiles):
        scale_ref[t] = step_scale / (light[t + 2, win : win + tile_r, :] + 1.0)


def strips_kernel(canvas_ref, ya_ref, yb_ref, sa_ref, sb_ref):
    tiles = canvas_ref.shape[1] - 2
    margin = LANES
    tile_r = canvas_ref.shape[2] - 2 * margin
    lower_first = even("row")
    right_first = even("col")
    for c in range(2):
        for r in range(0, tile_r, margin):
            sides = []
            for t in (0, tiles + 1):
                value = canvas_ref[c, t, margin + r : 2 * margin + r, :]
                k = (c * (tiles + 2) + t) * margin
                a, b = ya_ref[k : k + margin, :].astype(f32), yb_ref[k : k + margin, :].astype(f32)
                if r == 0:
                    value += jnp.where(lower_first, b, a)
                if r == tile_r - margin:
                    value += jnp.where(lower_first, a, b)
                sides.append(value)
            rows = slice(c * tile_r + r, c * tile_r + r + margin)
            sa_ref[rows, :] = jnp.where(right_first, sides[1], sides[0]).astype(bf16)
            sb_ref[rows, :] = jnp.where(right_first, sides[0], sides[1]).astype(bf16)


def update_kernel(outer, *refs):
    if outer:
        obj_ref, canvas_ref, ya_ref, yb_ref, scale_ref, sa_ref, sb_ref, _, _, grad_hbm, out_hbm, grad, out, sem = refs
    else:
        obj_ref, canvas_ref, ya_ref, yb_ref, scale_ref, grad_hbm, out_hbm, grad, out, sem = refs
    tiles = canvas_ref.shape[1] - 2
    margin = LANES
    tile_r = canvas_ref.shape[2] - 2 * margin
    part = 256
    lower_first = even("row")
    right_first = even("col")
    copies = []
    for r in range(0, tile_r, part):
        for k, t in enumerate((0, tiles - 1) if outer else range(1, tiles - 1)):
            cols = slice(LANES * t, LANES * (t + 1))
            rows = slice(r, r + part)
            for c in range(2):
                value = canvas_ref[c, t + 1, margin + r : margin + r + part, :]
                if outer:
                    at = slice(c * tile_r + r, c * tile_r + r + part)
                    a, b = sa_ref[at, :].astype(f32), sb_ref[at, :].astype(f32)
                    value += jnp.where(right_first, b, a) if t == 0 else jnp.where(right_first, a, b)
                at = (c * (tiles + 2) + t + 1) * margin
                if r == 0 or r + part == tile_r:
                    a = ya_ref[at : at + margin, :].astype(f32)
                    b = yb_ref[at : at + margin, :].astype(f32)
                    if r == 0:
                        top = value[:margin] + jnp.where(lower_first, b, a)
                        value = jnp.concatenate([top, value[margin:]], 0)
                    else:
                        bottom = value[part - margin :] + jnp.where(lower_first, a, b)
                        value = jnp.concatenate([value[: part - margin], bottom], 0)
                grad[c, k, rows, :] = value
                out[c, k, rows, :] = obj_ref[c, rows, cols] - scale_ref[t, rows, :] * value
            for n, (source, target) in enumerate(((grad, grad_hbm), (out, out_hbm))):
                copy = pltpu.make_async_copy(
                    source.at[:, k, pl.ds(r, part), :],
                    target.at[:, pl.ds(r, part), pl.ds(LANES * t, LANES)],
                    sem.at[n, k, r // part],
                )
                copy.start()
                copies.append(copy)
    for copy in copies:
        copy.wait()


def on_device(object_field, probe, amplitudes, positions, counts):
    tile_r, tile_c = object_field.shape[1:]
    window = probe.shape[1]
    margin = window // 2
    batches, slots = amplitudes.shape[2:4]
    tiles = tile_c // LANES
    padded = (2, tiles + 2, tile_r + 2 * margin, LANES)
    real, imag = dft_parts(window)
    fwd = jnp.concatenate([jnp.concatenate([real, -imag], 1), jnp.concatenate([imag, real], 1)], 0)
    bwd = jnp.concatenate([jnp.concatenate([real, imag], 1), jnp.concatenate([-imag, real], 1)], 0)
    tables = jnp.stack([real, imag]).astype(f32)
    ext = jnp.concatenate([tables, tables], 1).reshape(2, 2 * window, 2, LANES).transpose(0, 2, 1, 3)
    places = jnp.swapaxes(positions, 3, 4)
    shape = jax.ShapeDtypeStruct
    side = shape((2 * tile_r + PACK, LANES), bf16)
    strip = shape((2 * (tiles + 2) * margin, LANES), bf16)

    za, zb, own = pl.pallas_call(
        edges_kernel,
        out_shape=(side, side, shape((PACK, LANES), bf16)),
        in_specs=[SMEM, SMEM, ANY],
        out_specs=(VMEM,) * 3,
        scratch_shapes=[pltpu.VMEM((2 * tile_r, LANES), f32)] * 2 + [pltpu.SemaphoreType.DMA((2, 2 * tile_r // 256))],
        name="edges",
    )(places, counts, object_field)
    za, zb = swap(za, "col", 0), swap(zb, "col", 1)
    obj, canvas = pl.pallas_call(
        prepare_kernel,
        out_shape=(shape(padded, f32), shape(padded, f32)),
        in_specs=[ANY],
        out_specs=(VMEM, VMEM),
        scratch_shapes=[pltpu.SemaphoreType.DMA((2, tiles))],
        compiler_params=pltpu.CompilerParams(vmem_limit_bytes=4 << 20),
        cost_estimate=pl.CostEstimate(flops=4 << 20, bytes_accessed=16 << 20, transcendentals=0),
        name="prepare",
    )(object_field)
    obj, fwd, bwd, ext = lax.optimization_barrier((obj, fwd, bwd, ext))
    amps = amplitudes.reshape(batches * slots, window, window)
    tail = (probe, amps, fwd, bwd, ext)

    def run(kind, obj, canvas, *halo):
        edge = len(halo)
        big = shape(padded, f32)
        return pl.pallas_call(
            functools.partial(slots_kernel, kind),
            out_shape=(big, big, strip) if edge else big,
            in_specs=[SMEM, SMEM] + [VMEM] * (7 + edge),
            out_specs=(VMEM,) * 3 if edge else VMEM,
            input_output_aliases={2: 0, 3: 1} if edge else {3: 0},
            scratch_shapes=[
                pltpu.SMEM((batches * slots,), jnp.int32),
                pltpu.VMEM((GROUP, 2, 2, window, LANES), f32),
                pltpu.VMEM((2 * window, GROUP * window), bf16),
                pltpu.VMEM((GROUP, window, 2 * window), bf16),
                pltpu.VMEM((GROUP, 2 * window, 2 * window), bf16),
            ],
            compiler_params=pltpu.CompilerParams(vmem_limit_bytes=14 << 20),
            cost_estimate=pl.CostEstimate(flops=2 << 30, bytes_accessed=8 << 20, transcendentals=0),
            name=kind,
        )(places, counts, obj, canvas, *halo, *tail)

    canvas = run("core", obj, canvas)
    obj, canvas, za, zb = lax.optimization_barrier((obj, canvas, za, zb))
    packed = shape((strip.shape[0] + 3 * PACK, LANES), bf16)
    obj, ya, yb, meta = pl.pallas_call(
        sides_kernel,
        out_shape=(shape(padded, f32), packed, packed, shape((3 * PACK, LANES), bf16)),
        in_specs=[VMEM] * 4,
        out_specs=(VMEM,) * 4,
        input_output_aliases={0: 0},
        compiler_params=pltpu.CompilerParams(vmem_limit_bytes=4 << 20),
        name="sides",
    )(obj, za, zb, own)
    yb, ya = swap(yb, "row", 1), swap(ya, "row", 0)
    canvas = run("inner", obj, canvas)
    obj, canvas, rb = run("far", obj, canvas, yb)
    rb = swap(rb, "row", 1)
    obj, canvas, ra = run("near", obj, canvas, ya)
    ra = swap(ra, "row", 0)
    rim = shape((2 * tile_r, LANES), bf16)
    sa, sb = pl.pallas_call(
        strips_kernel,
        out_shape=(rim, rim),
        in_specs=[VMEM] * 3,
        out_specs=(VMEM, VMEM),
        compiler_params=pltpu.CompilerParams(vmem_limit_bytes=4 << 20),
        name="strips",
    )(canvas, ra, rb)
    sa, sb, probe = lax.optimization_barrier((sa, sb, probe))
    sa, sb = swap(sa, "col", 0), swap(sb, "col", 1)
    scale = pl.pallas_call(
        light_kernel,
        out_shape=shape((tiles, tile_r, LANES), f32),
        in_specs=[VMEM] * 4,
        out_specs=VMEM,
        scratch_shapes=[
            pltpu.VMEM((2, window, LANES), f32),
            pltpu.VMEM((tiles + 4, tile_r + 2 * window, LANES), f32),
            pltpu.VMEM((PACK, LANES), jnp.int32),
            pltpu.SMEM((PACK, LANES), jnp.int32),
            pltpu.SemaphoreType.DMA,
        ],
        compiler_params=pltpu.CompilerParams(vmem_limit_bytes=9 << 20),
        cost_estimate=pl.CostEstimate(flops=8 << 20, bytes_accessed=12 << 20, transcendentals=0),
        name="light",
    )(meta, ya, yb, probe)
    field = shape((2, tile_r, tile_c), f32)

    def update(outer, aliases, *args):
        return pl.pallas_call(
            functools.partial(update_kernel, outer),
            out_shape=(field, field),
            in_specs=[VMEM] * (7 if outer else 5) + [ANY] * len(aliases),
            out_specs=(ANY, ANY),
            input_output_aliases=aliases,
            scratch_shapes=[pltpu.VMEM((2, 2, tile_r, LANES), f32)] * 2
            + [pltpu.SemaphoreType.DMA((2, 2, tile_r // 256))],
            compiler_params=pltpu.CompilerParams(vmem_limit_bytes=8 << 20),
            cost_estimate=pl.CostEstimate(flops=4 << 20, bytes_accessed=10 << 20, transcendentals=0),
            name="rims" if outer else "middle",
        )(*args)

    grad, out = update(False, {}, object_field, canvas, ra, rb, scale)
    return update(True, {7: 0, 8: 1}, object_field, canvas, ra, rb, scale, sa, sb, grad, out)


def solution(mesh):
    in_specs = (
        P(None, "row", "col"),
        P(),
        P("row", "col", None, None, None, None),
        P("row", "col", None, None, None),
        P("row", "col", None),
    )
    out_specs = (P(None, "row", "col"), P(None, "row", "col"))
    return jax.shard_map(
        on_device, mesh=mesh, in_specs=in_specs, out_specs=out_specs, check_vma=False
    )
```

```python
import functools
import math

import jax
import jax.numpy as jnp
import ml_dtypes
import numpy as np
from jax import lax
from jax.experimental import pallas as pl
from jax.experimental.pallas import tpu as pltpu
from jax.sharding import PartitionSpec as P

step_scale = 0.5
LANES = 128
PACK = 16
CHUNK = 32
GROUP = 2
f32 = jnp.float32
bf16 = jnp.bfloat16
VMEM = pl.BlockSpec(memory_space=pltpu.VMEM)
SMEM = pl.BlockSpec(memory_space=pltpu.SMEM)
ANY = pl.BlockSpec(memory_space=pl.ANY)


def swap(block, axis, parity):
    size = lax.axis_size(axis)
    route = []
    for i in range(parity, size - 1, 2):
        route += [(i, i + 1), (i + 1, i)]
    return lax.ppermute(block, axis, route)


def even(axis):
    return lax.rem(lax.axis_index(axis), 2) == 0


def dft_parts(window):
    counter = np.arange(window)
    angles = 2.0 * math.pi / window * (counter[:, None] * counter[None, :] % window)
    scale_value = 1.0 / math.sqrt(window)
    parts = np.stack([np.cos(angles), -np.sin(angles)]) * scale_value
    return parts.astype(np.float32).astype(ml_dtypes.bfloat16)


def meta_rows(pos_ref, counts_ref):
    batches, slots = pos_ref.shape[2], pos_ref.shape[4]
    lane = lax.broadcasted_iota(jnp.int32, (PACK, LANES), 1)
    row = jnp.zeros((PACK, LANES), jnp.int32)
    fields = 2 * batches * slots
    for k in range(fields):
        value = pos_ref[0, 0, k // (2 * slots), k % 2, k // 2 % slots] + LANES
        row = jnp.where(lane == k, value // 16, row)
        row = jnp.where(lane == fields + k, lax.rem(value, 16), row)
    for k in range(batches):
        row = jnp.where(lane == 2 * fields + k, counts_ref[0, 0, k], row)
    return row.astype(f32).astype(bf16)


def edges_kernel(pos_ref, counts_ref, obj_hbm, first_ref, second_ref, meta_ref, low, high, sem):
    tile_r, tile_c = obj_hbm.shape[1:]
    part = 256
    copies = []
    for k in range(2 * tile_r // part):
        c, r = divmod(k * part, tile_r)
        for side, (start, target) in enumerate(((0, low), (tile_c - LANES, high))):
            source = obj_hbm.at[c, pl.ds(r, part), pl.ds(start, LANES)]
            copies.append(pltpu.make_async_copy(source, target.at[pl.ds(k * part, part), :], sem.at[side, k]))
    for copy in copies:
        copy.start()
    upward = even("col")
    meta = meta_rows(pos_ref, counts_ref)
    first_ref[2 * tile_r :, :] = meta
    second_ref[2 * tile_r :, :] = meta
    meta_ref[...] = meta
    for k in range(2 * tile_r // part):
        copies[2 * k].wait()
        copies[2 * k + 1].wait()
        rows = slice(k * part, (k + 1) * part)
        a, b = low[rows, :], high[rows, :]
        first_ref[rows, :] = jnp.where(upward, b, a).astype(bf16)
        second_ref[rows, :] = jnp.where(upward, a, b).astype(bf16)


def prepare_kernel(obj_hbm, base_ref, obj_ref, canvas_ref, pa_ref, pb_ref, fwd_ref, bwd_ref, ext_ref, sem):
    tile_r, tile_c = obj_hbm.shape[1:]
    margin = (obj_ref.shape[2] - tile_r) // 2
    tiles = tile_c // LANES
    win = base_ref.shape[1]
    body = pl.ds(margin, tile_r)
    copies = [
        pltpu.make_async_copy(
            obj_hbm.at[c, :, pl.ds(LANES * t, LANES)], obj_ref.at[c, t + 1, body, :], sem.at[c, t]
        )
        for c in range(2)
        for t in range(tiles)
    ]
    for copy in copies:
        copy.start()
    downward = even("row")
    for k, copy in enumerate(copies):
        copy.wait()
        c, t = divmod(k, tiles)
        obj_ref[c, t + 1, body, :] = obj_ref[c, t + 1, body, :].astype(bf16).astype(f32)
        top = obj_ref[c, t + 1, margin : 2 * margin, :]
        bottom = obj_ref[c, t + 1, tile_r : tile_r + margin, :]
        rows = slice(k * margin, (k + 1) * margin)
        pa_ref[rows, :] = jnp.where(downward, bottom, top).astype(bf16)
        pb_ref[rows, :] = jnp.where(downward, top, bottom).astype(bf16)
    canvas_ref[...] = jnp.zeros_like(canvas_ref)
    real, imag = base_ref[0], base_ref[1]
    fwd_ref[:win, :win] = real
    fwd_ref[:win, win:] = -imag
    fwd_ref[win:, :win] = imag
    fwd_ref[win:, win:] = real
    bwd_ref[:win, :win] = real
    bwd_ref[:win, win:] = imag
    bwd_ref[win:, :win] = -imag
    bwd_ref[win:, win:] = real
    for n in range(2):
        for h in range(2):
            half = base_ref[n, :, LANES * h : LANES * (h + 1)].astype(f32)
            ext_ref[n, h, :win, :] = half
            ext_ref[n, h, win:, :] = half


def sides_kernel(obj_in, za_ref, zb_ref, own_ref, obj_ref, ca_ref, cb_ref, meta_ref):
    tiles = obj_ref.shape[1] - 2
    margin = LANES
    tile_r = obj_ref.shape[2] - 2 * margin
    right_first = even("col")
    downward = even("row")
    for c in range(2):
        for r in range(0, tile_r, 128):
            rows = slice(c * tile_r + r, c * tile_r + r + 128)
            a = za_ref[rows, :].astype(f32)
            b = zb_ref[rows, :].astype(f32)
            at = slice(margin + r, margin + r + 128)
            obj_ref[c, 0, at, :] = jnp.where(right_first, b, a)
            obj_ref[c, tiles + 1, at, :] = jnp.where(right_first, a, b)
        for h, t in enumerate((0, tiles + 1)):
            top = obj_ref[c, t, margin : 2 * margin, :]
            bottom = obj_ref[c, t, tile_r : tile_r + margin, :]
            k = (2 * c + h) * margin
            ca_ref[k : k + margin, :] = jnp.where(downward, bottom, top).astype(bf16)
            cb_ref[k : k + margin, :] = jnp.where(downward, top, bottom).astype(bf16)
    tail = 4 * margin
    a = za_ref[2 * tile_r :, :].astype(f32)
    b = zb_ref[2 * tile_r :, :].astype(f32)
    metas = (jnp.where(right_first, b, a).astype(bf16), own_ref[...], jnp.where(right_first, a, b).astype(bf16))
    for k, meta in enumerate(metas):
        rows = slice(tail + PACK * k, tail + PACK * (k + 1))
        ca_ref[rows, :] = meta
        cb_ref[rows, :] = meta
        meta_ref[PACK * k : PACK * (k + 1), :] = meta


def slots_kernel(kind, *refs):
    if kind in ("far", "near"):
        (pos_ref, counts_ref, obj_in, canvas_in, halo_ref, corner_ref, probe_ref, amp_ref, fwd_ref, bwd_ref, ext_ref,
         obj, canvas_ref, rim_ref, todo, prb, xs, hs, er) = refs
    else:
        (pos_ref, counts_ref, obj, canvas_in, probe_ref, amp_ref, fwd_ref, bwd_ref, ext_ref,
         canvas_ref, todo, prb, xs, hs, er) = refs
    batches, slots = pos_ref.shape[2], pos_ref.shape[4]
    win = probe_ref.shape[1]
    margin = win // 2
    tiles = obj.shape[1] - 2
    tile_r = obj.shape[2] - 2 * margin
    tile_c = tiles * LANES
    upper = even("row") == (kind == "far")
    place = pl.multiple_of(jnp.where(upper, 0, margin + tile_r), margin)
    if kind in ("far", "near"):
        for c in range(2):
            for t in range(tiles):
                k = (c * tiles + t) * margin
                obj[c, t + 1, pl.ds(place, margin), :] = halo_ref[k : k + margin, :].astype(f32)
            for h, t in enumerate((0, tiles + 1)):
                k = (2 * c + h) * margin
                obj[c, t, pl.ds(place, margin), :] = corner_ref[k : k + margin, :].astype(f32)

    def member(row, col):
        inside = (row >= 0) & (row <= tile_r - win)
        between = (col >= 0) & (col <= tile_c - win)
        if kind == "core":
            return inside & between
        if kind == "inner":
            return inside & jnp.logical_not(between)
        return jnp.logical_not(inside) & ((row < 0) == upper)

    def collect(slot, count):
        batch = slot // slots
        row = pos_ref[0, 0, batch, 0, slot - batch * slots]
        col = pos_ref[0, 0, batch, 1, slot - batch * slots]
        live = (slot - batch * slots < counts_ref[0, 0, batch]) & member(row, col)

        @pl.when(live)
        def _():
            todo[count] = slot

        return count + live.astype(jnp.int32)

    total = lax.fori_loop(0, batches * slots, collect, jnp.int32(0))
    lane = lax.broadcasted_iota(jnp.int32, (CHUNK, LANES), 1)

    def group(first, width):
        chosen = []
        for g in range(width):
            slot = todo[first + g]
            batch = slot // slots
            row = pos_ref[0, 0, batch, 0, slot - batch * slots] + margin
            col = pos_ref[0, 0, batch, 1, slot - batch * slots] + margin
            tile = col // LANES
            shift = col - tile * LANES
            chosen.append((slot, row, tile, jnp.minimum(tile + 2, tiles + 1), shift))

        def exit_waves(g):
            slot, row, tile, wrapped, shift = chosen[g]
            low = lane < shift
            for i in range(0, win, CHUNK):
                turned = []
                window = []
                for c in range(2):
                    one = pltpu.roll(probe_ref[c, i : i + CHUNK, 0:LANES], shift, 1)
                    two = pltpu.roll(probe_ref[c, i : i + CHUNK, LANES:], shift, 1)
                    turned.append((jnp.where(low, two, one), jnp.where(low, one, two)))
                    at = pl.ds(row + i, CHUNK)
                    window.append(
                        (jnp.where(low, obj[c, wrapped, at, :], obj[c, tile, at, :]), obj[c, tile + 1, at, :])
                    )
                for h in range(2):
                    pr, pi = turned[0][h], turned[1][h]
                    wr, wi = window[0][h], window[1][h]
                    prb[g, 0, h, i : i + CHUNK, :] = pr
                    prb[g, 1, h, i : i + CHUNK, :] = pi
                    cols = slice(win * g + LANES * h, win * g + LANES * (h + 1))
                    xs[i : i + CHUNK, cols] = (pr * wr - pi * wi).astype(bf16)
                    xs[win + i : win + i + CHUNK, cols] = (pr * wi + pi * wr).astype(bf16)

        def rolled_table(g):
            shift = chosen[g][4]
            for i in range(0, win, CHUNK):
                for h in range(2):
                    real = ext_ref[0, h, pl.ds(win - shift + i, CHUNK), :].astype(bf16)
                    imag = ext_ref[1, h, pl.ds(win - shift + i, CHUNK), :].astype(bf16)
                    a = slice(LANES * h, LANES * (h + 1))
                    b = slice(win + LANES * h, win + LANES * (h + 1))
                    er[g, i : i + CHUNK, a] = real
                    er[g, i : i + CHUNK, b] = imag
                    er[g, win + i : win + i + CHUNK, a] = -imag
                    er[g, win + i : win + i + CHUNK, b] = real

        def rows_dft(table_ref):
            for g in range(width):
                for part in range(2):
                    out = jnp.dot(
                        table_ref[win * part : win * (part + 1), :],
                        xs[:, win * g : win * (g + 1)],
                        preferred_element_type=f32,
                    )
                    hs[g, :, win * part : win * (part + 1)] = out.astype(bf16)

        def residual_waves(g):
            far = jnp.dot(hs[g], er[g], preferred_element_type=f32)
            real, imag = far[:, :win], far[:, win:]
            scale = 1.0 - amp_ref[chosen[g][0]].astype(f32) * lax.rsqrt(real * real + imag * imag + 1.0)
            xs[:win, win * g : win * (g + 1)] = (real * scale).astype(bf16)
            xs[win:, win * g : win * (g + 1)] = (imag * scale).astype(bf16)

        def accumulate(g):
            slot, row, tile, wrapped, shift = chosen[g]
            back = lax.dot_general(hs[g], er[g], (((1,), (1,)), ((), ())), preferred_element_type=f32)
            keep = lax.broadcasted_iota(jnp.int32, (win, LANES), 1) < shift
            at = pl.ds(row, win)
            for h in range(2):
                pr, pi = prb[g, 0, h], prb[g, 1, h]
                br = back[:, LANES * h : LANES * (h + 1)]
                bi = back[:, win + LANES * h : win + LANES * (h + 1)]
                terms = [pr * br + pi * bi, pr * bi - pi * br]
                for c in range(2):
                    if h == 0:
                        canvas_ref[c, tile, at, :] += jnp.where(keep, 0.0, terms[c])
                        canvas_ref[c, wrapped, at, :] += jnp.where(keep, terms[c], 0.0)
                    else:
                        canvas_ref[c, tile + 1, at, :] += terms[c]

        for g in range(width):
            exit_waves(g)
        rows_dft(fwd_ref)
        for g in range(width):
            rolled_table(g)
        for g in range(width):
            residual_waves(g)
        rows_dft(bwd_ref)
        for g in range(width):
            accumulate(g)

    def full_group(p, carry):
        group(p * GROUP, GROUP)
        return carry

    lax.fori_loop(0, total // GROUP, full_group, 0)

    @pl.when(lax.rem(total, GROUP) == 1)
    def _():
        group(total - 1, 1)

    if kind in ("far", "near"):
        for c in range(2):
            for t in range(tiles + 2):
                k = (c * (tiles + 2) + t) * margin
                rim_ref[k : k + margin, :] = canvas_ref[c, t, pl.ds(place, margin), :].astype(bf16)
        spare = 2 * (tiles + 2) * margin
        if rim_ref.shape[0] > spare:
            rim_ref[spare:, :] = jnp.zeros((rim_ref.shape[0] - spare, LANES), bf16)


def light_kernel(meta_ref, ya_ref, yb_ref, probe_ref, scale_ref, power, light, rows_ref, table_ref, sem):
    win = probe_ref.shape[1]
    tiles, tile_r = scale_ref.shape[:2]
    tile_c = tiles * LANES
    batches = 3
    slots = 4
    step = 2 * batches * slots
    lower_first = even("row")
    tail = ya_ref.shape[0] - 3 * PACK
    for k in range(3):
        rows = slice(tail + PACK * k, tail + PACK * (k + 1))
        a, b = ya_ref[rows, :].astype(f32), yb_ref[rows, :].astype(f32)
        rows_ref[k : k + 1, :] = jnp.where(lower_first, b, a)[0:1].astype(jnp.int32)
        rows_ref[3 + k : 4 + k, :] = meta_ref[PACK * k : PACK * (k + 1), :].astype(f32)[0:1].astype(jnp.int32)
        rows_ref[6 + k : 7 + k, :] = jnp.where(lower_first, a, b)[0:1].astype(jnp.int32)
    copy = pltpu.make_async_copy(rows_ref, table_ref, sem)
    copy.start()
    for t in range(tiles + 4):
        light[t] = jnp.zeros_like(light[t])
    for h in range(2):
        cols = slice(LANES * h, LANES * (h + 1))
        real, imag = probe_ref[0, :, cols], probe_ref[1, :, cols]
        power[h] = real * real + imag * imag
    copy.wait()

    def tile_slots(n, carry):
        down = n // 3 - 1
        across = n - (down + 1) * 3 - 1

        def one(slot, inner):
            row = table_ref[n, 2 * slot] * 16 + table_ref[n, step + 2 * slot] - LANES + down * tile_r
            col = table_ref[n, 2 * slot + 1] * 16 + table_ref[n, step + 2 * slot + 1] - LANES + across * tile_c
            meets = (row > -win) & (row < tile_r) & (col > -win) & (col < tile_c)

            @pl.when(meets)
            def _():
                place = col + win
                tile = place // LANES
                shift = place - tile * LANES
                low = lax.broadcasted_iota(jnp.int32, (64, LANES), 1) < shift
                for i in range(0, win, 64):
                    one_half = pltpu.roll(power[0, i : i + 64, :], shift, 1)
                    two_half = pltpu.roll(power[1, i : i + 64, :], shift, 1)
                    at = pl.ds(row + win + i, 64)
                    light[tile, at, :] += jnp.where(low, 0.0, one_half)
                    light[tile + 1, at, :] += jnp.where(low, one_half, two_half)
                    light[tile + 2, at, :] += jnp.where(low, two_half, 0.0)

            return inner

        for batch in range(batches):
            carry = lax.fori_loop(slots * batch, slots * batch + table_ref[n, 2 * step + batch], one, carry)
        return carry

    lax.fori_loop(0, 9, tile_slots, 0)
    for t in range(tiles):
        scale_ref[t] = step_scale / (light[t + 2, win : win + tile_r, :] + 1.0)


def strips_kernel(canvas_ref, ya_ref, yb_ref, sa_ref, sb_ref):
    tiles = canvas_ref.shape[1] - 2
    margin = LANES
    tile_r = canvas_ref.shape[2] - 2 * margin
    lower_first = even("row")
    right_first = even("col")
    for c in range(2):
        for r in range(0, tile_r, margin):
            sides = []
            for t in (0, tiles + 1):
                value = canvas_ref[c, t, margin + r : 2 * margin + r, :]
                k = (c * (tiles + 2) + t) * margin
                a, b = ya_ref[k : k + margin, :].astype(f32), yb_ref[k : k + margin, :].astype(f32)
                if r == 0:
                    value += jnp.where(lower_first, b, a)
                if r == tile_r - margin:
                    value += jnp.where(lower_first, a, b)
                sides.append(value)
            rows = slice(c * tile_r + r, c * tile_r + r + margin)
            sa_ref[rows, :] = jnp.where(right_first, sides[1], sides[0]).astype(bf16)
            sb_ref[rows, :] = jnp.where(right_first, sides[0], sides[1]).astype(bf16)


def update_kernel(outer, *refs):
    if outer:
        obj_ref, canvas_ref, ya_ref, yb_ref, scale_ref, sa_ref, sb_ref, _, _, grad_hbm, out_hbm, grad, out, sem = refs
    else:
        obj_ref, canvas_ref, ya_ref, yb_ref, scale_ref, grad_hbm, out_hbm, grad, out, sem = refs
    tiles = canvas_ref.shape[1] - 2
    margin = LANES
    tile_r = canvas_ref.shape[2] - 2 * margin
    part = 256
    lower_first = even("row")
    right_first = even("col")
    copies = []
    for r in range(0, tile_r, part):
        for k, t in enumerate((0, tiles - 1) if outer else range(1, tiles - 1)):
            cols = slice(LANES * t, LANES * (t + 1))
            rows = slice(r, r + part)
            for c in range(2):
                value = canvas_ref[c, t + 1, margin + r : margin + r + part, :]
                if outer:
                    at = slice(c * tile_r + r, c * tile_r + r + part)
                    a, b = sa_ref[at, :].astype(f32), sb_ref[at, :].astype(f32)
                    value += jnp.where(right_first, b, a) if t == 0 else jnp.where(right_first, a, b)
                at = (c * (tiles + 2) + t + 1) * margin
                if r == 0 or r + part == tile_r:
                    a = ya_ref[at : at + margin, :].astype(f32)
                    b = yb_ref[at : at + margin, :].astype(f32)
                    if r == 0:
                        top = value[:margin] + jnp.where(lower_first, b, a)
                        value = jnp.concatenate([top, value[margin:]], 0)
                    else:
                        bottom = value[part - margin :] + jnp.where(lower_first, a, b)
                        value = jnp.concatenate([value[: part - margin], bottom], 0)
                grad[c, k, rows, :] = value
                out[c, k, rows, :] = obj_ref[c, rows, cols] - scale_ref[t, rows, :] * value
            for n, (source, target) in enumerate(((grad, grad_hbm), (out, out_hbm))):
                copy = pltpu.make_async_copy(
                    source.at[:, k, pl.ds(r, part), :],
                    target.at[:, pl.ds(r, part), pl.ds(LANES * t, LANES)],
                    sem.at[n, k, r // part],
                )
                copy.start()
                copies.append(copy)
    for copy in copies:
        copy.wait()


def on_device(object_field, probe, amplitudes, positions, counts):
    tile_r, tile_c = object_field.shape[1:]
    window = probe.shape[1]
    margin = window // 2
    batches, slots = amplitudes.shape[2:4]
    tiles = tile_c // LANES
    padded = (2, tiles + 2, tile_r + 2 * margin, LANES)
    base = dft_parts(window)
    places = jnp.swapaxes(positions, 3, 4)
    shape = jax.ShapeDtypeStruct
    side = shape((2 * tile_r + PACK, LANES), bf16)
    strip = shape((2 * (tiles + 2) * margin, LANES), bf16)

    za, zb, own = pl.pallas_call(
        edges_kernel,
        out_shape=(side, side, shape((PACK, LANES), bf16)),
        in_specs=[SMEM, SMEM, ANY],
        out_specs=(VMEM,) * 3,
        scratch_shapes=[pltpu.VMEM((2 * tile_r, LANES), f32)] * 2 + [pltpu.SemaphoreType.DMA((2, 2 * tile_r // 256))],
        name="edges",
    )(places, counts, object_field)
    za, zb = swap(za, "col", 0), swap(zb, "col", 1)
    block = shape((2 * window, 2 * window), bf16)
    row_halo = shape((2 * tiles * margin, LANES), bf16)
    obj, canvas, pa, pb, fwd, bwd, ext = pl.pallas_call(
        prepare_kernel,
        out_shape=(
            shape(padded, f32), shape(padded, f32), row_halo, row_halo,
            block, block, shape((2, 2, 2 * window, LANES), f32),
        ),
        in_specs=[ANY, VMEM],
        out_specs=(VMEM,) * 7,
        scratch_shapes=[pltpu.SemaphoreType.DMA((2, tiles))],
        compiler_params=pltpu.CompilerParams(vmem_limit_bytes=4 << 20),
        cost_estimate=pl.CostEstimate(flops=4 << 20, bytes_accessed=16 << 20, transcendentals=0),
        name="prepare",
    )(object_field, base)
    pb, pa = swap(pb, "row", 1), swap(pa, "row", 0)
    amps = amplitudes.reshape(batches * slots, window, window)
    tail = (probe, amps, fwd, bwd, ext)

    long_strip = shape((strip.shape[0] + margin, LANES), bf16)

    def run(kind, obj, canvas, *halo):
        edge = bool(halo)
        big = shape(padded, f32)
        return pl.pallas_call(
            functools.partial(slots_kernel, kind),
            out_shape=(big, big, long_strip if kind == "far" else strip) if edge else big,
            in_specs=[SMEM, SMEM] + [VMEM] * (7 + len(halo)),
            out_specs=(VMEM,) * 3 if edge else VMEM,
            input_output_aliases={2: 0, 3: 1} if edge else {3: 0},
            scratch_shapes=[
                pltpu.SMEM((batches * slots,), jnp.int32),
                pltpu.VMEM((GROUP, 2, 2, window, LANES), f32),
                pltpu.VMEM((2 * window, GROUP * window), bf16),
                pltpu.VMEM((GROUP, window, 2 * window), bf16),
                pltpu.VMEM((GROUP, 2 * window, 2 * window), bf16),
            ],
            compiler_params=pltpu.CompilerParams(vmem_limit_bytes=14 << 20),
            cost_estimate=pl.CostEstimate(flops=2 << 30, bytes_accessed=8 << 20, transcendentals=0),
            name=kind,
        )(places, counts, obj, canvas, *halo, *tail)

    canvas = run("core", obj, canvas)
    obj, canvas, za, zb = lax.optimization_barrier((obj, canvas, za, zb))
    packed = shape((4 * margin + 3 * PACK, LANES), bf16)
    obj, ca, cb, meta = pl.pallas_call(
        sides_kernel,
        out_shape=(shape(padded, f32), packed, packed, shape((3 * PACK, LANES), bf16)),
        in_specs=[VMEM] * 4,
        out_specs=(VMEM,) * 4,
        input_output_aliases={0: 0},
        compiler_params=pltpu.CompilerParams(vmem_limit_bytes=4 << 20),
        name="sides",
    )(obj, za, zb, own)
    cb, ca = swap(cb, "row", 1), swap(ca, "row", 0)
    canvas = run("inner", obj, canvas)
    obj, canvas, rb = run("far", obj, canvas, pb, cb)
    rb = swap(rb, "row", 1)
    obj, canvas, ra = run("near", obj, canvas, pa, ca)
    ra = swap(ra, "row", 0)
    rim = shape((2 * tile_r, LANES), bf16)
    sa, sb = pl.pallas_call(
        strips_kernel,
        out_shape=(rim, rim),
        in_specs=[VMEM] * 3,
        out_specs=(VMEM, VMEM),
        compiler_params=pltpu.CompilerParams(vmem_limit_bytes=4 << 20),
        name="strips",
    )(canvas, ra, rb)
    sa, sb, probe = lax.optimization_barrier((sa, sb, probe))
    sa, sb = swap(sa, "col", 0), swap(sb, "col", 1)
    scale = pl.pallas_call(
        light_kernel,
        out_shape=shape((tiles, tile_r, LANES), f32),
        in_specs=[VMEM] * 4,
        out_specs=VMEM,
        scratch_shapes=[
            pltpu.VMEM((2, window, LANES), f32),
            pltpu.VMEM((tiles + 4, tile_r + 2 * window, LANES), f32),
            pltpu.VMEM((PACK, LANES), jnp.int32),
            pltpu.SMEM((PACK, LANES), jnp.int32),
            pltpu.SemaphoreType.DMA,
        ],
        compiler_params=pltpu.CompilerParams(vmem_limit_bytes=9 << 20),
        cost_estimate=pl.CostEstimate(flops=8 << 20, bytes_accessed=12 << 20, transcendentals=0),
        name="light",
    )(meta, ca, cb, probe)
    field = shape((2, tile_r, tile_c), f32)

    def update(outer, aliases, *args):
        return pl.pallas_call(
            functools.partial(update_kernel, outer),
            out_shape=(field, field),
            in_specs=[VMEM] * (7 if outer else 5) + [ANY] * len(aliases),
            out_specs=(ANY, ANY),
            input_output_aliases=aliases,
            scratch_shapes=[pltpu.VMEM((2, 2, tile_r, LANES), f32)] * 2
            + [pltpu.SemaphoreType.DMA((2, 2, tile_r // 256))],
            compiler_params=pltpu.CompilerParams(vmem_limit_bytes=8 << 20),
            cost_estimate=pl.CostEstimate(flops=4 << 20, bytes_accessed=10 << 20, transcendentals=0),
            name="rims" if outer else "middle",
        )(*args)

    grad, out = update(False, {}, object_field, canvas, ra, rb, scale)
    return update(True, {7: 0, 8: 1}, object_field, canvas, ra, rb, scale, sa, sb, grad, out)


def solution(mesh):
    in_specs = (
        P(None, "row", "col"),
        P(),
        P("row", "col", None, None, None, None),
        P("row", "col", None, None, None),
        P("row", "col", None),
    )
    out_specs = (P(None, "row", "col"), P(None, "row", "col"))
    return jax.shard_map(
        on_device, mesh=mesh, in_specs=in_specs, out_specs=out_specs, check_vma=False
    )
```

```python
import functools
import math

import jax
import jax.numpy as jnp
import ml_dtypes
import numpy as np
from jax import lax
from jax.experimental import pallas as pl
from jax.experimental.pallas import tpu as pltpu
from jax.sharding import PartitionSpec as P

step_scale = 0.5
LANES = 128
PACK = 16
CHUNK = 32
GROUP = 2
f32 = jnp.float32
bf16 = jnp.bfloat16
VMEM = pl.BlockSpec(memory_space=pltpu.VMEM)
SMEM = pl.BlockSpec(memory_space=pltpu.SMEM)
ANY = pl.BlockSpec(memory_space=pl.ANY)


def swap(block, axis, parity):
    size = lax.axis_size(axis)
    route = []
    for i in range(parity, size - 1, 2):
        route += [(i, i + 1), (i + 1, i)]
    return lax.ppermute(block, axis, route)


def even(axis):
    return lax.rem(lax.axis_index(axis), 2) == 0


def dft_parts(window):
    counter = np.arange(window)
    angles = 2.0 * math.pi / window * (counter[:, None] * counter[None, :] % window)
    scale_value = 1.0 / math.sqrt(window)
    parts = np.stack([np.cos(angles), -np.sin(angles)]) * scale_value
    return parts.astype(np.float32).astype(ml_dtypes.bfloat16)


def meta_rows(pos_ref, counts_ref):
    batches, slots = pos_ref.shape[2], pos_ref.shape[4]
    lane = lax.broadcasted_iota(jnp.int32, (PACK, LANES), 1)
    row = jnp.zeros((PACK, LANES), jnp.int32)
    fields = 2 * batches * slots
    for k in range(fields):
        value = pos_ref[0, 0, k // (2 * slots), k % 2, k // 2 % slots] + LANES
        row = jnp.where(lane == k, value // 16, row)
        row = jnp.where(lane == fields + k, lax.rem(value, 16), row)
    for k in range(batches):
        row = jnp.where(lane == 2 * fields + k, counts_ref[0, 0, k], row)
    return row.astype(f32).astype(bf16)


def edges_kernel(pos_ref, counts_ref, obj_hbm, first_ref, second_ref, low, high, sem):
    tile_r, tile_c = obj_hbm.shape[1:]
    part = 256
    copies = []
    for k in range(2 * tile_r // part):
        c, r = divmod(k * part, tile_r)
        for side, (start, target) in enumerate(((0, low), (tile_c - LANES, high))):
            source = obj_hbm.at[c, pl.ds(r, part), pl.ds(start, LANES)]
            copies.append(pltpu.make_async_copy(source, target.at[pl.ds(k * part, part), :], sem.at[side, k]))
    for copy in copies:
        copy.start()
    upward = even("col")
    meta = meta_rows(pos_ref, counts_ref)
    first_ref[2 * tile_r :, :] = meta
    second_ref[2 * tile_r :, :] = meta
    for k in range(2 * tile_r // part):
        copies[2 * k].wait()
        copies[2 * k + 1].wait()
        rows = slice(k * part, (k + 1) * part)
        a, b = low[rows, :], high[rows, :]
        first_ref[rows, :] = jnp.where(upward, b, a).astype(bf16)
        second_ref[rows, :] = jnp.where(upward, a, b).astype(bf16)


def prepare_kernel(
    pos_ref, counts_ref, obj_hbm, base_ref, obj_ref, canvas_ref, pa_ref, pb_ref, fwd_ref, bwd_ref, ext_ref, meta_ref, sem
):
    tile_r, tile_c = obj_hbm.shape[1:]
    margin = (obj_ref.shape[2] - tile_r) // 2
    tiles = tile_c // LANES
    win = base_ref.shape[1]
    body = pl.ds(margin, tile_r)
    copies = [
        pltpu.make_async_copy(
            obj_hbm.at[c, :, pl.ds(LANES * t, LANES)], obj_ref.at[c, t + 1, body, :], sem.at[c, t]
        )
        for c in range(2)
        for t in range(tiles)
    ]
    for copy in copies:
        copy.start()
    downward = even("row")
    for k, copy in enumerate(copies):
        copy.wait()
        c, t = divmod(k, tiles)
        obj_ref[c, t + 1, body, :] = obj_ref[c, t + 1, body, :].astype(bf16).astype(f32)
        top = obj_ref[c, t + 1, margin : 2 * margin, :]
        bottom = obj_ref[c, t + 1, tile_r : tile_r + margin, :]
        rows = slice(k * margin, (k + 1) * margin)
        pa_ref[rows, :] = jnp.where(downward, bottom, top).astype(bf16)
        pb_ref[rows, :] = jnp.where(downward, top, bottom).astype(bf16)
    canvas_ref[...] = jnp.zeros_like(canvas_ref)
    meta_ref[...] = meta_rows(pos_ref, counts_ref)
    real, imag = base_ref[0], base_ref[1]
    fwd_ref[:win, :win] = real
    fwd_ref[:win, win:] = -imag
    fwd_ref[win:, :win] = imag
    fwd_ref[win:, win:] = real
    bwd_ref[:win, :win] = real
    bwd_ref[:win, win:] = imag
    bwd_ref[win:, :win] = -imag
    bwd_ref[win:, win:] = real
    for n in range(2):
        for h in range(2):
            half = base_ref[n, :, LANES * h : LANES * (h + 1)].astype(f32)
            ext_ref[n, h, :win, :] = half
            ext_ref[n, h, win:, :] = half


def sides_kernel(obj_in, za_ref, zb_ref, own_ref, obj_ref, ca_ref, cb_ref, meta_ref):
    tiles = obj_ref.shape[1] - 2
    margin = LANES
    tile_r = obj_ref.shape[2] - 2 * margin
    right_first = even("col")
    downward = even("row")
    for c in range(2):
        for r in range(0, tile_r, 128):
            rows = slice(c * tile_r + r, c * tile_r + r + 128)
            a = za_ref[rows, :].astype(f32)
            b = zb_ref[rows, :].astype(f32)
            at = slice(margin + r, margin + r + 128)
            obj_ref[c, 0, at, :] = jnp.where(right_first, b, a)
            obj_ref[c, tiles + 1, at, :] = jnp.where(right_first, a, b)
        for h, t in enumerate((0, tiles + 1)):
            top = obj_ref[c, t, margin : 2 * margin, :]
            bottom = obj_ref[c, t, tile_r : tile_r + margin, :]
            k = (2 * c + h) * margin
            ca_ref[k : k + margin, :] = jnp.where(downward, bottom, top).astype(bf16)
            cb_ref[k : k + margin, :] = jnp.where(downward, top, bottom).astype(bf16)
    tail = 4 * margin
    a = za_ref[2 * tile_r :, :].astype(f32)
    b = zb_ref[2 * tile_r :, :].astype(f32)
    metas = (jnp.where(right_first, b, a).astype(bf16), own_ref[...], jnp.where(right_first, a, b).astype(bf16))
    for k, meta in enumerate(metas):
        rows = slice(tail + PACK * k, tail + PACK * (k + 1))
        ca_ref[rows, :] = meta
        cb_ref[rows, :] = meta
        meta_ref[PACK * k : PACK * (k + 1), :] = meta


def slots_kernel(kind, *refs):
    if kind in ("far", "near"):
        (pos_ref, counts_ref, obj_in, canvas_in, halo_ref, corner_ref, probe_ref, amp_ref, fwd_ref, bwd_ref, ext_ref,
         obj, canvas_ref, rim_ref, todo, prb, xs, hs, er) = refs
    else:
        (pos_ref, counts_ref, obj, canvas_in, probe_ref, amp_ref, fwd_ref, bwd_ref, ext_ref,
         canvas_ref, todo, prb, xs, hs, er) = refs
    batches, slots = pos_ref.shape[2], pos_ref.shape[4]
    win = probe_ref.shape[1]
    margin = win // 2
    tiles = obj.shape[1] - 2
    tile_r = obj.shape[2] - 2 * margin
    tile_c = tiles * LANES
    upper = even("row") == (kind == "far")
    place = pl.multiple_of(jnp.where(upper, 0, margin + tile_r), margin)
    if kind in ("far", "near"):
        for c in range(2):
            for t in range(tiles):
                k = (c * tiles + t) * margin
                obj[c, t + 1, pl.ds(place, margin), :] = halo_ref[k : k + margin, :].astype(f32)
            for h, t in enumerate((0, tiles + 1)):
                k = (2 * c + h) * margin
                obj[c, t, pl.ds(place, margin), :] = corner_ref[k : k + margin, :].astype(f32)

    def member(row, col):
        inside = (row >= 0) & (row <= tile_r - win)
        between = (col >= 0) & (col <= tile_c - win)
        if kind == "core":
            return inside & between
        if kind == "inner":
            return inside & jnp.logical_not(between)
        return jnp.logical_not(inside) & ((row < 0) == upper)

    def collect(slot, count):
        batch = slot // slots
        row = pos_ref[0, 0, batch, 0, slot - batch * slots]
        col = pos_ref[0, 0, batch, 1, slot - batch * slots]
        live = (slot - batch * slots < counts_ref[0, 0, batch]) & member(row, col)

        @pl.when(live)
        def _():
            todo[count] = slot

        return count + live.astype(jnp.int32)

    total = lax.fori_loop(0, batches * slots, collect, jnp.int32(0))
    lane = lax.broadcasted_iota(jnp.int32, (CHUNK, LANES), 1)

    def group(first, width):
        chosen = []
        for g in range(width):
            slot = todo[first + g]
            batch = slot // slots
            row = pos_ref[0, 0, batch, 0, slot - batch * slots] + margin
            col = pos_ref[0, 0, batch, 1, slot - batch * slots] + margin
            tile = col // LANES
            shift = col - tile * LANES
            chosen.append((slot, row, tile, jnp.minimum(tile + 2, tiles + 1), shift))

        def exit_waves(g):
            slot, row, tile, wrapped, shift = chosen[g]
            low = lane < shift
            for i in range(0, win, CHUNK):
                turned = []
                window = []
                for c in range(2):
                    one = pltpu.roll(probe_ref[c, i : i + CHUNK, 0:LANES], shift, 1)
                    two = pltpu.roll(probe_ref[c, i : i + CHUNK, LANES:], shift, 1)
                    turned.append((jnp.where(low, two, one), jnp.where(low, one, two)))
                    at = pl.ds(row + i, CHUNK)
                    window.append(
                        (jnp.where(low, obj[c, wrapped, at, :], obj[c, tile, at, :]), obj[c, tile + 1, at, :])
                    )
                for h in range(2):
                    pr, pi = turned[0][h], turned[1][h]
                    wr, wi = window[0][h], window[1][h]
                    prb[g, 0, h, i : i + CHUNK, :] = pr
                    prb[g, 1, h, i : i + CHUNK, :] = pi
                    cols = slice(win * g + LANES * h, win * g + LANES * (h + 1))
                    xs[i : i + CHUNK, cols] = (pr * wr - pi * wi).astype(bf16)
                    xs[win + i : win + i + CHUNK, cols] = (pr * wi + pi * wr).astype(bf16)

        def rolled_table(g):
            shift = chosen[g][4]
            for i in range(0, win, CHUNK):
                for h in range(2):
                    real = ext_ref[0, h, pl.ds(win - shift + i, CHUNK), :].astype(bf16)
                    imag = ext_ref[1, h, pl.ds(win - shift + i, CHUNK), :].astype(bf16)
                    a = slice(LANES * h, LANES * (h + 1))
                    b = slice(win + LANES * h, win + LANES * (h + 1))
                    er[g, i : i + CHUNK, a] = real
                    er[g, i : i + CHUNK, b] = imag
                    er[g, win + i : win + i + CHUNK, a] = -imag
                    er[g, win + i : win + i + CHUNK, b] = real

        def rows_dft(table_ref):
            for g in range(width):
                for part in range(2):
                    out = jnp.dot(
                        table_ref[win * part : win * (part + 1), :],
                        xs[:, win * g : win * (g + 1)],
                        preferred_element_type=f32,
                    )
                    hs[g, :, win * part : win * (part + 1)] = out.astype(bf16)

        def residual_waves(g):
            far = jnp.dot(hs[g], er[g], preferred_element_type=f32)
            real, imag = far[:, :win], far[:, win:]
            scale = 1.0 - amp_ref[chosen[g][0]].astype(f32) * lax.rsqrt(real * real + imag * imag + 1.0)
            xs[:win, win * g : win * (g + 1)] = (real * scale).astype(bf16)
            xs[win:, win * g : win * (g + 1)] = (imag * scale).astype(bf16)

        def accumulate(g):
            slot, row, tile, wrapped, shift = chosen[g]
            back = lax.dot_general(hs[g], er[g], (((1,), (1,)), ((), ())), preferred_element_type=f32)
            keep = lax.broadcasted_iota(jnp.int32, (win, LANES), 1) < shift
            at = pl.ds(row, win)
            for h in range(2):
                pr, pi = prb[g, 0, h], prb[g, 1, h]
                br = back[:, LANES * h : LANES * (h + 1)]
                bi = back[:, win + LANES * h : win + LANES * (h + 1)]
                terms = [pr * br + pi * bi, pr * bi - pi * br]
                for c in range(2):
                    if h == 0:
                        canvas_ref[c, tile, at, :] += jnp.where(keep, 0.0, terms[c])
                        canvas_ref[c, wrapped, at, :] += jnp.where(keep, terms[c], 0.0)
                    else:
                        canvas_ref[c, tile + 1, at, :] += terms[c]

        for g in range(width):
            exit_waves(g)
        rows_dft(fwd_ref)
        for g in range(width):
            rolled_table(g)
        for g in range(width):
            residual_waves(g)
        rows_dft(bwd_ref)
        for g in range(width):
            accumulate(g)

    def full_group(p, carry):
        group(p * GROUP, GROUP)
        return carry

    lax.fori_loop(0, total // GROUP, full_group, 0)

    @pl.when(lax.rem(total, GROUP) == 1)
    def _():
        group(total - 1, 1)

    if kind in ("far", "near"):
        for c in range(2):
            for t in range(tiles + 2):
                k = (c * (tiles + 2) + t) * margin
                rim_ref[k : k + margin, :] = canvas_ref[c, t, pl.ds(place, margin), :].astype(bf16)
        spare = 2 * (tiles + 2) * margin
        if rim_ref.shape[0] > spare:
            rim_ref[spare:, :] = jnp.zeros((rim_ref.shape[0] - spare, LANES), bf16)


def light_kernel(meta_ref, ya_ref, yb_ref, probe_ref, scale_ref, power, light, rows_ref, table_ref, sem):
    win = probe_ref.shape[1]
    tiles, tile_r = scale_ref.shape[:2]
    tile_c = tiles * LANES
    batches = 3
    slots = 4
    step = 2 * batches * slots
    lower_first = even("row")
    tail = ya_ref.shape[0] - 3 * PACK
    for k in range(3):
        rows = slice(tail + PACK * k, tail + PACK * (k + 1))
        a, b = ya_ref[rows, :].astype(f32), yb_ref[rows, :].astype(f32)
        rows_ref[k : k + 1, :] = jnp.where(lower_first, b, a)[0:1].astype(jnp.int32)
        rows_ref[3 + k : 4 + k, :] = meta_ref[PACK * k : PACK * (k + 1), :].astype(f32)[0:1].astype(jnp.int32)
        rows_ref[6 + k : 7 + k, :] = jnp.where(lower_first, a, b)[0:1].astype(jnp.int32)
    copy = pltpu.make_async_copy(rows_ref, table_ref, sem)
    copy.start()
    for t in range(tiles + 4):
        light[t] = jnp.zeros_like(light[t])
    for h in range(2):
        cols = slice(LANES * h, LANES * (h + 1))
        real, imag = probe_ref[0, :, cols], probe_ref[1, :, cols]
        power[h] = real * real + imag * imag
    copy.wait()

    def tile_slots(n, carry):
        down = n // 3 - 1
        across = n - (down + 1) * 3 - 1

        def one(slot, inner):
            row = table_ref[n, 2 * slot] * 16 + table_ref[n, step + 2 * slot] - LANES + down * tile_r
            col = table_ref[n, 2 * slot + 1] * 16 + table_ref[n, step + 2 * slot + 1] - LANES + across * tile_c
            meets = (row > -win) & (row < tile_r) & (col > -win) & (col < tile_c)

            @pl.when(meets)
            def _():
                place = col + win
                tile = place // LANES
                shift = place - tile * LANES
                low = lax.broadcasted_iota(jnp.int32, (64, LANES), 1) < shift
                for i in range(0, win, 64):
                    one_half = pltpu.roll(power[0, i : i + 64, :], shift, 1)
                    two_half = pltpu.roll(power[1, i : i + 64, :], shift, 1)
                    at = pl.ds(row + win + i, 64)
                    light[tile, at, :] += jnp.where(low, 0.0, one_half)
                    light[tile + 1, at, :] += jnp.where(low, one_half, two_half)
                    light[tile + 2, at, :] += jnp.where(low, two_half, 0.0)

            return inner

        for batch in range(batches):
            carry = lax.fori_loop(slots * batch, slots * batch + table_ref[n, 2 * step + batch], one, carry)
        return carry

    lax.fori_loop(0, 9, tile_slots, 0)
    for t in range(tiles):
        scale_ref[t] = step_scale / (light[t + 2, win : win + tile_r, :] + 1.0)


def strips_kernel(canvas_ref, ya_ref, yb_ref, sa_ref, sb_ref):
    tiles = canvas_ref.shape[1] - 2
    margin = LANES
    tile_r = canvas_ref.shape[2] - 2 * margin
    lower_first = even("row")
    right_first = even("col")
    for c in range(2):
        for r in range(0, tile_r, margin):
            sides = []
            for t in (0, tiles + 1):
                value = canvas_ref[c, t, margin + r : 2 * margin + r, :]
                k = (c * (tiles + 2) + t) * margin
                a, b = ya_ref[k : k + margin, :].astype(f32), yb_ref[k : k + margin, :].astype(f32)
                if r == 0:
                    value += jnp.where(lower_first, b, a)
                if r == tile_r - margin:
                    value += jnp.where(lower_first, a, b)
                sides.append(value)
            rows = slice(c * tile_r + r, c * tile_r + r + margin)
            sa_ref[rows, :] = jnp.where(right_first, sides[1], sides[0]).astype(bf16)
            sb_ref[rows, :] = jnp.where(right_first, sides[0], sides[1]).astype(bf16)


def update_kernel(parity, *refs):
    outer = parity is not None
    if outer:
        obj_ref, canvas_ref, ya_ref, yb_ref, scale_ref, side_ref, _, _, grad_hbm, out_hbm, grad, out, sem = refs
    else:
        obj_ref, canvas_ref, ya_ref, yb_ref, scale_ref, grad_hbm, out_hbm, grad, out, sem = refs
    tiles = canvas_ref.shape[1] - 2
    margin = LANES
    tile_r = canvas_ref.shape[2] - 2 * margin
    part = 256
    lower_first = even("row")
    rightmost = jnp.where(even("col") == (parity == 0), tiles - 1, 0)
    copies = []
    for r in range(0, tile_r, part):
        for k, t in enumerate((rightmost,) if outer else range(1, tiles - 1)):
            cols = pl.ds(pl.multiple_of(LANES * t, LANES), LANES) if outer else pl.ds(LANES * t, LANES)
            rows = slice(r, r + part)
            for c in range(2):
                value = canvas_ref[c, t + 1, margin + r : margin + r + part, :]
                if outer:
                    value += side_ref[c * tile_r + r : c * tile_r + r + part, :].astype(f32)
                if r == 0 or r + part == tile_r:
                    at = (c * (tiles + 2) + t + 1) * margin
                    strip = pl.ds(pl.multiple_of(at, margin), margin) if outer else pl.ds(at, margin)
                    a = ya_ref[strip, :].astype(f32)
                    b = yb_ref[strip, :].astype(f32)
                    if r == 0:
                        top = value[:margin] + jnp.where(lower_first, b, a)
                        value = jnp.concatenate([top, value[margin:]], 0)
                    else:
                        bottom = value[part - margin :] + jnp.where(lower_first, a, b)
                        value = jnp.concatenate([value[: part - margin], bottom], 0)
                grad[c, k, rows, :] = value
                out[c, k, rows, :] = obj_ref[c, rows, cols] - scale_ref[t, rows, :] * value
            for n, (source, target) in enumerate(((grad, grad_hbm), (out, out_hbm))):
                copy = pltpu.make_async_copy(
                    source.at[:, k, pl.ds(r, part), :],
                    target.at[:, pl.ds(r, part), cols],
                    sem.at[n, k, r // part],
                )
                copy.start()
                copies.append(copy)
    for copy in copies:
        copy.wait()


def on_device(object_field, probe, amplitudes, positions, counts):
    tile_r, tile_c = object_field.shape[1:]
    window = probe.shape[1]
    margin = window // 2
    batches, slots = amplitudes.shape[2:4]
    tiles = tile_c // LANES
    padded = (2, tiles + 2, tile_r + 2 * margin, LANES)
    base = dft_parts(window)
    places = jnp.swapaxes(positions, 3, 4)
    shape = jax.ShapeDtypeStruct
    side = shape((2 * tile_r + PACK, LANES), bf16)
    strip = shape((2 * (tiles + 2) * margin, LANES), bf16)

    za, zb = pl.pallas_call(
        edges_kernel,
        out_shape=(side, side),
        in_specs=[SMEM, SMEM, ANY],
        out_specs=(VMEM, VMEM),
        scratch_shapes=[pltpu.VMEM((2 * tile_r, LANES), f32)] * 2 + [pltpu.SemaphoreType.DMA((2, 2 * tile_r // 256))],
        name="edges",
    )(places, counts, object_field)
    za, zb = swap(za, "col", 0), swap(zb, "col", 1)
    block = shape((2 * window, 2 * window), bf16)
    row_halo = shape((2 * tiles * margin, LANES), bf16)
    obj, canvas, pa, pb, fwd, bwd, ext, own = pl.pallas_call(
        prepare_kernel,
        out_shape=(
            shape(padded, f32), shape(padded, f32), row_halo, row_halo,
            block, block, shape((2, 2, 2 * window, LANES), f32), shape((PACK, LANES), bf16),
        ),
        in_specs=[SMEM, SMEM, ANY, VMEM],
        out_specs=(VMEM,) * 8,
        scratch_shapes=[pltpu.SemaphoreType.DMA((2, tiles))],
        compiler_params=pltpu.CompilerParams(vmem_limit_bytes=4 << 20),
        cost_estimate=pl.CostEstimate(flops=4 << 20, bytes_accessed=16 << 20, transcendentals=0),
        name="prepare",
    )(places, counts, object_field, base)
    pb, pa = swap(pb, "row", 1), swap(pa, "row", 0)
    amps = amplitudes.reshape(batches * slots, window, window)
    tail = (probe, amps, fwd, bwd, ext)

    long_strip = shape((strip.shape[0] + margin, LANES), bf16)

    def run(kind, obj, canvas, *halo):
        edge = bool(halo)
        big = shape(padded, f32)
        return pl.pallas_call(
            functools.partial(slots_kernel, kind),
            out_shape=(big, big, long_strip if kind == "far" else strip) if edge else big,
            in_specs=[SMEM, SMEM] + [VMEM] * (7 + len(halo)),
            out_specs=(VMEM,) * 3 if edge else VMEM,
            input_output_aliases={2: 0, 3: 1} if edge else {3: 0},
            scratch_shapes=[
                pltpu.SMEM((batches * slots,), jnp.int32),
                pltpu.VMEM((GROUP, 2, 2, window, LANES), f32),
                pltpu.VMEM((2 * window, GROUP * window), bf16),
                pltpu.VMEM((GROUP, window, 2 * window), bf16),
                pltpu.VMEM((GROUP, 2 * window, 2 * window), bf16),
            ],
            compiler_params=pltpu.CompilerParams(vmem_limit_bytes=14 << 20),
            cost_estimate=pl.CostEstimate(flops=2 << 30, bytes_accessed=8 << 20, transcendentals=0),
            name=kind,
        )(places, counts, obj, canvas, *halo, *tail)

    packed = shape((4 * margin + 3 * PACK, LANES), bf16)
    obj, ca, cb, meta = pl.pallas_call(
        sides_kernel,
        out_shape=(shape(padded, f32), packed, packed, shape((3 * PACK, LANES), bf16)),
        in_specs=[VMEM] * 4,
        out_specs=(VMEM,) * 4,
        input_output_aliases={0: 0},
        compiler_params=pltpu.CompilerParams(vmem_limit_bytes=4 << 20),
        name="sides",
    )(obj, za, zb, own)
    cb, ca = swap(cb, "row", 1), swap(ca, "row", 0)
    canvas = run("inner", obj, canvas)
    obj, canvas, rb = run("far", obj, canvas, pb, cb)
    rb = swap(rb, "row", 1)
    obj, canvas, ra = run("near", obj, canvas, pa, ca)
    ra = swap(ra, "row", 0)
    canvas = run("core", obj, canvas)
    rim = shape((2 * tile_r, LANES), bf16)
    sa, sb = pl.pallas_call(
        strips_kernel,
        out_shape=(rim, rim),
        in_specs=[VMEM] * 3,
        out_specs=(VMEM, VMEM),
        compiler_params=pltpu.CompilerParams(vmem_limit_bytes=4 << 20),
        name="strips",
    )(canvas, ra, rb)
    sa, sb, probe = lax.optimization_barrier((sa, sb, probe))
    sa, sb = swap(sa, "col", 0), swap(sb, "col", 1)
    scale = pl.pallas_call(
        light_kernel,
        out_shape=shape((tiles, tile_r, LANES), f32),
        in_specs=[VMEM] * 4,
        out_specs=VMEM,
        scratch_shapes=[
            pltpu.VMEM((2, window, LANES), f32),
            pltpu.VMEM((tiles + 4, tile_r + 2 * window, LANES), f32),
            pltpu.VMEM((PACK, LANES), jnp.int32),
            pltpu.SMEM((PACK, LANES), jnp.int32),
            pltpu.SemaphoreType.DMA,
        ],
        compiler_params=pltpu.CompilerParams(vmem_limit_bytes=9 << 20),
        cost_estimate=pl.CostEstimate(flops=8 << 20, bytes_accessed=12 << 20, transcendentals=0),
        name="light",
    )(meta, ca, cb, probe)
    field = shape((2, tile_r, tile_c), f32)

    def update(parity, aliases, *args):
        width = 2 if parity is None else 1
        return pl.pallas_call(
            functools.partial(update_kernel, parity),
            out_shape=(field, field),
            in_specs=[VMEM] * (len(args) - len(aliases)) + [ANY] * len(aliases),
            out_specs=(ANY, ANY),
            input_output_aliases=aliases,
            scratch_shapes=[pltpu.VMEM((2, width, tile_r, LANES), f32)] * 2
            + [pltpu.SemaphoreType.DMA((2, width, tile_r // 256))],
            compiler_params=pltpu.CompilerParams(vmem_limit_bytes=8 << 20),
            cost_estimate=pl.CostEstimate(flops=4 << 20, bytes_accessed=10 << 20, transcendentals=0),
            name="middle" if parity is None else "rim",
        )(*args)

    grad, out = update(None, {}, object_field, canvas, ra, rb, scale)
    grad, out = update(0, {6: 0, 7: 1}, object_field, canvas, ra, rb, scale, sa, grad, out)
    return update(1, {6: 0, 7: 1}, object_field, canvas, ra, rb, scale, sb, grad, out)


def solution(mesh):
    in_specs = (
        P(None, "row", "col"),
        P(),
        P("row", "col", None, None, None, None),
        P("row", "col", None, None, None),
        P("row", "col", None),
    )
    out_specs = (P(None, "row", "col"), P(None, "row", "col"))
    return jax.shard_map(
        on_device, mesh=mesh, in_specs=in_specs, out_specs=out_specs, check_vma=False
    )
```

```python
import functools
import math

import jax
import jax.numpy as jnp
import ml_dtypes
import numpy as np
from jax import lax
from jax.experimental import pallas as pl
from jax.experimental.pallas import tpu as pltpu
from jax.sharding import PartitionSpec as P

step_scale = 0.5
LANES = 128
PACK = 16
CHUNK = 32
GROUP = 2
f32 = jnp.float32
bf16 = jnp.bfloat16
VMEM = pl.BlockSpec(memory_space=pltpu.VMEM)
SMEM = pl.BlockSpec(memory_space=pltpu.SMEM)
ANY = pl.BlockSpec(memory_space=pl.ANY)


def swap(block, axis, parity):
    size = lax.axis_size(axis)
    route = []
    for i in range(parity, size - 1, 2):
        route += [(i, i + 1), (i + 1, i)]
    return lax.ppermute(block, axis, route)


def even(axis):
    return lax.rem(lax.axis_index(axis), 2) == 0


def dft_parts(window):
    counter = np.arange(window)
    angles = 2.0 * math.pi / window * (counter[:, None] * counter[None, :] % window)
    scale_value = 1.0 / math.sqrt(window)
    parts = np.stack([np.cos(angles), -np.sin(angles)]) * scale_value
    return parts.astype(np.float32).astype(ml_dtypes.bfloat16)


def meta_rows(pos_ref, counts_ref):
    batches, slots = pos_ref.shape[2], pos_ref.shape[4]
    lane = lax.broadcasted_iota(jnp.int32, (PACK, LANES), 1)
    row = jnp.zeros((PACK, LANES), jnp.int32)
    fields = 2 * batches * slots
    for k in range(fields):
        value = pos_ref[0, 0, k // (2 * slots), k % 2, k // 2 % slots] + LANES
        row = jnp.where(lane == k, value // 16, row)
        row = jnp.where(lane == fields + k, lax.rem(value, 16), row)
    for k in range(batches):
        row = jnp.where(lane == 2 * fields + k, counts_ref[0, 0, k], row)
    return row.astype(f32).astype(bf16)


def edges_kernel(pos_ref, counts_ref, obj_hbm, first_ref, second_ref, low, high, sem):
    tile_r, tile_c = obj_hbm.shape[1:]
    part = 256
    copies = []
    for k in range(2 * tile_r // part):
        c, r = divmod(k * part, tile_r)
        for side, (start, target) in enumerate(((0, low), (tile_c - LANES, high))):
            source = obj_hbm.at[c, pl.ds(r, part), pl.ds(start, LANES)]
            copies.append(pltpu.make_async_copy(source, target.at[pl.ds(k * part, part), :], sem.at[side, k]))
    for copy in copies:
        copy.start()
    upward = even("col")
    meta = meta_rows(pos_ref, counts_ref)
    first_ref[2 * tile_r :, :] = meta
    second_ref[2 * tile_r :, :] = meta
    for k in range(2 * tile_r // part):
        copies[2 * k].wait()
        copies[2 * k + 1].wait()
        rows = slice(k * part, (k + 1) * part)
        a, b = low[rows, :], high[rows, :]
        first_ref[rows, :] = jnp.where(upward, b, a).astype(bf16)
        second_ref[rows, :] = jnp.where(upward, a, b).astype(bf16)


def prepare_kernel(obj_hbm, obj_ref, pa_ref, pb_ref, sem):
    tile_r, tile_c = obj_hbm.shape[1:]
    margin = (obj_ref.shape[2] - tile_r) // 2
    tiles = tile_c // LANES
    body = pl.ds(margin, tile_r)
    copies = [
        pltpu.make_async_copy(
            obj_hbm.at[c, :, pl.ds(LANES * t, LANES)], obj_ref.at[c, t + 1, body, :], sem.at[c, t]
        )
        for c in range(2)
        for t in range(tiles)
    ]
    for copy in copies:
        copy.start()
    downward = even("row")
    for k, copy in enumerate(copies):
        copy.wait()
        c, t = divmod(k, tiles)
        obj_ref[c, t + 1, body, :] = obj_ref[c, t + 1, body, :].astype(bf16).astype(f32)
        top = obj_ref[c, t + 1, margin : 2 * margin, :]
        bottom = obj_ref[c, t + 1, tile_r : tile_r + margin, :]
        rows = slice(k * margin, (k + 1) * margin)
        pa_ref[rows, :] = jnp.where(downward, bottom, top).astype(bf16)
        pb_ref[rows, :] = jnp.where(downward, top, bottom).astype(bf16)


def tables_kernel(base_ref, canvas_ref, fwd_ref, bwd_ref, ext_ref):
    win = base_ref.shape[1]
    canvas_ref[...] = jnp.zeros_like(canvas_ref)
    real, imag = base_ref[0], base_ref[1]
    fwd_ref[:win, :win] = real
    fwd_ref[:win, win:] = -imag
    fwd_ref[win:, :win] = imag
    fwd_ref[win:, win:] = real
    bwd_ref[:win, :win] = real
    bwd_ref[:win, win:] = imag
    bwd_ref[win:, :win] = -imag
    bwd_ref[win:, win:] = real
    for n in range(2):
        for h in range(2):
            half = base_ref[n, :, LANES * h : LANES * (h + 1)].astype(f32)
            ext_ref[n, h, :win, :] = half
            ext_ref[n, h, win:, :] = half


def sides_kernel(pos_ref, counts_ref, obj_in, za_ref, zb_ref, obj_ref, ca_ref, cb_ref, meta_ref):
    tiles = obj_ref.shape[1] - 2
    margin = LANES
    tile_r = obj_ref.shape[2] - 2 * margin
    right_first = even("col")
    downward = even("row")
    for c in range(2):
        for r in range(0, tile_r, 128):
            rows = slice(c * tile_r + r, c * tile_r + r + 128)
            a = za_ref[rows, :].astype(f32)
            b = zb_ref[rows, :].astype(f32)
            at = slice(margin + r, margin + r + 128)
            obj_ref[c, 0, at, :] = jnp.where(right_first, b, a)
            obj_ref[c, tiles + 1, at, :] = jnp.where(right_first, a, b)
        for h, t in enumerate((0, tiles + 1)):
            top = obj_ref[c, t, margin : 2 * margin, :]
            bottom = obj_ref[c, t, tile_r : tile_r + margin, :]
            k = (2 * c + h) * margin
            ca_ref[k : k + margin, :] = jnp.where(downward, bottom, top).astype(bf16)
            cb_ref[k : k + margin, :] = jnp.where(downward, top, bottom).astype(bf16)
    tail = 4 * margin
    a = za_ref[2 * tile_r :, :].astype(f32)
    b = zb_ref[2 * tile_r :, :].astype(f32)
    own = meta_rows(pos_ref, counts_ref)
    metas = (jnp.where(right_first, b, a).astype(bf16), own, jnp.where(right_first, a, b).astype(bf16))
    for k, meta in enumerate(metas):
        rows = slice(tail + PACK * k, tail + PACK * (k + 1))
        ca_ref[rows, :] = meta
        cb_ref[rows, :] = meta
        meta_ref[PACK * k : PACK * (k + 1), :] = meta


def slots_kernel(kind, *refs):
    if kind in ("far", "near"):
        (pos_ref, counts_ref, obj_in, canvas_in, halo_ref, corner_ref, probe_ref, amp_ref, fwd_ref, bwd_ref, ext_ref,
         obj, canvas_ref, rim_ref, todo, prb, xs, hs, er) = refs
    else:
        (pos_ref, counts_ref, obj, canvas_in, probe_ref, amp_ref, fwd_ref, bwd_ref, ext_ref,
         canvas_ref, todo, prb, xs, hs, er) = refs
    batches, slots = pos_ref.shape[2], pos_ref.shape[4]
    win = probe_ref.shape[1]
    margin = win // 2
    tiles = obj.shape[1] - 2
    tile_r = obj.shape[2] - 2 * margin
    tile_c = tiles * LANES
    upper = even("row") == (kind == "far")
    place = pl.multiple_of(jnp.where(upper, 0, margin + tile_r), margin)
    if kind in ("far", "near"):
        for c in range(2):
            for t in range(tiles):
                k = (c * tiles + t) * margin
                obj[c, t + 1, pl.ds(place, margin), :] = halo_ref[k : k + margin, :].astype(f32)
            for h, t in enumerate((0, tiles + 1)):
                k = (2 * c + h) * margin
                obj[c, t, pl.ds(place, margin), :] = corner_ref[k : k + margin, :].astype(f32)

    def member(row, col):
        inside = (row >= 0) & (row <= tile_r - win)
        between = (col >= 0) & (col <= tile_c - win)
        if kind == "core":
            return inside & between
        if kind == "inner":
            return inside & jnp.logical_not(between)
        return jnp.logical_not(inside) & ((row < 0) == upper)

    def collect(slot, count):
        batch = slot // slots
        row = pos_ref[0, 0, batch, 0, slot - batch * slots]
        col = pos_ref[0, 0, batch, 1, slot - batch * slots]
        live = (slot - batch * slots < counts_ref[0, 0, batch]) & member(row, col)

        @pl.when(live)
        def _():
            todo[count] = slot

        return count + live.astype(jnp.int32)

    total = lax.fori_loop(0, batches * slots, collect, jnp.int32(0))
    lane = lax.broadcasted_iota(jnp.int32, (CHUNK, LANES), 1)

    def group(first, width):
        chosen = []
        for g in range(width):
            slot = todo[first + g]
            batch = slot // slots
            row = pos_ref[0, 0, batch, 0, slot - batch * slots] + margin
            col = pos_ref[0, 0, batch, 1, slot - batch * slots] + margin
            tile = col // LANES
            shift = col - tile * LANES
            chosen.append((slot, row, tile, jnp.minimum(tile + 2, tiles + 1), shift))

        def exit_waves(g):
            slot, row, tile, wrapped, shift = chosen[g]
            low = lane < shift
            for i in range(0, win, CHUNK):
                turned = []
                window = []
                for c in range(2):
                    one = pltpu.roll(probe_ref[c, i : i + CHUNK, 0:LANES], shift, 1)
                    two = pltpu.roll(probe_ref[c, i : i + CHUNK, LANES:], shift, 1)
                    turned.append((jnp.where(low, two, one), jnp.where(low, one, two)))
                    at = pl.ds(row + i, CHUNK)
                    window.append(
                        (jnp.where(low, obj[c, wrapped, at, :], obj[c, tile, at, :]), obj[c, tile + 1, at, :])
                    )
                for h in range(2):
                    pr, pi = turned[0][h], turned[1][h]
                    wr, wi = window[0][h], window[1][h]
                    prb[g, 0, h, i : i + CHUNK, :] = pr
                    prb[g, 1, h, i : i + CHUNK, :] = pi
                    cols = slice(win * g + LANES * h, win * g + LANES * (h + 1))
                    xs[i : i + CHUNK, cols] = (pr * wr - pi * wi).astype(bf16)
                    xs[win + i : win + i + CHUNK, cols] = (pr * wi + pi * wr).astype(bf16)

        def rolled_table(g):
            shift = chosen[g][4]
            for i in range(0, win, CHUNK):
                for h in range(2):
                    real = ext_ref[0, h, pl.ds(win - shift + i, CHUNK), :].astype(bf16)
                    imag = ext_ref[1, h, pl.ds(win - shift + i, CHUNK), :].astype(bf16)
                    a = slice(LANES * h, LANES * (h + 1))
                    b = slice(win + LANES * h, win + LANES * (h + 1))
                    er[g, i : i + CHUNK, a] = real
                    er[g, i : i + CHUNK, b] = imag
                    er[g, win + i : win + i + CHUNK, a] = -imag
                    er[g, win + i : win + i + CHUNK, b] = real

        def rows_dft(table_ref):
            for g in range(width):
                for part in range(2):
                    out = jnp.dot(
                        table_ref[win * part : win * (part + 1), :],
                        xs[:, win * g : win * (g + 1)],
                        preferred_element_type=f32,
                    )
                    hs[g, :, win * part : win * (part + 1)] = out.astype(bf16)

        def residual_waves(g):
            far = jnp.dot(hs[g], er[g], preferred_element_type=f32)
            real, imag = far[:, :win], far[:, win:]
            scale = 1.0 - amp_ref[chosen[g][0]].astype(f32) * lax.rsqrt(real * real + imag * imag + 1.0)
            xs[:win, win * g : win * (g + 1)] = (real * scale).astype(bf16)
            xs[win:, win * g : win * (g + 1)] = (imag * scale).astype(bf16)

        def accumulate(g):
            slot, row, tile, wrapped, shift = chosen[g]
            back = lax.dot_general(hs[g], er[g], (((1,), (1,)), ((), ())), preferred_element_type=f32)
            keep = lax.broadcasted_iota(jnp.int32, (win, LANES), 1) < shift
            at = pl.ds(row, win)
            for h in range(2):
                pr, pi = prb[g, 0, h], prb[g, 1, h]
                br = back[:, LANES * h : LANES * (h + 1)]
                bi = back[:, win + LANES * h : win + LANES * (h + 1)]
                terms = [pr * br + pi * bi, pr * bi - pi * br]
                for c in range(2):
                    if h == 0:
                        canvas_ref[c, tile, at, :] += jnp.where(keep, 0.0, terms[c])
                        canvas_ref[c, wrapped, at, :] += jnp.where(keep, terms[c], 0.0)
                    else:
                        canvas_ref[c, tile + 1, at, :] += terms[c]

        for g in range(width):
            exit_waves(g)
        rows_dft(fwd_ref)
        for g in range(width):
            rolled_table(g)
        for g in range(width):
            residual_waves(g)
        rows_dft(bwd_ref)
        for g in range(width):
            accumulate(g)

    def full_group(p, carry):
        group(p * GROUP, GROUP)
        return carry

    lax.fori_loop(0, total // GROUP, full_group, 0)

    @pl.when(lax.rem(total, GROUP) == 1)
    def _():
        group(total - 1, 1)

    if kind in ("far", "near"):
        for c in range(2):
            for t in range(tiles + 2):
                k = (c * (tiles + 2) + t) * margin
                rim_ref[k : k + margin, :] = canvas_ref[c, t, pl.ds(place, margin), :].astype(bf16)
        spare = 2 * (tiles + 2) * margin
        if rim_ref.shape[0] > spare:
            rim_ref[spare:, :] = jnp.zeros((rim_ref.shape[0] - spare, LANES), bf16)


def light_kernel(meta_ref, ya_ref, yb_ref, probe_ref, scale_ref, power, light, rows_ref, table_ref, sem):
    win = probe_ref.shape[1]
    tiles, tile_r = scale_ref.shape[:2]
    tile_c = tiles * LANES
    batches = 3
    slots = 4
    step = 2 * batches * slots
    lower_first = even("row")
    tail = ya_ref.shape[0] - 3 * PACK
    for k in range(3):
        rows = slice(tail + PACK * k, tail + PACK * (k + 1))
        a, b = ya_ref[rows, :].astype(f32), yb_ref[rows, :].astype(f32)
        rows_ref[k : k + 1, :] = jnp.where(lower_first, b, a)[0:1].astype(jnp.int32)
        rows_ref[3 + k : 4 + k, :] = meta_ref[PACK * k : PACK * (k + 1), :].astype(f32)[0:1].astype(jnp.int32)
        rows_ref[6 + k : 7 + k, :] = jnp.where(lower_first, a, b)[0:1].astype(jnp.int32)
    copy = pltpu.make_async_copy(rows_ref, table_ref, sem)
    copy.start()
    for t in range(tiles + 4):
        light[t] = jnp.zeros_like(light[t])
    for h in range(2):
        cols = slice(LANES * h, LANES * (h + 1))
        real, imag = probe_ref[0, :, cols], probe_ref[1, :, cols]
        power[h] = real * real + imag * imag
    copy.wait()

    def tile_slots(n, carry):
        down = n // 3 - 1
        across = n - (down + 1) * 3 - 1

        def one(slot, inner):
            row = table_ref[n, 2 * slot] * 16 + table_ref[n, step + 2 * slot] - LANES + down * tile_r
            col = table_ref[n, 2 * slot + 1] * 16 + table_ref[n, step + 2 * slot + 1] - LANES + across * tile_c
            meets = (row > -win) & (row < tile_r) & (col > -win) & (col < tile_c)

            @pl.when(meets)
            def _():
                place = col + win
                tile = place // LANES
                shift = place - tile * LANES
                low = lax.broadcasted_iota(jnp.int32, (64, LANES), 1) < shift
                for i in range(0, win, 64):
                    one_half = pltpu.roll(power[0, i : i + 64, :], shift, 1)
                    two_half = pltpu.roll(power[1, i : i + 64, :], shift, 1)
                    at = pl.ds(row + win + i, 64)
                    light[tile, at, :] += jnp.where(low, 0.0, one_half)
                    light[tile + 1, at, :] += jnp.where(low, one_half, two_half)
                    light[tile + 2, at, :] += jnp.where(low, two_half, 0.0)

            return inner

        for batch in range(batches):
            carry = lax.fori_loop(slots * batch, slots * batch + table_ref[n, 2 * step + batch], one, carry)
        return carry

    lax.fori_loop(0, 9, tile_slots, 0)
    for t in range(tiles):
        scale_ref[t] = step_scale / (light[t + 2, win : win + tile_r, :] + 1.0)


def strips_kernel(canvas_ref, ya_ref, yb_ref, sa_ref, sb_ref):
    tiles = canvas_ref.shape[1] - 2
    margin = LANES
    tile_r = canvas_ref.shape[2] - 2 * margin
    lower_first = even("row")
    right_first = even("col")
    for c in range(2):
        for r in range(0, tile_r, margin):
            sides = []
            for t in (0, tiles + 1):
                value = canvas_ref[c, t, margin + r : 2 * margin + r, :]
                k = (c * (tiles + 2) + t) * margin
                a, b = ya_ref[k : k + margin, :].astype(f32), yb_ref[k : k + margin, :].astype(f32)
                if r == 0:
                    value += jnp.where(lower_first, b, a)
                if r == tile_r - margin:
                    value += jnp.where(lower_first, a, b)
                sides.append(value)
            rows = slice(c * tile_r + r, c * tile_r + r + margin)
            sa_ref[rows, :] = jnp.where(right_first, sides[1], sides[0]).astype(bf16)
            sb_ref[rows, :] = jnp.where(right_first, sides[0], sides[1]).astype(bf16)


def update_kernel(parity, *refs):
    outer = parity is not None
    if outer:
        obj_ref, canvas_ref, ya_ref, yb_ref, scale_ref, side_ref, _, _, grad_hbm, out_hbm, grad, out, sem = refs
    else:
        obj_ref, canvas_ref, ya_ref, yb_ref, scale_ref, grad_hbm, out_hbm, grad, out, sem = refs
    tiles = canvas_ref.shape[1] - 2
    margin = LANES
    tile_r = canvas_ref.shape[2] - 2 * margin
    part = 256
    lower_first = even("row")
    rightmost = jnp.where(even("col") == (parity == 0), tiles - 1, 0)
    copies = []
    for r in range(0, tile_r, part):
        for k, t in enumerate((rightmost,) if outer else range(1, tiles - 1)):
            cols = pl.ds(pl.multiple_of(LANES * t, LANES), LANES) if outer else pl.ds(LANES * t, LANES)
            rows = slice(r, r + part)
            for c in range(2):
                value = canvas_ref[c, t + 1, margin + r : margin + r + part, :]
                if outer:
                    value += side_ref[c * tile_r + r : c * tile_r + r + part, :].astype(f32)
                if r == 0 or r + part == tile_r:
                    at = (c * (tiles + 2) + t + 1) * margin
                    strip = pl.ds(pl.multiple_of(at, margin), margin) if outer else pl.ds(at, margin)
                    a = ya_ref[strip, :].astype(f32)
                    b = yb_ref[strip, :].astype(f32)
                    if r == 0:
                        top = value[:margin] + jnp.where(lower_first, b, a)
                        value = jnp.concatenate([top, value[margin:]], 0)
                    else:
                        bottom = value[part - margin :] + jnp.where(lower_first, a, b)
                        value = jnp.concatenate([value[: part - margin], bottom], 0)
                grad[c, k, rows, :] = value
                out[c, k, rows, :] = obj_ref[c, rows, cols] - scale_ref[t, rows, :] * value
            for n, (source, target) in enumerate(((grad, grad_hbm), (out, out_hbm))):
                copy = pltpu.make_async_copy(
                    source.at[:, k, pl.ds(r, part), :],
                    target.at[:, pl.ds(r, part), cols],
                    sem.at[n, k, r // part],
                )
                copy.start()
                copies.append(copy)
    for copy in copies:
        copy.wait()


def on_device(object_field, probe, amplitudes, positions, counts):
    tile_r, tile_c = object_field.shape[1:]
    window = probe.shape[1]
    margin = window // 2
    batches, slots = amplitudes.shape[2:4]
    tiles = tile_c // LANES
    padded = (2, tiles + 2, tile_r + 2 * margin, LANES)
    base = dft_parts(window)
    places = jnp.swapaxes(positions, 3, 4)
    shape = jax.ShapeDtypeStruct
    side = shape((2 * tile_r + PACK, LANES), bf16)
    strip = shape((2 * (tiles + 2) * margin, LANES), bf16)

    za, zb = pl.pallas_call(
        edges_kernel,
        out_shape=(side, side),
        in_specs=[SMEM, SMEM, ANY],
        out_specs=(VMEM, VMEM),
        scratch_shapes=[pltpu.VMEM((2 * tile_r, LANES), f32)] * 2 + [pltpu.SemaphoreType.DMA((2, 2 * tile_r // 256))],
        name="edges",
    )(places, counts, object_field)
    za, zb = swap(za, "col", 0), swap(zb, "col", 1)
    block = shape((2 * window, 2 * window), bf16)
    row_halo = shape((2 * tiles * margin, LANES), bf16)
    obj, pa, pb = pl.pallas_call(
        prepare_kernel,
        out_shape=(shape(padded, f32), row_halo, row_halo),
        in_specs=[ANY],
        out_specs=(VMEM,) * 3,
        scratch_shapes=[pltpu.SemaphoreType.DMA((2, tiles))],
        compiler_params=pltpu.CompilerParams(vmem_limit_bytes=4 << 20),
        cost_estimate=pl.CostEstimate(flops=4 << 20, bytes_accessed=16 << 20, transcendentals=0),
        name="prepare",
    )(object_field)
    pb, pa = swap(pb, "row", 1), swap(pa, "row", 0)
    obj, base = lax.optimization_barrier((obj, jnp.asarray(base)))
    canvas, fwd, bwd, ext = pl.pallas_call(
        tables_kernel,
        out_shape=(shape(padded, f32), block, block, shape((2, 2, 2 * window, LANES), f32)),
        in_specs=[VMEM],
        out_specs=(VMEM,) * 4,
        compiler_params=pltpu.CompilerParams(vmem_limit_bytes=4 << 20),
        cost_estimate=pl.CostEstimate(flops=4 << 20, bytes_accessed=8 << 20, transcendentals=0),
        name="tables",
    )(base)
    obj, canvas, fwd, bwd, ext = lax.optimization_barrier((obj, canvas, fwd, bwd, ext))
    amps = amplitudes.reshape(batches * slots, window, window)
    tail = (probe, amps, fwd, bwd, ext)

    long_strip = shape((strip.shape[0] + margin, LANES), bf16)

    def run(kind, obj, canvas, *halo):
        edge = bool(halo)
        big = shape(padded, f32)
        return pl.pallas_call(
            functools.partial(slots_kernel, kind),
            out_shape=(big, big, long_strip if kind == "far" else strip) if edge else big,
            in_specs=[SMEM, SMEM] + [VMEM] * (7 + len(halo)),
            out_specs=(VMEM,) * 3 if edge else VMEM,
            input_output_aliases={2: 0, 3: 1} if edge else {3: 0},
            scratch_shapes=[
                pltpu.SMEM((batches * slots,), jnp.int32),
                pltpu.VMEM((GROUP, 2, 2, window, LANES), f32),
                pltpu.VMEM((2 * window, GROUP * window), bf16),
                pltpu.VMEM((GROUP, window, 2 * window), bf16),
                pltpu.VMEM((GROUP, 2 * window, 2 * window), bf16),
            ],
            compiler_params=pltpu.CompilerParams(vmem_limit_bytes=14 << 20),
            cost_estimate=pl.CostEstimate(flops=2 << 30, bytes_accessed=8 << 20, transcendentals=0),
            name=kind,
        )(places, counts, obj, canvas, *halo, *tail)

    packed = shape((4 * margin + 3 * PACK, LANES), bf16)
    obj, ca, cb, meta = pl.pallas_call(
        sides_kernel,
        out_shape=(shape(padded, f32), packed, packed, shape((3 * PACK, LANES), bf16)),
        in_specs=[SMEM, SMEM] + [VMEM] * 3,
        out_specs=(VMEM,) * 4,
        input_output_aliases={2: 0},
        compiler_params=pltpu.CompilerParams(vmem_limit_bytes=4 << 20),
        name="sides",
    )(places, counts, obj, za, zb)
    cb, ca = swap(cb, "row", 1), swap(ca, "row", 0)
    canvas = run("inner", obj, canvas)
    obj, canvas, rb = run("far", obj, canvas, pb, cb)
    rb = swap(rb, "row", 1)
    obj, canvas, ra = run("near", obj, canvas, pa, ca)
    ra = swap(ra, "row", 0)
    canvas = run("core", obj, canvas)
    rim = shape((2 * tile_r, LANES), bf16)
    sa, sb = pl.pallas_call(
        strips_kernel,
        out_shape=(rim, rim),
        in_specs=[VMEM] * 3,
        out_specs=(VMEM, VMEM),
        compiler_params=pltpu.CompilerParams(vmem_limit_bytes=4 << 20),
        name="strips",
    )(canvas, ra, rb)
    sa, sb, probe = lax.optimization_barrier((sa, sb, probe))
    sa, sb = swap(sa, "col", 0), swap(sb, "col", 1)
    scale = pl.pallas_call(
        light_kernel,
        out_shape=shape((tiles, tile_r, LANES), f32),
        in_specs=[VMEM] * 4,
        out_specs=VMEM,
        scratch_shapes=[
            pltpu.VMEM((2, window, LANES), f32),
            pltpu.VMEM((tiles + 4, tile_r + 2 * window, LANES), f32),
            pltpu.VMEM((PACK, LANES), jnp.int32),
            pltpu.SMEM((PACK, LANES), jnp.int32),
            pltpu.SemaphoreType.DMA,
        ],
        compiler_params=pltpu.CompilerParams(vmem_limit_bytes=9 << 20),
        cost_estimate=pl.CostEstimate(flops=8 << 20, bytes_accessed=12 << 20, transcendentals=0),
        name="light",
    )(meta, ca, cb, probe)
    field = shape((2, tile_r, tile_c), f32)

    def update(parity, aliases, *args):
        width = 2 if parity is None else 1
        return pl.pallas_call(
            functools.partial(update_kernel, parity),
            out_shape=(field, field),
            in_specs=[VMEM] * (len(args) - len(aliases)) + [ANY] * len(aliases),
            out_specs=(ANY, ANY),
            input_output_aliases=aliases,
            scratch_shapes=[pltpu.VMEM((2, width, tile_r, LANES), f32)] * 2
            + [pltpu.SemaphoreType.DMA((2, width, tile_r // 256))],
            compiler_params=pltpu.CompilerParams(vmem_limit_bytes=8 << 20),
            cost_estimate=pl.CostEstimate(flops=4 << 20, bytes_accessed=10 << 20, transcendentals=0),
            name="middle" if parity is None else "rim",
        )(*args)

    grad, out = update(None, {}, object_field, canvas, ra, rb, scale)
    grad, out = update(0, {6: 0, 7: 1}, object_field, canvas, ra, rb, scale, sa, grad, out)
    return update(1, {6: 0, 7: 1}, object_field, canvas, ra, rb, scale, sb, grad, out)


def solution(mesh):
    in_specs = (
        P(None, "row", "col"),
        P(),
        P("row", "col", None, None, None, None),
        P("row", "col", None, None, None),
        P("row", "col", None),
    )
    out_specs = (P(None, "row", "col"), P(None, "row", "col"))
    return jax.shard_map(
        on_device, mesh=mesh, in_specs=in_specs, out_specs=out_specs, check_vma=False
    )
```

```python
import functools
import math

import jax
import jax.numpy as jnp
import ml_dtypes
import numpy as np
from jax import lax
from jax.experimental import pallas as pl
from jax.experimental.pallas import tpu as pltpu
from jax.sharding import PartitionSpec as P

step_scale = 0.5
LANES = 128
PACK = 16
CHUNK = 32
GROUP = 2
f32 = jnp.float32
bf16 = jnp.bfloat16
VMEM = pl.BlockSpec(memory_space=pltpu.VMEM)
SMEM = pl.BlockSpec(memory_space=pltpu.SMEM)
ANY = pl.BlockSpec(memory_space=pl.ANY)


def swap(block, axis, parity):
    size = lax.axis_size(axis)
    route = []
    for i in range(parity, size - 1, 2):
        route += [(i, i + 1), (i + 1, i)]
    return lax.ppermute(block, axis, route)


def even(axis):
    return lax.rem(lax.axis_index(axis), 2) == 0


def dft_parts(window):
    counter = np.arange(window)
    angles = 2.0 * math.pi / window * (counter[:, None] * counter[None, :] % window)
    scale_value = 1.0 / math.sqrt(window)
    parts = np.stack([np.cos(angles), -np.sin(angles)]) * scale_value
    return parts.astype(np.float32).astype(ml_dtypes.bfloat16)


def meta_rows(pos_ref, counts_ref):
    batches, slots = pos_ref.shape[2], pos_ref.shape[4]
    lane = lax.broadcasted_iota(jnp.int32, (PACK, LANES), 1)
    row = jnp.zeros((PACK, LANES), jnp.int32)
    fields = 2 * batches * slots
    for k in range(fields):
        value = pos_ref[0, 0, k // (2 * slots), k % 2, k // 2 % slots] + LANES
        row = jnp.where(lane == k, value // 16, row)
        row = jnp.where(lane == fields + k, lax.rem(value, 16), row)
    for k in range(batches):
        row = jnp.where(lane == 2 * fields + k, counts_ref[0, 0, k], row)
    return row.astype(f32).astype(bf16)


def edges_kernel(pos_ref, counts_ref, obj_hbm, first_ref, second_ref, low, high, sem):
    tile_r, tile_c = obj_hbm.shape[1:]
    part = 256
    copies = []
    for k in range(2 * tile_r // part):
        c, r = divmod(k * part, tile_r)
        for side, (start, target) in enumerate(((0, low), (tile_c - LANES, high))):
            source = obj_hbm.at[c, pl.ds(r, part), pl.ds(start, LANES)]
            copies.append(pltpu.make_async_copy(source, target.at[pl.ds(k * part, part), :], sem.at[side, k]))
    for copy in copies:
        copy.start()
    upward = even("col")
    meta = meta_rows(pos_ref, counts_ref)
    first_ref[2 * tile_r :, :] = meta
    second_ref[2 * tile_r :, :] = meta
    for k in range(2 * tile_r // part):
        copies[2 * k].wait()
        copies[2 * k + 1].wait()
        rows = slice(k * part, (k + 1) * part)
        a, b = low[rows, :], high[rows, :]
        first_ref[rows, :] = jnp.where(upward, b, a).astype(bf16)
        second_ref[rows, :] = jnp.where(upward, a, b).astype(bf16)


def prepare_kernel(obj_hbm, obj_ref, pa_ref, pb_ref, sem):
    tile_r, tile_c = obj_hbm.shape[1:]
    margin = (obj_ref.shape[2] - tile_r) // 2
    tiles = tile_c // LANES
    body = pl.ds(margin, tile_r)
    copies = [
        pltpu.make_async_copy(
            obj_hbm.at[c, :, pl.ds(LANES * t, LANES)], obj_ref.at[c, t + 1, body, :], sem.at[c, t]
        )
        for c in range(2)
        for t in range(tiles)
    ]
    for copy in copies:
        copy.start()
    downward = even("row")
    for k, copy in enumerate(copies):
        copy.wait()
        c, t = divmod(k, tiles)
        obj_ref[c, t + 1, body, :] = obj_ref[c, t + 1, body, :].astype(bf16).astype(f32)
        top = obj_ref[c, t + 1, margin : 2 * margin, :]
        bottom = obj_ref[c, t + 1, tile_r : tile_r + margin, :]
        rows = slice(k * margin, (k + 1) * margin)
        pa_ref[rows, :] = jnp.where(downward, bottom, top).astype(bf16)
        pb_ref[rows, :] = jnp.where(downward, top, bottom).astype(bf16)


def tables_kernel(base_ref, canvas_ref, fwd_ref, bwd_ref, ext_ref):
    win = base_ref.shape[1]
    canvas_ref[...] = jnp.zeros_like(canvas_ref)
    real, imag = base_ref[0], base_ref[1]
    fwd_ref[:win, :win] = real
    fwd_ref[:win, win:] = -imag
    fwd_ref[win:, :win] = imag
    fwd_ref[win:, win:] = real
    bwd_ref[:win, :win] = real
    bwd_ref[:win, win:] = imag
    bwd_ref[win:, :win] = -imag
    bwd_ref[win:, win:] = real
    for n in range(2):
        for h in range(2):
            half = base_ref[n, :, LANES * h : LANES * (h + 1)].astype(f32)
            ext_ref[n, h, :win, :] = half
            ext_ref[n, h, win:, :] = half


def sides_kernel(pos_ref, counts_ref, obj_in, za_ref, zb_ref, obj_ref, ca_ref, cb_ref, meta_ref):
    tiles = obj_ref.shape[1] - 2
    margin = LANES
    tile_r = obj_ref.shape[2] - 2 * margin
    right_first = even("col")
    downward = even("row")
    for c in range(2):
        for r in range(0, tile_r, 128):
            rows = slice(c * tile_r + r, c * tile_r + r + 128)
            a = za_ref[rows, :].astype(f32)
            b = zb_ref[rows, :].astype(f32)
            at = slice(margin + r, margin + r + 128)
            obj_ref[c, 0, at, :] = jnp.where(right_first, b, a)
            obj_ref[c, tiles + 1, at, :] = jnp.where(right_first, a, b)
        for h, t in enumerate((0, tiles + 1)):
            top = obj_ref[c, t, margin : 2 * margin, :]
            bottom = obj_ref[c, t, tile_r : tile_r + margin, :]
            k = (2 * c + h) * margin
            ca_ref[k : k + margin, :] = jnp.where(downward, bottom, top).astype(bf16)
            cb_ref[k : k + margin, :] = jnp.where(downward, top, bottom).astype(bf16)
    tail = 4 * margin
    a = za_ref[2 * tile_r :, :].astype(f32)
    b = zb_ref[2 * tile_r :, :].astype(f32)
    own = meta_rows(pos_ref, counts_ref)
    metas = (jnp.where(right_first, b, a).astype(bf16), own, jnp.where(right_first, a, b).astype(bf16))
    for k, meta in enumerate(metas):
        rows = slice(tail + PACK * k, tail + PACK * (k + 1))
        ca_ref[rows, :] = meta
        cb_ref[rows, :] = meta
        meta_ref[PACK * k : PACK * (k + 1), :] = meta


def slots_kernel(kind, *refs):
    if kind in ("far", "near"):
        (pos_ref, counts_ref, obj_in, canvas_in, halo_ref, corner_ref, probe_ref, amp_ref, fwd_ref, bwd_ref, ext_ref,
         obj, canvas_ref, rim_ref, todo, prb, xs, hs, er) = refs
    else:
        (pos_ref, counts_ref, obj, canvas_in, probe_ref, amp_ref, fwd_ref, bwd_ref, ext_ref,
         canvas_ref, todo, prb, xs, hs, er) = refs
    batches, slots = pos_ref.shape[2], pos_ref.shape[4]
    win = probe_ref.shape[1]
    margin = win // 2
    tiles = obj.shape[1] - 2
    tile_r = obj.shape[2] - 2 * margin
    tile_c = tiles * LANES
    upper = even("row") == (kind == "far")
    place = pl.multiple_of(jnp.where(upper, 0, margin + tile_r), margin)
    if kind in ("far", "near"):
        for c in range(2):
            for t in range(tiles):
                k = (c * tiles + t) * margin
                obj[c, t + 1, pl.ds(place, margin), :] = halo_ref[k : k + margin, :].astype(f32)
            for h, t in enumerate((0, tiles + 1)):
                k = (2 * c + h) * margin
                obj[c, t, pl.ds(place, margin), :] = corner_ref[k : k + margin, :].astype(f32)

    def member(row, col):
        inside = (row >= 0) & (row <= tile_r - win)
        between = (col >= 0) & (col <= tile_c - win)
        if kind == "core":
            return inside & between
        if kind == "inner":
            return inside & jnp.logical_not(between)
        return jnp.logical_not(inside) & ((row < 0) == upper)

    def collect(slot, count):
        batch = slot // slots
        row = pos_ref[0, 0, batch, 0, slot - batch * slots]
        col = pos_ref[0, 0, batch, 1, slot - batch * slots]
        live = (slot - batch * slots < counts_ref[0, 0, batch]) & member(row, col)

        @pl.when(live)
        def _():
            todo[count] = slot

        return count + live.astype(jnp.int32)

    total = lax.fori_loop(0, batches * slots, collect, jnp.int32(0))
    lane = lax.broadcasted_iota(jnp.int32, (CHUNK, LANES), 1)

    def group(first, width):
        chosen = []
        for g in range(width):
            slot = todo[first + g]
            batch = slot // slots
            row = pos_ref[0, 0, batch, 0, slot - batch * slots] + margin
            col = pos_ref[0, 0, batch, 1, slot - batch * slots] + margin
            tile = col // LANES
            shift = col - tile * LANES
            chosen.append((slot, row, tile, jnp.minimum(tile + 2, tiles + 1), shift))

        def exit_waves(g):
            slot, row, tile, wrapped, shift = chosen[g]
            low = lane < shift
            for i in range(0, win, CHUNK):
                turned = []
                window = []
                for c in range(2):
                    one = pltpu.roll(probe_ref[c, i : i + CHUNK, 0:LANES], shift, 1)
                    two = pltpu.roll(probe_ref[c, i : i + CHUNK, LANES:], shift, 1)
                    turned.append((jnp.where(low, two, one), jnp.where(low, one, two)))
                    at = pl.ds(row + i, CHUNK)
                    window.append(
                        (jnp.where(low, obj[c, wrapped, at, :], obj[c, tile, at, :]), obj[c, tile + 1, at, :])
                    )
                for h in range(2):
                    pr, pi = turned[0][h], turned[1][h]
                    wr, wi = window[0][h], window[1][h]
                    prb[g, 0, h, i : i + CHUNK, :] = pr
                    prb[g, 1, h, i : i + CHUNK, :] = pi
                    cols = slice(win * g + LANES * h, win * g + LANES * (h + 1))
                    xs[i : i + CHUNK, cols] = (pr * wr - pi * wi).astype(bf16)
                    xs[win + i : win + i + CHUNK, cols] = (pr * wi + pi * wr).astype(bf16)

        def rolled_table(g):
            shift = chosen[g][4]
            for i in range(0, win, CHUNK):
                for h in range(2):
                    real = ext_ref[0, h, pl.ds(win - shift + i, CHUNK), :].astype(bf16)
                    imag = ext_ref[1, h, pl.ds(win - shift + i, CHUNK), :].astype(bf16)
                    a = slice(LANES * h, LANES * (h + 1))
                    b = slice(win + LANES * h, win + LANES * (h + 1))
                    er[g, i : i + CHUNK, a] = real
                    er[g, i : i + CHUNK, b] = imag
                    er[g, win + i : win + i + CHUNK, a] = -imag
                    er[g, win + i : win + i + CHUNK, b] = real

        def rows_dft(table_ref):
            for g in range(width):
                for part in range(2):
                    out = jnp.dot(
                        table_ref[win * part : win * (part + 1), :],
                        xs[:, win * g : win * (g + 1)],
                        preferred_element_type=f32,
                    )
                    hs[g, :, win * part : win * (part + 1)] = out.astype(bf16)

        def residual_waves(g):
            far = jnp.dot(hs[g], er[g], preferred_element_type=f32)
            real, imag = far[:, :win], far[:, win:]
            scale = 1.0 - amp_ref[chosen[g][0]].astype(f32) * lax.rsqrt(real * real + imag * imag + 1.0)
            xs[:win, win * g : win * (g + 1)] = (real * scale).astype(bf16)
            xs[win:, win * g : win * (g + 1)] = (imag * scale).astype(bf16)

        def accumulate(g):
            slot, row, tile, wrapped, shift = chosen[g]
            back = lax.dot_general(hs[g], er[g], (((1,), (1,)), ((), ())), preferred_element_type=f32)
            keep = lax.broadcasted_iota(jnp.int32, (win, LANES), 1) < shift
            at = pl.ds(row, win)
            for h in range(2):
                pr, pi = prb[g, 0, h], prb[g, 1, h]
                br = back[:, LANES * h : LANES * (h + 1)]
                bi = back[:, win + LANES * h : win + LANES * (h + 1)]
                terms = [pr * br + pi * bi, pr * bi - pi * br]
                for c in range(2):
                    if h == 0:
                        canvas_ref[c, tile, at, :] += jnp.where(keep, 0.0, terms[c])
                        canvas_ref[c, wrapped, at, :] += jnp.where(keep, terms[c], 0.0)
                    else:
                        canvas_ref[c, tile + 1, at, :] += terms[c]

        for g in range(width):
            exit_waves(g)
        rows_dft(fwd_ref)
        for g in range(width):
            rolled_table(g)
        for g in range(width):
            residual_waves(g)
        rows_dft(bwd_ref)
        for g in range(width):
            accumulate(g)

    def full_group(p, carry):
        group(p * GROUP, GROUP)
        return carry

    lax.fori_loop(0, total // GROUP, full_group, 0)

    @pl.when(lax.rem(total, GROUP) == 1)
    def _():
        group(total - 1, 1)

    if kind in ("far", "near"):
        for c in range(2):
            for t in range(tiles + 2):
                k = (c * (tiles + 2) + t) * margin
                rim_ref[k : k + margin, :] = canvas_ref[c, t, pl.ds(place, margin), :].astype(bf16)
        spare = 2 * (tiles + 2) * margin
        if rim_ref.shape[0] > spare:
            rim_ref[spare:, :] = jnp.zeros((rim_ref.shape[0] - spare, LANES), bf16)


def light_kernel(meta_ref, ya_ref, yb_ref, probe_ref, scale_ref, power, light, rows_ref, table_ref, sem):
    win = probe_ref.shape[1]
    tiles, tile_r = scale_ref.shape[:2]
    tile_c = tiles * LANES
    batches = 3
    slots = 4
    step = 2 * batches * slots
    lower_first = even("row")
    tail = ya_ref.shape[0] - 3 * PACK
    for k in range(3):
        rows = slice(tail + PACK * k, tail + PACK * (k + 1))
        a, b = ya_ref[rows, :].astype(f32), yb_ref[rows, :].astype(f32)
        rows_ref[k : k + 1, :] = jnp.where(lower_first, b, a)[0:1].astype(jnp.int32)
        rows_ref[3 + k : 4 + k, :] = meta_ref[PACK * k : PACK * (k + 1), :].astype(f32)[0:1].astype(jnp.int32)
        rows_ref[6 + k : 7 + k, :] = jnp.where(lower_first, a, b)[0:1].astype(jnp.int32)
    copy = pltpu.make_async_copy(rows_ref, table_ref, sem)
    copy.start()
    for t in range(tiles + 4):
        light[t] = jnp.zeros_like(light[t])
    for h in range(2):
        cols = slice(LANES * h, LANES * (h + 1))
        real, imag = probe_ref[0, :, cols], probe_ref[1, :, cols]
        power[h] = real * real + imag * imag
    copy.wait()

    def tile_slots(n, carry):
        down = n // 3 - 1
        across = n - (down + 1) * 3 - 1

        def one(slot, inner):
            row = table_ref[n, 2 * slot] * 16 + table_ref[n, step + 2 * slot] - LANES + down * tile_r
            col = table_ref[n, 2 * slot + 1] * 16 + table_ref[n, step + 2 * slot + 1] - LANES + across * tile_c
            meets = (row > -win) & (row < tile_r) & (col > -win) & (col < tile_c)

            @pl.when(meets)
            def _():
                place = col + win
                tile = place // LANES
                shift = place - tile * LANES
                low = lax.broadcasted_iota(jnp.int32, (64, LANES), 1) < shift
                for i in range(0, win, 64):
                    one_half = pltpu.roll(power[0, i : i + 64, :], shift, 1)
                    two_half = pltpu.roll(power[1, i : i + 64, :], shift, 1)
                    at = pl.ds(row + win + i, 64)
                    light[tile, at, :] += jnp.where(low, 0.0, one_half)
                    light[tile + 1, at, :] += jnp.where(low, one_half, two_half)
                    light[tile + 2, at, :] += jnp.where(low, two_half, 0.0)

            return inner

        for batch in range(batches):
            carry = lax.fori_loop(slots * batch, slots * batch + table_ref[n, 2 * step + batch], one, carry)
        return carry

    lax.fori_loop(0, 9, tile_slots, 0)
    for t in range(tiles):
        scale_ref[t] = step_scale / (light[t + 2, win : win + tile_r, :] + 1.0)


def strips_kernel(canvas_ref, ya_ref, yb_ref, sa_ref, sb_ref):
    tiles = canvas_ref.shape[1] - 2
    margin = LANES
    tile_r = canvas_ref.shape[2] - 2 * margin
    lower_first = even("row")
    right_first = even("col")
    for c in range(2):
        for r in range(0, tile_r, margin):
            sides = []
            for t in (0, tiles + 1):
                value = canvas_ref[c, t, margin + r : 2 * margin + r, :]
                k = (c * (tiles + 2) + t) * margin
                a, b = ya_ref[k : k + margin, :].astype(f32), yb_ref[k : k + margin, :].astype(f32)
                if r == 0:
                    value += jnp.where(lower_first, b, a)
                if r == tile_r - margin:
                    value += jnp.where(lower_first, a, b)
                sides.append(value)
            rows = slice(c * tile_r + r, c * tile_r + r + margin)
            sa_ref[rows, :] = jnp.where(right_first, sides[1], sides[0]).astype(bf16)
            sb_ref[rows, :] = jnp.where(right_first, sides[0], sides[1]).astype(bf16)


def update_kernel(parity, *refs):
    outer = parity is not None
    if outer:
        obj_ref, canvas_ref, ya_ref, yb_ref, scale_ref, side_ref, _, _, grad_hbm, out_hbm, grad, out, sem = refs
    else:
        obj_ref, canvas_ref, ya_ref, yb_ref, scale_ref, grad_hbm, out_hbm, grad, out, sem = refs
    tiles = canvas_ref.shape[1] - 2
    margin = LANES
    tile_r = canvas_ref.shape[2] - 2 * margin
    part = 256
    lower_first = even("row")
    rightmost = jnp.where(even("col") == (parity == 0), tiles - 1, 0)
    copies = []
    for r in range(0, tile_r, part):
        for k, t in enumerate((rightmost,) if outer else range(1, tiles - 1)):
            cols = pl.ds(pl.multiple_of(LANES * t, LANES), LANES) if outer else pl.ds(LANES * t, LANES)
            rows = slice(r, r + part)
            for c in range(2):
                value = canvas_ref[c, t + 1, margin + r : margin + r + part, :]
                if outer:
                    value += side_ref[c * tile_r + r : c * tile_r + r + part, :].astype(f32)
                if r == 0 or r + part == tile_r:
                    at = (c * (tiles + 2) + t + 1) * margin
                    strip = pl.ds(pl.multiple_of(at, margin), margin) if outer else pl.ds(at, margin)
                    a = ya_ref[strip, :].astype(f32)
                    b = yb_ref[strip, :].astype(f32)
                    if r == 0:
                        top = value[:margin] + jnp.where(lower_first, b, a)
                        value = jnp.concatenate([top, value[margin:]], 0)
                    else:
                        bottom = value[part - margin :] + jnp.where(lower_first, a, b)
                        value = jnp.concatenate([value[: part - margin], bottom], 0)
                grad[c, k, rows, :] = value
                out[c, k, rows, :] = obj_ref[c, rows, cols] - scale_ref[t, rows, :] * value
            for n, (source, target) in enumerate(((grad, grad_hbm), (out, out_hbm))):
                copy = pltpu.make_async_copy(
                    source.at[:, k, pl.ds(r, part), :],
                    target.at[:, pl.ds(r, part), cols],
                    sem.at[n, k, r // part],
                )
                copy.start()
                copies.append(copy)
    for copy in copies:
        copy.wait()


def on_device(object_field, probe, amplitudes, positions, counts):
    tile_r, tile_c = object_field.shape[1:]
    window = probe.shape[1]
    margin = window // 2
    batches, slots = amplitudes.shape[2:4]
    tiles = tile_c // LANES
    padded = (2, tiles + 2, tile_r + 2 * margin, LANES)
    base = dft_parts(window)
    places = jnp.swapaxes(positions, 3, 4)
    shape = jax.ShapeDtypeStruct
    side = shape((2 * tile_r + PACK, LANES), bf16)
    strip = shape((2 * (tiles + 2) * margin, LANES), bf16)

    za, zb = pl.pallas_call(
        edges_kernel,
        out_shape=(side, side),
        in_specs=[SMEM, SMEM, ANY],
        out_specs=(VMEM, VMEM),
        scratch_shapes=[pltpu.VMEM((2 * tile_r, LANES), f32)] * 2 + [pltpu.SemaphoreType.DMA((2, 2 * tile_r // 256))],
        name="edges",
    )(places, counts, object_field)
    za, zb = swap(za, "col", 0), swap(zb, "col", 1)
    block = shape((2 * window, 2 * window), bf16)
    row_halo = shape((2 * tiles * margin, LANES), bf16)
    obj, pa, pb = pl.pallas_call(
        prepare_kernel,
        out_shape=(shape(padded, f32), row_halo, row_halo),
        in_specs=[ANY],
        out_specs=(VMEM,) * 3,
        scratch_shapes=[pltpu.SemaphoreType.DMA((2, tiles))],
        compiler_params=pltpu.CompilerParams(vmem_limit_bytes=4 << 20),
        cost_estimate=pl.CostEstimate(flops=4 << 20, bytes_accessed=16 << 20, transcendentals=0),
        name="prepare",
    )(object_field)
    pb, pa = swap(pb, "row", 1), swap(pa, "row", 0)
    obj, base = lax.optimization_barrier((obj, jnp.asarray(base)))
    canvas, fwd, bwd, ext = pl.pallas_call(
        tables_kernel,
        out_shape=(shape(padded, f32), block, block, shape((2, 2, 2 * window, LANES), f32)),
        in_specs=[VMEM],
        out_specs=(VMEM,) * 4,
        compiler_params=pltpu.CompilerParams(vmem_limit_bytes=4 << 20),
        cost_estimate=pl.CostEstimate(flops=4 << 20, bytes_accessed=8 << 20, transcendentals=0),
        name="tables",
    )(base)
    amps = amplitudes.reshape(batches * slots, window, window)
    tail = (probe, amps, fwd, bwd, ext)

    long_strip = shape((strip.shape[0] + margin, LANES), bf16)

    def run(kind, obj, canvas, *halo):
        edge = bool(halo)
        big = shape(padded, f32)
        return pl.pallas_call(
            functools.partial(slots_kernel, kind),
            out_shape=(big, big, long_strip if kind == "far" else strip) if edge else big,
            in_specs=[SMEM, SMEM] + [VMEM] * (7 + len(halo)),
            out_specs=(VMEM,) * 3 if edge else VMEM,
            input_output_aliases={2: 0, 3: 1} if edge else {3: 0},
            scratch_shapes=[
                pltpu.SMEM((batches * slots,), jnp.int32),
                pltpu.VMEM((GROUP, 2, 2, window, LANES), f32),
                pltpu.VMEM((2 * window, GROUP * window), bf16),
                pltpu.VMEM((GROUP, window, 2 * window), bf16),
                pltpu.VMEM((GROUP, 2 * window, 2 * window), bf16),
            ],
            compiler_params=pltpu.CompilerParams(vmem_limit_bytes=14 << 20),
            cost_estimate=pl.CostEstimate(flops=2 << 30, bytes_accessed=8 << 20, transcendentals=0),
            name=kind,
        )(places, counts, obj, canvas, *halo, *tail)

    canvas = run("core", obj, canvas)
    obj, canvas, za, zb = lax.optimization_barrier((obj, canvas, za, zb))
    packed = shape((4 * margin + 3 * PACK, LANES), bf16)
    obj, ca, cb, meta = pl.pallas_call(
        sides_kernel,
        out_shape=(shape(padded, f32), packed, packed, shape((3 * PACK, LANES), bf16)),
        in_specs=[SMEM, SMEM] + [VMEM] * 3,
        out_specs=(VMEM,) * 4,
        input_output_aliases={2: 0},
        compiler_params=pltpu.CompilerParams(vmem_limit_bytes=4 << 20),
        name="sides",
    )(places, counts, obj, za, zb)
    cb, ca = swap(cb, "row", 1), swap(ca, "row", 0)
    canvas = run("inner", obj, canvas)
    obj, canvas, rb = run("far", obj, canvas, pb, cb)
    rb = swap(rb, "row", 1)
    obj, canvas, ra = run("near", obj, canvas, pa, ca)
    ra = swap(ra, "row", 0)
    scale = pl.pallas_call(
        light_kernel,
        out_shape=shape((tiles, tile_r, LANES), f32),
        in_specs=[VMEM] * 4,
        out_specs=VMEM,
        scratch_shapes=[
            pltpu.VMEM((2, window, LANES), f32),
            pltpu.VMEM((tiles + 4, tile_r + 2 * window, LANES), f32),
            pltpu.VMEM((PACK, LANES), jnp.int32),
            pltpu.SMEM((PACK, LANES), jnp.int32),
            pltpu.SemaphoreType.DMA,
        ],
        compiler_params=pltpu.CompilerParams(vmem_limit_bytes=9 << 20),
        cost_estimate=pl.CostEstimate(flops=8 << 20, bytes_accessed=12 << 20, transcendentals=0),
        name="light",
    )(meta, ca, cb, probe)
    canvas, scale = lax.optimization_barrier((canvas, scale))
    rim = shape((2 * tile_r, LANES), bf16)
    sa, sb = pl.pallas_call(
        strips_kernel,
        out_shape=(rim, rim),
        in_specs=[VMEM] * 3,
        out_specs=(VMEM, VMEM),
        compiler_params=pltpu.CompilerParams(vmem_limit_bytes=4 << 20),
        name="strips",
    )(canvas, ra, rb)
    sa, sb = swap(sa, "col", 0), swap(sb, "col", 1)
    field = shape((2, tile_r, tile_c), f32)

    def update(parity, aliases, *args):
        width = 2 if parity is None else 1
        return pl.pallas_call(
            functools.partial(update_kernel, parity),
            out_shape=(field, field),
            in_specs=[VMEM] * (len(args) - len(aliases)) + [ANY] * len(aliases),
            out_specs=(ANY, ANY),
            input_output_aliases=aliases,
            scratch_shapes=[pltpu.VMEM((2, width, tile_r, LANES), f32)] * 2
            + [pltpu.SemaphoreType.DMA((2, width, tile_r // 256))],
            compiler_params=pltpu.CompilerParams(vmem_limit_bytes=8 << 20),
            cost_estimate=pl.CostEstimate(flops=4 << 20, bytes_accessed=10 << 20, transcendentals=0),
            name="middle" if parity is None else "rim",
        )(*args)

    grad, out = update(None, {}, object_field, canvas, ra, rb, scale)
    grad, out = update(0, {6: 0, 7: 1}, object_field, canvas, ra, rb, scale, sa, grad, out)
    return update(1, {6: 0, 7: 1}, object_field, canvas, ra, rb, scale, sb, grad, out)


def solution(mesh):
    in_specs = (
        P(None, "row", "col"),
        P(),
        P("row", "col", None, None, None, None),
        P("row", "col", None, None, None),
        P("row", "col", None),
    )
    out_specs = (P(None, "row", "col"), P(None, "row", "col"))
    return jax.shard_map(
        on_device, mesh=mesh, in_specs=in_specs, out_specs=out_specs, check_vma=False
    )
```
